32 devices in a mesh: design: 2 (over y), space: 8 (over z, x), case: 2 (over core).
Axes of the slice: x: 2, y: 2, z: 4, core: 2. Of those that a mesh axis runs over, the one named last changes fastest.
Arguments:
- displacement: float32 [16, 3, 96, 16, 128], P(('design', 'case'), None, 'space'), parts along dimension 0, may hold values from -3 to 3
- forces: float32 [16, 3, 96, 16, 128], P(('design', 'case'), None, 'space'), parts along dimension 0, may hold values from -13.6 to 13.6
- density: float32 [192, 16, 128], P(('design', 'space')), parts along dimension 0, may hold values from 0.1 to 1
- support_mask: int32 [192, 16, 128], P(('design', 'space')), parts along dimension 0, may hold values 0 or 1
- void_mask: int32 [192, 16, 128], P(('design', 'space')), parts along dimension 0, may hold values 0 or 1
Outputs:
- smoothed: float32 [16, 3, 96, 16, 128], P(('design', 'case'), None, 'space'), parts along dimension 0
- new_density: float32 [192, 16, 128], P(('design', 'space')), parts along dimension 0
- ks_value: float32 [2], P('design'), parts along dimension 0
The draws below stay inside these ranges and needn't reach their ends.
There are 2 independent parts, one for each index of `design`. The reference program is written for one: setup_inputs(seed, part) draws one part's arguments, and reference() takes and returns one part's arrays. A program takes and returns all parts, laid end to end along the dimension named above; each array names one. Nothing has to cross between parts.
All inputs are finite; a program needn't handle non-finite values. No bound on the sum of `support_mask` or of `void_mask` on one device may be relied on, other than what follows from the above.
Results may differ from the reference program's by a relative error of at most 0.00002.
Values sent between devices are 32-bit elements; how exact they have to be, the bound alone decides.
A program may use at most 64 MiB of HBM per device.

```python
import math
import jax
import jax.numpy as jnp
from jax import lax

NY = 16
NZ = 128
CASES = 8
NX = 96


def draw_forces(key, part):
    key_scale, key_base = jax.random.split(jax.random.fold_in(key, 11))
    scales = jnp.exp(jax.random.uniform(key_scale, (CASES, 1, 1, 1, 1), jnp.float32, -0.7, 0.7))
    base = jnp.clip(jax.random.normal(key_base, (CASES, 3, NX, NY, NZ), jnp.float32), -4.0, 4.0)
    return scales * base


def plant(result, key, low, high):
    spot = [jax.random.randint(jax.random.fold_in(key, axis), (), 0, length) for axis, length in enumerate(result.shape)]
    main_axis = result.shape.index(max(result.shape))
    beside = spot[:main_axis] + [(spot[main_axis] + 1) % result.shape[main_axis]] + spot[main_axis + 1:]
    return result.at[tuple(spot)].set(low).at[tuple(beside)].set(high)


def levels(key, dims, cuts, low, top_value):
    gain, own = 1.0, jax.random.fold_in(key, 6)
    for position, blocks in cuts:
        heights = jnp.exp(jax.random.uniform(jax.random.fold_in(own, position), (blocks,), jnp.float32, low / len(cuts), top_value / len(cuts)))
        gain = gain * jnp.repeat(heights, dims[position] // blocks).reshape([-1 if axis == position else 1 for axis in range(len(dims))])
    return gain


def gaussian(stream_key, shape, scale, bound, pieces=(), held_as=jnp.bfloat16):
    result = jax.random.normal(stream_key, shape, jnp.float32) * scale
    if len(pieces) > 0:
        result = levels(stream_key, shape, pieces, -0.22, 0.18) * result
    return jnp.clip(result, min=-bound, max=bound).astype(held_as)


def setup_inputs(seed: int = 0, part: int = 0) -> dict:
    keys = jax.random.split(jax.random.key(seed), 6)
    part_splits = jax.random.split(jax.random.fold_in(keys[5], part), 6)
    return {
        "displacement": gaussian(part_splits[0], (CASES, 3, NX, NY, NZ), 0.5, 3.0, ((0, 2), (2, 8)), jnp.float32),
        "forces": draw_forces(jax.random.fold_in(jax.random.fold_in(keys[5], part), 71), part),
        "density": jnp.clip(0.1 + 0.9 * jax.random.uniform(part_splits[2], (NX, NY, NZ), jnp.float32) ** levels(part_splits[2], (NX, NY, NZ), ((0, 8),), -0.2, 0.2), 0.1, 1.0),
        "support_mask": plant((jax.random.randint(part_splits[3], (NX, NY, NZ), 0, 16) < 1).astype(jnp.int32), jax.random.fold_in(part_splits[3], 1), 0, 1),
        "void_mask": plant((jax.random.randint(part_splits[4], (NX, NY, NZ), 0, 8) < 1).astype(jnp.int32), jax.random.fold_in(part_splits[4], 1), 0, 1),
    }


STIFF_MIN = 0.001
DIAG_SHIFT = 0.5
KS_BETA = 8.0
MOVE_LIMIT = 0.2
DENSITY_MIN = 0.001
STEP_ONE = 1.0 / (1.15 + 0.85 * math.cos(math.pi / 4))
STEP_TWO = 1.0 / (1.15 - 0.85 * math.cos(math.pi / 4))


def pad_axis(values, axis, width):
    widths = [(0, 0)] * values.ndim
    widths[values.ndim + axis] = (width, width)
    return jnp.pad(values, widths)


def stencil(fields, cube):
    face_x = STIFF_MIN + 0.5 * (cube[:-1] + cube[1:])
    middle = cube[1:-1]
    cube_y = pad_axis(middle, -2, 1)
    face_y = STIFF_MIN + 0.5 * (cube_y[:, :-1] + cube_y[:, 1:])
    cube_z = pad_axis(middle, -1, 1)
    face_z = STIFF_MIN + 0.5 * (cube_z[:, :, :-1] + cube_z[:, :, 1:])
    centre = fields[..., 1:-1, :, :]
    padded_y = pad_axis(centre, -2, 1)
    padded_z = pad_axis(centre, -1, 1)
    fluxes = face_x[1:] * (centre - fields[..., 2:, :, :]) + face_x[:-1] * (centre - fields[..., :-2, :, :])
    fluxes = fluxes + face_y[:, 1:] * (centre - padded_y[..., 2:, :]) + face_y[:, :-1] * (centre - padded_y[..., :-2, :])
    fluxes = fluxes + face_z[:, :, 1:] * (centre - padded_z[..., 2:]) + face_z[:, :, :-1] * (centre - padded_z[..., :-2])
    diagonal = DIAG_SHIFT + face_x[1:] + face_x[:-1] + face_y[:, 1:] + face_y[:, :-1] + face_z[:, :, 1:] + face_z[:, :, :-1]
    return DIAG_SHIFT * centre + fluxes, diagonal


def smooth_sweep(fields, loads, cube, keep, factor):
    applied, diagonal = stencil(fields, cube)
    centre = fields[..., 1:-1, :, :]
    return keep * (centre + factor * (loads - applied) / diagonal)


def energy(extended, density):
    centre = extended[..., 1:-1, :, :]
    padded_y = pad_axis(centre, -2, 1)
    padded_z = pad_axis(centre, -1, 1)
    squares = (centre - extended[..., 2:, :, :]) ** 2 + (centre - extended[..., :-2, :, :]) ** 2
    squares = squares + (centre - padded_y[..., 2:, :]) ** 2 + (centre - padded_y[..., :-2, :]) ** 2
    squares = squares + (centre - padded_z[..., 2:]) ** 2 + (centre - padded_z[..., :-2]) ** 2
    return -1.5 * density * density * jnp.sum(squares, axis=-4)


def reference(displacement, forces, density, support_mask, void_mask):
    cube_pad = pad_axis(density ** 3, -3, 1)
    keep = (1 - support_mask).astype(jnp.float32)

    def one_case(pair):
        motion, loads = pair
        motion = smooth_sweep(pad_axis(motion, -3, 1), loads, cube_pad, keep, STEP_ONE)
        motion = smooth_sweep(pad_axis(motion, -3, 1), loads, cube_pad, keep, STEP_TWO)
        case_sens = energy(pad_axis(motion, -3, 1), density)
        return motion, case_sens, jnp.sum(loads * motion)

    smoothed, all_sens, compliance = lax.map(one_case, (displacement, forces))
    scores = KS_BETA * compliance / (3.0 * NX * NY * NZ)
    highest = jnp.max(scores)
    exponent = jnp.exp(scores - highest)
    denominator = jnp.sum(exponent)
    weights = exponent / denominator
    ks_value = (highest + jnp.log(denominator)) / KS_BETA
    combined = jnp.sum(weights[:, None, None, None] * all_sens, axis=0)
    product = density * combined
    padded = jnp.pad(product, 1)
    ones_pad = jnp.pad(jnp.ones_like(product), 1)
    neighbours = padded[2:, 1:-1, 1:-1] + padded[:-2, 1:-1, 1:-1] + padded[1:-1, 2:, 1:-1]
    neighbours = neighbours + padded[1:-1, :-2, 1:-1] + padded[1:-1, 1:-1, 2:] + padded[1:-1, 1:-1, :-2]
    counts = ones_pad[2:, 1:-1, 1:-1] + ones_pad[:-2, 1:-1, 1:-1] + ones_pad[1:-1, 2:, 1:-1]
    counts = counts + ones_pad[1:-1, :-2, 1:-1] + ones_pad[1:-1, 1:-1, 2:] + ones_pad[1:-1, 1:-1, :-2]
    filtered = (2.0 * product + neighbours) / (density * (2.0 + counts))
    scale = jnp.sum(-filtered) / (NX * NY * NZ) + 1e-6
    updated = jnp.clip(density + MOVE_LIMIT * (-filtered / scale - 1.0), DENSITY_MIN, 1.0)
    new_density = jnp.where(void_mask == 1, DENSITY_MIN, updated)
    return smoothed, new_density, ks_value.reshape(1)
```

```python
import functools
import math

import jax
import jax.numpy as jnp
from jax import lax
from jax.experimental import pallas as pl
from jax.experimental.pallas import tpu as pltpu
from jax.sharding import PartitionSpec as P

STIFF_MIN = 0.001
DIAG_SHIFT = 0.5
KS_BETA = 8.0
MOVE_LIMIT = 0.2
DENSITY_MIN = 0.001
STEP_ONE = 1.0 / (1.15 + 0.85 * math.cos(math.pi / 4))
STEP_TWO = 1.0 / (1.15 - 0.85 * math.cos(math.pi / 4))
F32 = jnp.float32
MESH = pl.DeviceIdType.MESH


def kernel(
    n_space, n_case,
    disp, forces, dens, sup, void,
    s2, newd, ks,
    v, f, s1, d, cube, inv, sup_v, void_v,
    kx, kyp, kym, kzp, kzm, keep, rdk, hsum, e, u, up,
    acc, gath,
    load_sem, dens_load, out_sem,
    send_sem, recv_sem, dsend, drecv, usend, urecv, gsend, grecv, known,
):
    cases, comps, planes, rows, lanes = disp.shape
    s = lax.axis_index("space")
    mine = lax.axis_index("case")
    members = n_space * n_case
    me = s * n_case + mine
    has_lo = s > 0
    has_hi = s < n_space - 1
    lo = jnp.maximum(s - 1, 0)
    hi = jnp.minimum(s + 1, n_space - 1)
    last = planes + 1

    other = 1 - mine if n_case == 2 else lax.rem(mine + 1, n_case)

    barrier = pltpu.get_barrier_semaphore()

    def greet(sem, distance):
        @pl.when(s >= distance)
        def _():
            pl.semaphore_signal(
                sem, inc=1, device_id={"space": jnp.maximum(s - distance, 0)}, device_id_type=MESH
            )

        @pl.when(s < n_space - distance)
        def _():
            pl.semaphore_signal(
                sem, inc=1, device_id={"space": jnp.minimum(s + distance, n_space - 1)},
                device_id_type=MESH,
            )

    def greeted(distance):
        return (s >= distance).astype(jnp.int32) + (s < n_space - distance).astype(jnp.int32)

    greet(barrier, 1)
    for step in range(1, n_case):
        pl.semaphore_signal(
            barrier, inc=1, device_id={"case": lax.rem(mine + step, n_case)}, device_id_type=MESH
        )

    distances = [1]
    while distances[-1] < n_space:
        distances.append(2 * distances[-1])
    distances = [1] + distances[:-1] if n_space > 1 else []
    distances = distances[1:]

    def widen_start(k):
        if k < len(distances):
            greet(known.at[k], distances[k])

    def widen_wait(k):
        if k < len(distances):
            pl.semaphore_wait(known.at[k], greeted(distances[k]))

    own = pl.ds(1, planes)
    dens_loads = [
        pltpu.make_async_copy(dens, d.at[own], dens_load.at[0]),
        pltpu.make_async_copy(sup, sup_v, dens_load.at[1]),
        pltpu.make_async_copy(void, void_v, dens_load.at[2]),
    ]
    for copy in dens_loads:
        copy.start()

    def disp_load(c):
        return pltpu.make_async_copy(disp.at[c], v.at[c, :, own], load_sem.at[0, c])

    def force_load(c):
        return pltpu.make_async_copy(forces.at[c], f.at[c], load_sem.at[1, c])

    for c in range(cases):
        disp_load(c).start()
        force_load(c).start()

    @pl.when(s == 0)
    def _():
        zero = jnp.zeros((rows, lanes), F32)
        d[0] = zero
        u[0] = zero
        up[0] = zero
        for ref in (v, s1, s2):
            ref[:, :, 0] = jnp.zeros((cases, comps, rows, lanes), F32)

    @pl.when(s == n_space - 1)
    def _():
        zero = jnp.zeros((rows, lanes), F32)
        d[last] = zero
        u[last] = zero
        up[last] = zero
        for ref in (v, s1, s2):
            ref[:, :, last] = jnp.zeros((cases, comps, rows, lanes), F32)

    pl.semaphore_wait(barrier, greeted(1) + (n_case - 1))

    def remote(src, dst, ssem, rsem, peer):
        return pltpu.make_async_remote_copy(
            src_ref=src, dst_ref=dst, send_sem=ssem, recv_sem=rsem,
            device_id={"space": peer}, device_id_type=MESH,
        )

    def dens_up():
        return remote(dens.at[planes - 1], d.at[0], dsend.at[0], drecv.at[0], hi)

    def dens_down():
        return remote(dens.at[0], d.at[last], dsend.at[1], drecv.at[1], lo)

    bufs = (v, s1, s2)

    def face_up(stage, c):
        src = disp.at[c, :, planes - 1] if stage == 0 else bufs[stage].at[c, :, planes]
        return remote(
            src, bufs[stage].at[c, :, 0], send_sem.at[stage, c, 0], recv_sem.at[stage, c, 0], hi
        )

    def face_down(stage, c):
        src = disp.at[c, :, 0] if stage == 0 else bufs[stage].at[c, :, 1]
        return remote(
            src, bufs[stage].at[c, :, last], send_sem.at[stage, c, 1], recv_sem.at[stage, c, 1], lo
        )

    def send_faces(stage, c):
        @pl.when(has_hi)
        def _():
            face_up(stage, c).start()

        @pl.when(has_lo)
        def _():
            face_down(stage, c).start()

    def await_faces(stage, c):
        @pl.when(has_lo)
        def _():
            face_up(stage, c).wait_recv()

        @pl.when(has_hi)
        def _():
            face_down(stage, c).wait_recv()

    @pl.when(has_hi)
    def _():
        dens_up().start()

    @pl.when(has_lo)
    def _():
        dens_down().start()

    for c in range(cases):
        send_faces(0, c)
    widen_start(0)

    y_id = lax.broadcasted_iota(jnp.int32, (rows, lanes), 0)
    z_id = lax.broadcasted_iota(jnp.int32, (rows, lanes), 1)
    y_first, y_last = y_id == 0, y_id == rows - 1
    z_first, z_last = z_id == 0, z_id == lanes - 1
    yz_count = (
        4.0 + 2.0 - y_first.astype(F32) - y_last.astype(F32)
        - z_first.astype(F32) - z_last.astype(F32)
    )

    def next_y(value):
        return pltpu.roll(value, rows - 1, value.ndim - 2)

    def prev_y(value):
        return pltpu.roll(value, 1, value.ndim - 2)

    def next_z(value):
        return pltpu.roll(value, lanes - 1, value.ndim - 1)

    def prev_z(value):
        return pltpu.roll(value, 1, value.ndim - 1)

    total_planes = planes * n_space

    def cube_of(j, n=1):
        value = d[pl.ds(j, n)]
        cube[pl.ds(j, n)] = value * value * value

    def inv_of(j, n=1):
        g = s * planes + j - 1 + lax.broadcasted_iota(jnp.int32, (n, rows, lanes), 0)
        x_count = (g > 0).astype(F32) + (g < total_planes - 1).astype(F32)
        inside = jnp.logical_and(g >= 0, g < total_planes)
        value = jnp.where(inside, d[pl.ds(j, n)], 1.0)
        inv[pl.ds(j, n)] = jnp.where(inside, 1.0 / (value * (yz_count + x_count)), 0.0)

    def coefficients(j, n=1):
        at = pl.ds(j - 1, n)
        here = cube[pl.ds(j, n)]
        face_lo = STIFF_MIN + 0.5 * (cube[at] + here)
        face_hi = STIFF_MIN + 0.5 * (here + cube[pl.ds(j + 1, n)])
        y_hi = STIFF_MIN + 0.5 * (here + jnp.where(y_last, 0.0, next_y(here)))
        y_lo = STIFF_MIN + 0.5 * (here + jnp.where(y_first, 0.0, prev_y(here)))
        z_hi = STIFF_MIN + 0.5 * (here + jnp.where(z_last, 0.0, next_z(here)))
        z_lo = STIFF_MIN + 0.5 * (here + jnp.where(z_first, 0.0, prev_z(here)))
        kept = (1 - sup_v[at]).astype(F32)
        diagonal = DIAG_SHIFT + face_hi + face_lo + y_hi + y_lo + z_hi + z_lo
        scaled = kept / diagonal
        kx[at] = face_lo
        kx[pl.ds(j, n)] = face_hi
        kyp[at] = jnp.where(y_last, 0.0, y_hi)
        kym[at] = jnp.where(y_first, 0.0, y_lo)
        kzp[at] = jnp.where(z_last, 0.0, z_hi)
        kzm[at] = jnp.where(z_first, 0.0, z_lo)
        keep[at] = kept
        rdk[at] = scaled

    def around(value):
        return (
            jnp.where(y_last, 0.0, next_y(value)) + jnp.where(y_first, 0.0, prev_y(value))
            + jnp.where(z_last, 0.0, next_z(value)) + jnp.where(z_first, 0.0, prev_z(value))
        )

    def filter_sum(j, n=1):
        here = inv[pl.ds(j, n)]
        total = 2.0 * here + inv[pl.ds(j - 1, n)] + inv[pl.ds(j + 1, n)] + around(here)
        hsum[pl.ds(j - 1, n)] = 1.5 * cube[pl.ds(j, n)] * total

    def loop(start, stop, fn, unroll=1):
        def step(i, carry):
            fn(i)
            return carry

        lax.fori_loop(start, stop, step, 0, unroll=unroll)

    def blocks(start, stop, size):
        return [(j, min(size, stop - j)) for j in range(start, stop, size)]

    inner = blocks(2, planes, 2)

    for copy in dens_loads:
        copy.wait()
    for j, n in blocks(1, last, 2):
        cube_of(j, n)
    for j, n in inner:
        coefficients(j, n)

    def sweep(src, dst, c, j, n, factor):
        at = pl.ds(j - 1, n)
        centre = src[c, :, pl.ds(j, n)]
        load = f[c, :, at]
        total = load + kx[at] * src[c, :, at] + kx[pl.ds(j, n)] * src[c, :, pl.ds(j + 1, n)]
        total = total + kyp[at] * next_y(centre) + kym[at] * prev_y(centre)
        total = total + kzp[at] * next_z(centre) + kzm[at] * prev_z(centre)
        result = (keep[at] * (1.0 - factor)) * centre + (rdk[at] * factor) * total
        dst[c, :, pl.ds(j, n)] = result
        return jnp.sum(jnp.sum(load * result, axis=0), axis=0)

    def energy(c, j, n):
        centre = s2[c, :, pl.ds(j, n)]
        low = centre - s2[c, :, pl.ds(j - 1, n)]
        high = centre - s2[c, :, pl.ds(j + 1, n)]
        y_hi = centre - jnp.where(y_last, 0.0, next_y(centre))
        y_lo = centre - jnp.where(y_first, 0.0, prev_y(centre))
        z_hi = centre - jnp.where(z_last, 0.0, next_z(centre))
        z_lo = centre - jnp.where(z_first, 0.0, prev_z(centre))
        squares = low * low + high * high + y_hi * y_hi + y_lo * y_lo + z_hi * z_hi + z_lo * z_lo
        value = jnp.sum(squares, axis=0)
        e[c, pl.ds(j - 1, n)] = value
        return jnp.sum(value * hsum[pl.ds(j - 1, n)], axis=0)

    def interior_one(c):
        disp_load(c).wait()
        force_load(c).wait()
        for j, n in inner:
            sweep(v, s1, c, j, n, STEP_ONE)

    loop(0, cases, interior_one)
    widen_wait(0)
    widen_start(1)

    @pl.when(has_lo)
    def _():
        dens_up().wait_recv()

    @pl.when(has_hi)
    def _():
        dens_down().wait_recv()

    cube_of(0)
    cube_of(last)
    coefficients(1)
    coefficients(planes)

    for c in range(cases):
        await_faces(0, c)
        sweep(v, s1, c, 1, 1, STEP_ONE)
        sweep(v, s1, c, planes, 1, STEP_ONE)
        send_faces(1, c)

    widen_wait(1)
    widen_start(2)
    for j, n in blocks(0, last + 1, 2):
        inv_of(j, n)
    for j, n in blocks(1, last, 2):
        filter_sum(j, n)

    def interior_two(c):
        acc[0, c] = sum(sweep(s1, s2, c, j, n, STEP_TWO) for j, n in inner)

    loop(0, cases, interior_two)

    for c in range(cases):
        await_faces(1, c)
        part = sweep(s1, s2, c, 1, 1, STEP_TWO)
        acc[0, c] = acc[0, c] + part + sweep(s1, s2, c, planes, 1, STEP_TWO)
        send_faces(2, c)

    lane = lax.broadcasted_iota(jnp.int32, (1, lanes), 1)

    def gather_copy(which, peer):
        return pltpu.make_async_remote_copy(
            src_ref=gath.at[which, me], dst_ref=gath.at[which, me],
            send_sem=gsend.at[which], recv_sem=grecv.at[which],
            device_id={"space": peer // n_case, "case": lax.rem(peer, n_case)},
            device_id_type=MESH,
        )

    def gather_start(which):
        row = jnp.zeros((1, lanes), F32)
        for c in range(cases):
            part = jnp.sum(jnp.sum(acc[which, c], axis=0, keepdims=True), axis=1, keepdims=True)
            row = jnp.where(lane == mine * cases + c, part, row)
        gath[which, me] = row
        loop(1, members, lambda step: gather_copy(which, lax.rem(me + step, members)).start())

    def whole(which):
        return gath.at[which, pl.ds(0, members - 1)]

    def gather_wait(which):
        pltpu.make_async_copy(whole(which), whole(which), grecv.at[which]).wait()
        return jnp.sum(gath[which], axis=0)

    for k in range(2, len(distances)):
        if k > 2:
            widen_start(k)
        widen_wait(k)
    gather_start(0)

    def interior_three(c):
        acc[1, c] = sum(energy(c, j, n) for j, n in inner)

    loop(0, cases, interior_three)

    for c in range(cases):
        await_faces(2, c)
        acc[1, c] = acc[1, c] + energy(c, 1, 1) + energy(c, planes, 1)

    gather_start(1)

    cells = total_planes * rows * lanes
    valid = lane < cases * n_case
    scores = (KS_BETA / (3.0 * cells)) * gather_wait(0)
    top = jnp.max(jnp.where(valid, scores, -3.0e38), axis=1, keepdims=True)
    exponent = jnp.where(valid, jnp.exp(jnp.where(valid, scores - top, 0.0)), 0.0)
    total = jnp.sum(exponent, axis=1, keepdims=True)
    weights = exponent / total
    ks[...] = jnp.broadcast_to((top + jnp.log(total)) / KS_BETA, (1, lanes))
    picks = [
        jnp.sum(jnp.where(lane == mine * cases + c, weights, 0.0), axis=1, keepdims=True)
        for c in range(cases)
    ]

    def mix(j, n=1):
        at = pl.ds(j - 1, n)
        value = picks[0] * e[0, at]
        for c in range(1, cases):
            value = value + picks[c] * e[c, at]
        u[pl.ds(j, n)] = value

    mix(1)
    mix(planes)

    def rim(dst, index, peer, case, src):
        return pltpu.make_async_remote_copy(
            src_ref=u.at[src], dst_ref=dst,
            send_sem=usend.at[index], recv_sem=urecv.at[index],
            device_id={"space": peer, "case": case}, device_id_type=MESH,
        )

    rims_up = [rim(u.at[0], 0, hi, mine, planes), rim(up.at[0], 1, hi, other, planes)]
    rims_down = [rim(u.at[last], 2, lo, mine, 1), rim(up.at[last], 3, lo, other, 1)]

    @pl.when(has_hi)
    def _():
        for copy in rims_up:
            copy.start()

    @pl.when(has_lo)
    def _():
        for copy in rims_down:
            copy.start()

    for j, n in inner:
        mix(j, n)
    across = rim(up.at[own], 4, s, other, own)
    across.start()
    across.wait_recv()

    @pl.when(has_lo)
    def _():
        for copy in rims_up:
            copy.wait_recv()

    @pl.when(has_hi)
    def _():
        for copy in rims_down:
            copy.wait_recv()

    for j, n in blocks(0, last + 1, 2):
        at = pl.ds(j, n)
        cube[at] = 1.5 * cube[at] * (u[at] + up[at])

    for j, n in blocks(1, last, 2):
        here = cube[pl.ds(j, n)]
        beside = cube[pl.ds(j - 1, n)] + cube[pl.ds(j + 1, n)]
        kx[pl.ds(j - 1, n)] = inv[pl.ds(j, n)] * (2.0 * here + beside + around(here))

    sums = gather_wait(1)
    scale = jnp.sum(weights * jnp.where(valid, sums, 0.0), axis=1, keepdims=True) / cells + 1e-06
    gain = MOVE_LIMIT / scale

    for j, n in blocks(1, last, 2):
        at = pl.ds(j - 1, n)
        value = d[pl.ds(j, n)] + (kx[at] * gain - MOVE_LIMIT)
        value = jnp.minimum(jnp.maximum(value, DENSITY_MIN), 1.0)
        newd[at] = jnp.where(void_v[at] == 1, DENSITY_MIN, value)

    @pl.when(has_hi)
    def _():
        dens_up().wait_send()
        for copy in rims_up:
            copy.wait_send()
        for stage in range(3):
            loop(0, cases, lambda c: face_up(stage, c).wait_send())

    @pl.when(has_lo)
    def _():
        dens_down().wait_send()
        for copy in rims_down:
            copy.wait_send()
        for stage in range(3):
            loop(0, cases, lambda c: face_down(stage, c).wait_send())

    across.wait_send()
    for which in range(2):
        pltpu.make_async_copy(whole(which), whole(which), gsend.at[which]).wait()


def finish(pieces, smoothed, updated, score, out, newd, ks, sem):
    copies = [pltpu.make_async_copy(smoothed.at[c, :, pl.ds(1, out.shape[2])], out.at[c], sem.at[c]) for c in range(pieces)]
    last = pltpu.make_async_copy(updated, newd, sem.at[pieces])
    for copy in copies:
        copy.start()
    last.start()
    ks[0] = jnp.max(score[...])
    for copy in copies:
        copy.wait()
    last.wait()


def solution(mesh):
    n_space, n_case = mesh.shape["space"], mesh.shape["case"]
    members = n_space * n_case

    def body(displacement, forces, density, support_mask, void_mask):
        cases, comps, planes, rows, lanes = displacement.shape
        padded = (cases, comps, planes + 2, rows, lanes)
        slab = (planes, rows, lanes)
        thick = (planes + 2, rows, lanes)
        any_space = pl.BlockSpec(memory_space=pl.ANY)
        vmem = lambda shape, dtype=F32: pltpu.VMEM(shape, dtype)
        dma = pltpu.SemaphoreType.DMA
        smoothed, updated, score = pl.pallas_call(
            functools.partial(kernel, n_space, n_case),
            out_shape=(
                pltpu.VMEM(padded, F32),
                pltpu.VMEM(density.shape, F32),
                pltpu.VMEM((1, lanes), F32),
            ),
            in_specs=[pl.BlockSpec(memory_space=pltpu.HBM)] * 5,
            out_specs=(
                pl.BlockSpec(memory_space=pltpu.VMEM),
                pl.BlockSpec(memory_space=pltpu.VMEM),
                pl.BlockSpec(memory_space=pltpu.VMEM),
            ),
            scratch_shapes=[
                vmem(padded), vmem(displacement.shape), vmem(padded),
                vmem(thick), vmem(thick), vmem(thick),
                vmem(slab, jnp.int32), vmem(slab, jnp.int32),
                vmem((planes + 1, rows, lanes)),
                vmem(slab), vmem(slab), vmem(slab), vmem(slab), vmem(slab), vmem(slab),
                vmem(slab),
                vmem((cases,) + slab), vmem(thick), vmem(thick),
                vmem((2, cases, rows, lanes)),
                vmem((2, members, 1, lanes)),
                dma((2, cases)), dma((3,)), dma((cases,)),
                dma((3, cases, 2)), dma((3, cases, 2)), dma((2,)), dma((2,)),
                dma((5,)), dma((5,)), dma((2,)), dma((2,)),
                pltpu.SemaphoreType.REGULAR((8,)),
            ],
            compiler_params=pltpu.CompilerParams(collective_id=0, has_side_effects=True, vmem_limit_bytes=24 * 2**20),
        )(*(pltpu.with_memory_space_constraint(a, pltpu.HBM) for a in (displacement, forces, density, support_mask, void_mask)))
        return pl.pallas_call(
            functools.partial(finish, cases),
            out_shape=(
                jax.ShapeDtypeStruct(displacement.shape, F32),
                jax.ShapeDtypeStruct(density.shape, F32),
                jax.ShapeDtypeStruct((1,), F32),
            ),
            in_specs=[pl.BlockSpec(memory_space=pltpu.VMEM), pl.BlockSpec(memory_space=pltpu.VMEM), pl.BlockSpec(memory_space=pltpu.VMEM)],
            out_specs=(any_space, any_space, pl.BlockSpec(memory_space=pltpu.SMEM)),
            scratch_shapes=[dma((cases + 1,))],
            compiler_params=pltpu.CompilerParams(vmem_limit_bytes=24 * 2**20),
        )(smoothed, updated, score)

    return jax.shard_map(
        body,
        mesh=mesh,
        in_specs=(
            P(("design", "case"), None, "space", None, None),
            P(("design", "case"), None, "space", None, None),
            P(("design", "space"), None, None),
            P(("design", "space"), None, None),
            P(("design", "space"), None, None),
        ),
        out_specs=(
            P(("design", "case"), None, "space", None, None),
            P(("design", "space"), None, None),
            P("design"),
        ),
        check_vma=False,
    )
```

```python
import functools
import math

import jax
import jax.numpy as jnp
from jax import lax
from jax.experimental import pallas as pl
from jax.experimental.pallas import tpu as pltpu
from jax.sharding import PartitionSpec as P

STIFF_MIN = 0.001
DIAG_SHIFT = 0.5
KS_BETA = 8.0
MOVE_LIMIT = 0.2
DENSITY_MIN = 0.001
STEP_ONE = 1.0 / (1.15 + 0.85 * math.cos(math.pi / 4))
STEP_TWO = 1.0 / (1.15 - 0.85 * math.cos(math.pi / 4))
F32 = jnp.float32
MESH = pl.DeviceIdType.MESH
LO, HI = 0, 1


def loop(start, stop, fn, unroll=1):
    def step(i, carry):
        fn(i)
        return carry

    lax.fori_loop(start, stop, step, 0, unroll=unroll)


def blocks(start, stop, size):
    return [(j, min(size, stop - j)) for j in range(start, stop, size)]


def edges(rows, lanes):
    y_id = lax.broadcasted_iota(jnp.int32, (rows, lanes), 0)
    z_id = lax.broadcasted_iota(jnp.int32, (rows, lanes), 1)
    return y_id == 0, y_id == rows - 1, z_id == 0, z_id == lanes - 1


def next_y(value):
    return pltpu.roll(value, value.shape[-2] - 1, value.ndim - 2)


def prev_y(value):
    return pltpu.roll(value, 1, value.ndim - 2)


def next_z(value):
    return pltpu.roll(value, value.shape[-1] - 1, value.ndim - 1)


def prev_z(value):
    return pltpu.roll(value, 1, value.ndim - 1)


def around(value):
    y_first, y_last, z_first, z_last = edges(*value.shape[-2:])
    return (
        jnp.where(y_last, 0.0, next_y(value)) + jnp.where(y_first, 0.0, prev_y(value))
        + jnp.where(z_last, 0.0, next_z(value)) + jnp.where(z_first, 0.0, prev_z(value))
    )


def kernel(
    n_space, n_case,
    disp, forces, dens, sup, void,
    s2, e, gath, d, cube, inv, void_v,
    v, f, s1, sup_v, kx, kyp, kym, kzp, kzm, keep, rdk, hsum, bx,
    ab, ar, rb, rr, acc, stat,
    load_sem, dens_load, dsend, drecv, vsend, vrecv, asend, arecv, rsend, rrecv,
    csend, crecv, gsend, grecv, known,
):
    cases, comps, planes, rows, lanes = disp.shape
    s = lax.axis_index("space")
    mine = lax.axis_index("case")
    members = n_space * n_case
    me = s * n_case + mine
    has_lo = s > 0
    has_hi = s < n_space - 1
    lo = jnp.maximum(s - 1, 0)
    hi = jnp.minimum(s + 1, n_space - 1)
    last = planes + 1
    half = cases // 2
    no_lo = 1.0 - has_lo.astype(F32)
    no_hi = 1.0 - has_hi.astype(F32)
    y_first, y_last, z_first, z_last = edges(rows, lanes)

    barrier = pltpu.get_barrier_semaphore()

    def greet(sem, distance):
        @pl.when(s >= distance)
        def _():
            pl.semaphore_signal(
                sem, inc=1, device_id={"space": jnp.maximum(s - distance, 0)}, device_id_type=MESH
            )

        @pl.when(s < n_space - distance)
        def _():
            pl.semaphore_signal(
                sem, inc=1, device_id={"space": jnp.minimum(s + distance, n_space - 1)},
                device_id_type=MESH,
            )

    def greeted(distance):
        return (s >= distance).astype(jnp.int32) + (s < n_space - distance).astype(jnp.int32)

    greet(barrier, 1)
    for step in range(1, n_case):
        pl.semaphore_signal(
            barrier, inc=1, device_id={"case": lax.rem(mine + step, n_case)}, device_id_type=MESH
        )

    distances = []
    while 2 ** len(distances) < n_space:
        distances.append(2 ** len(distances))

    def widen_start(k):
        if k < len(distances):
            greet(known.at[k], distances[k])

    def widen_wait(k):
        if k < len(distances):
            pl.semaphore_wait(known.at[k], greeted(distances[k]))

    own = pl.ds(1, planes)
    d_own = pl.ds(2, planes)
    dens_loads = [
        pltpu.make_async_copy(dens, d.at[d_own], dens_load.at[0]),
        pltpu.make_async_copy(sup, sup_v.at[own], dens_load.at[1]),
        pltpu.make_async_copy(void, void_v, dens_load.at[2]),
    ]
    for copy in dens_loads:
        copy.start()

    def disp_load(c):
        return pltpu.make_async_copy(disp.at[c], v.at[c, :, own], load_sem.at[0, c])

    def force_load(c):
        return pltpu.make_async_copy(forces.at[c], f.at[c], load_sem.at[1, c])

    for c in range(cases):
        disp_load(c).start()
        force_load(c).start()

    for side, absent, wide, at in (
        (LO, s == 0, pl.ds(0, 2), 0), (HI, s == n_space - 1, pl.ds(planes + 2, 2), last)
    ):
        @pl.when(absent)
        def _():
            d[wide] = jnp.zeros((2, rows, lanes), F32)
            sup_v[at] = jnp.ones((rows, lanes), jnp.int32)
            v[:, :, at] = jnp.zeros((cases, comps, rows, lanes), F32)
            ar[:, side] = jnp.zeros((cases, 2 * comps, rows, lanes), F32)
            rr[:, side] = jnp.zeros((cases, 2, rows, lanes), F32)

    pl.semaphore_wait(barrier, greeted(1) + (n_case - 1))

    def remote(src, dst, ssem, rsem, side):
        return pltpu.make_async_remote_copy(
            src_ref=src, dst_ref=dst, send_sem=ssem, recv_sem=rsem,
            device_id={"space": hi if side == HI else lo}, device_id_type=MESH,
        )

    def dens_send(side):
        here = pl.ds(planes - 2, 2) if side == HI else pl.ds(0, 2)
        there = pl.ds(0, 2) if side == HI else pl.ds(planes + 2, 2)
        return remote(dens.at[here], d.at[there], dsend.at[side, 0], drecv.at[side, 0], side)

    def sup_send(side):
        here = planes - 1 if side == HI else 0
        there = 0 if side == HI else last
        return remote(sup.at[here], sup_v.at[there], dsend.at[side, 1], drecv.at[side, 1], side)

    def face_send(side, c):
        here = planes - 1 if side == HI else 0
        there = 0 if side == HI else last
        return remote(
            disp.at[c, :, here], v.at[c, :, there], vsend.at[side, c], vrecv.at[side, c], side
        )

    def whole_of(side, c, at_hi):
        return (c >= half) == (side == at_hi)

    def part_send(side, c):
        n = 2 * comps if whole_of(side, c, HI) else comps
        return remote(
            ab.at[c, side, pl.ds(0, n)], ar.at[c, 1 - side, pl.ds(0, n)],
            asend.at[side, c], arecv.at[side, c], side,
        )

    def rim_send(side, c):
        n = 2 if whole_of(side, c, LO) else 1
        return remote(
            rb.at[c, side, pl.ds(0, n)], rr.at[c, 1 - side, pl.ds(0, n)],
            rsend.at[side, c], rrecv.at[side, c], side,
        )

    def to_both(fn):
        @pl.when(has_hi)
        def _():
            fn(HI)

        @pl.when(has_lo)
        def _():
            fn(LO)

    def from_both(fn):
        @pl.when(has_lo)
        def _():
            fn(HI)

        @pl.when(has_hi)
        def _():
            fn(LO)

    def first_sends(side):
        dens_send(side).start()
        sup_send(side).start()

    to_both(first_sends)
    for c in range(cases):
        to_both(lambda side: face_send(side, c).start())
    widen_start(0)

    yz_count = (
        4.0 + 2.0 - y_first.astype(F32) - y_last.astype(F32)
        - z_first.astype(F32) - z_last.astype(F32)
    )
    total_planes = planes * n_space

    def cube_of(j, n=1):
        value = d[pl.ds(j + 1, n)]
        cube[pl.ds(j + 1, n)] = value * value * value

    def inv_of(j, n=1):
        g = s * planes + j - 1 + lax.broadcasted_iota(jnp.int32, (n, rows, lanes), 0)
        x_count = (g > 0).astype(F32) + (g < total_planes - 1).astype(F32)
        inside = jnp.logical_and(g >= 0, g < total_planes)
        value = jnp.where(inside, d[pl.ds(j + 1, n)], 1.0)
        inv[pl.ds(j + 1, n)] = jnp.where(inside, 1.0 / (value * (yz_count + x_count)), 0.0)

    def coefficients(j, n=1):
        at = pl.ds(j, n)
        here = cube[pl.ds(j + 1, n)]
        face_lo = STIFF_MIN + 0.5 * (cube[at] + here)
        face_hi = STIFF_MIN + 0.5 * (here + cube[pl.ds(j + 2, n)])
        y_hi = STIFF_MIN + 0.5 * (here + jnp.where(y_last, 0.0, next_y(here)))
        y_lo = STIFF_MIN + 0.5 * (here + jnp.where(y_first, 0.0, prev_y(here)))
        z_hi = STIFF_MIN + 0.5 * (here + jnp.where(z_last, 0.0, next_z(here)))
        z_lo = STIFF_MIN + 0.5 * (here + jnp.where(z_first, 0.0, prev_z(here)))
        kept = (1 - sup_v[at]).astype(F32)
        diagonal = DIAG_SHIFT + face_hi + face_lo + y_hi + y_lo + z_hi + z_lo
        if j >= 1:
            kx[pl.ds(j - 1, n)] = face_lo
        if j + n <= last:
            kx[at] = face_hi
        kyp[at] = jnp.where(y_last, 0.0, y_hi)
        kym[at] = jnp.where(y_first, 0.0, y_lo)
        kzp[at] = jnp.where(z_last, 0.0, z_hi)
        kzm[at] = jnp.where(z_first, 0.0, z_lo)
        keep[at] = kept
        rdk[at] = kept / diagonal

    def filter_sum(j, n=1):
        here = inv[pl.ds(j + 1, n)]
        total = 2.0 * here + inv[pl.ds(j, n)] + inv[pl.ds(j + 2, n)] + around(here)
        hsum[pl.ds(j, n)] = 1.5 * cube[pl.ds(j + 1, n)] * total

    def in_plane(centre, at):
        total = kyp[at] * next_y(centre) + kym[at] * prev_y(centre)
        return total + kzp[at] * next_z(centre) + kzm[at] * prev_z(centre)

    def settle(centre, total, at, factor):
        return (keep[at] * (1.0 - factor)) * centre + (rdk[at] * factor) * total

    def sweep(src, dst, c, j, n, factor):
        at = pl.ds(j, n)
        centre = src[c, :, at]
        load = f[c, :, pl.ds(j - 1, n)]
        total = load + kx[pl.ds(j - 1, n)] * src[c, :, pl.ds(j - 1, n)]
        total = total + kx[at] * src[c, :, pl.ds(j + 1, n)] + in_plane(centre, at)
        result = settle(centre, total, at, factor)
        dst[c, :, at] = result
        return jnp.sum(jnp.sum(load * result, axis=0), axis=0)

    def energy(c, j, n, low="in", high="in"):
        x_faces, y_faces, z_faces, squares, first, final = [], [], [], [], [], []
        for k in range(comps):
            centre = s2[c, k, pl.ds(j, n)]
            step = centre[1:] - centre[:-1]
            x_faces.append(step * step)
            if low == "end":
                step = centre[:1] * no_lo
            else:
                step = centre[:1] - s2[c, k, pl.ds(j - 1, 1)]
            first.append(step * step)
            if high == "end":
                step = centre[n - 1:] * no_hi
            else:
                step = centre[n - 1:] - s2[c, k, pl.ds(j + n, 1)]
            final.append(step * step)
            step = centre - jnp.where(y_last, 0.0, next_y(centre))
            y_faces.append(step * step)
            step = centre - jnp.where(z_last, 0.0, next_z(centre))
            z_faces.append(step * step)
            squares.append(centre * centre)
        x_faces, y_faces, z_faces, squares, first, final = (
            functools.reduce(lambda a, b: a + b, terms)
            for terms in (x_faces, y_faces, z_faces, squares, first, final)
        )
        value = y_faces + jnp.where(y_first, squares, prev_y(y_faces))
        value = value + z_faces + jnp.where(z_first, squares, prev_z(z_faces))
        value = value + jnp.concatenate([first, x_faces], axis=0)
        value = value + jnp.concatenate([x_faces, final], axis=0)
        e[mine, c, pl.ds(j, n)] = value
        return jnp.sum(value * hsum[pl.ds(j, n)], axis=0), first[0], final[0]

    for copy in dens_loads:
        copy.wait()
    for j, n in blocks(1, last, 2):
        cube_of(j, n)
    for j, n in blocks(2, planes, 2):
        coefficients(j, n)

    def interior_one(c):
        disp_load(c).wait()
        force_load(c).wait()
        for j, n in blocks(2, planes, 2):
            sweep(v, s1, c, j, n, STEP_ONE)

    loop(0, cases, interior_one)
    widen_wait(0)
    widen_start(1)

    def first_waits(side):
        dens_send(side).wait_recv()
        sup_send(side).wait_recv()

    from_both(first_waits)
    for j in (-1, last):
        cube_of(j, 2)
        coefficients(j + 1 if j < 0 else planes, 2)
    for at, plane, face in ((0, 0, 0), (1, 1, 0), (2, planes, planes), (3, last, planes)):
        bx[at] = (rdk[plane] * STEP_ONE) * kx[face]

    def partial(c, side):
        j = 1 if side == LO else planes
        beyond, face = (2, 1) if side == LO else (planes - 1, planes - 1)
        load = f[c, :, j - 1]
        centre = v[c, :, j]
        total = load + kx[face] * v[c, :, beyond] + in_plane(centre, j)
        ab[c, side, pl.ds(0, comps)] = settle(centre, total, j, STEP_ONE)
        if whole_of(side, c, HI):
            ab[c, side, pl.ds(comps, comps)] = load + kx[face] * s1[c, :, beyond]

    for c in range(cases):
        partial(c, LO)
        partial(c, HI)
        to_both(lambda side: part_send(side, c).start())

    widen_wait(1)
    widen_start(2)
    for j, n in blocks(-1, planes + 3, 2):
        inv_of(j, n)
    for j, n in blocks(0, last + 1, 2):
        filter_sum(j, n)

    def interior_two(c):
        acc[0, c] = sum(sweep(s1, s2, c, j, n, STEP_TWO) for j, n in blocks(3, planes - 1, 2))

    loop(0, cases, interior_two)
    for k in range(2, len(distances)):
        if k > 2:
            widen_start(k)
        widen_wait(k)

    def interior_three(c):
        acc[1, c] = sum(energy(c, j, n)[0] for j, n in blocks(4, planes - 2, 3))

    loop(0, cases, interior_three)

    def across(c, step, at, which):
        return pltpu.make_async_remote_copy(
            src_ref=e.at[mine, c, at], dst_ref=e.at[mine, c, at],
            send_sem=csend.at[step - 1, c, which], recv_sem=crecv.at[step - 1, c, which],
            device_id={"case": lax.rem(mine + step, n_case)}, device_id_type=MESH,
        )

    def across_wait(c, step, at, which):
        there = lax.rem(mine + n_case - step, n_case)
        pltpu.make_async_copy(
            e.at[there, c, at], e.at[there, c, at], crecv.at[step - 1, c, which]
        ).wait()

    pieces = ((pl.ds(2, planes - 2), 0), (pl.ds(0, 2), 1), (pl.ds(planes, 2), 2))

    def finish_edges(c):
        def face_waits(side):
            face_send(side, c).wait_recv()
            part_send(side, c).wait_recv()

        from_both(face_waits)
        s1[c, :, 1] = ab[c, LO, pl.ds(0, comps)] + bx[1] * v[c, :, 0]
        s1[c, :, planes] = ab[c, HI, pl.ds(0, comps)] + bx[2] * v[c, :, last]
        s1[c, :, 0] = ar[c, LO, pl.ds(0, comps)] + bx[0] * v[c, :, 1]
        s1[c, :, last] = ar[c, HI, pl.ds(0, comps)] + bx[3] * v[c, :, planes]
        part = sweep(s1, s2, c, 1, 2, STEP_TWO)
        acc[0, c] = acc[0, c] + part + sweep(s1, s2, c, planes - 1, 2, STEP_TWO)
        outside, inside, face, side = (0, 1, 0, LO) if c >= half else (last, planes, planes, HI)
        centre = s1[c, :, outside]
        total = ar[c, side, pl.ds(comps, comps)] + kx[face] * s1[c, :, inside]
        s2[c, :, outside] = settle(centre, total + in_plane(centre, outside), outside, STEP_TWO)

        at_lo, first, _ = energy(c, 1, 3, low="in" if c >= half else "end")
        at_hi, _, final = energy(c, planes - 2, 3, high="in" if c < half else "end")
        total = acc[1, c] + at_lo + at_hi
        if c >= half:
            rb[c, LO, 1] = first
            total = total + first * hsum[0]
        else:
            rb[c, HI, 1] = final
            total = total + final * hsum[last]
        rb[c, LO, 0] = e[mine, c, 1]
        rb[c, HI, 0] = e[mine, c, planes]
        acc[1, c] = total
        to_both(lambda side: rim_send(side, c).start())
        for step in range(1, n_case):
            across(c, step, *pieces[0]).start()

    for c in range(cases):
        finish_edges(c)

    def gather_copy(peer):
        return pltpu.make_async_remote_copy(
            src_ref=gath.at[me], dst_ref=gath.at[me], send_sem=gsend, recv_sem=grecv,
            device_id={"space": peer // n_case, "case": lax.rem(peer, n_case)},
            device_id_type=MESH,
        )

    for which in range(2):
        for c in range(cases):
            stat[pl.ds(which * cases + c, 1)] = jnp.sum(acc[which, c], axis=0, keepdims=True)
    row = lax.broadcasted_iota(jnp.int32, (2 * cases, lanes), 0)
    lane = lax.broadcasted_iota(jnp.int32, (2 * cases, lanes), 1)
    place = jnp.where(row < cases, row, row - cases + lanes // 2) + mine * cases
    sums = jnp.sum(stat[...], axis=1, keepdims=True)
    gath[me] = jnp.sum(jnp.where(lane == place, sums, 0.0), axis=0, keepdims=True)
    loop(1, members, lambda step: gather_copy(lax.rem(me + step, members)).start())

    def rim_waits(side):
        for c in range(cases):
            rim_send(side, c).wait_recv()

    from_both(rim_waits)
    for c in range(cases):
        if c >= half:
            e[mine, c, 0] = rr[c, LO, 0] + rb[c, LO, 1]
            e[mine, c, last] = rr[c, HI, 0]
            e[mine, c, planes] = rb[c, HI, 0] + rr[c, HI, 1]
        else:
            e[mine, c, 0] = rr[c, LO, 0]
            e[mine, c, 1] = rb[c, LO, 0] + rr[c, LO, 1]
            e[mine, c, last] = rr[c, HI, 0] + rb[c, HI, 1]
        for step in range(1, n_case):
            across(c, step, *pieces[1]).start()
            across(c, step, *pieces[2]).start()

    others = gath.at[pl.ds(0, members - 1)]
    for step in range(1, n_case):
        for c in range(cases):
            for at, which in pieces:
                across_wait(c, step, at, which)
    pltpu.make_async_copy(others, others, grecv).wait()

    def sent(side):
        dens_send(side).wait_send()
        sup_send(side).wait_send()
        for c in range(cases):
            face_send(side, c).wait_send()
            part_send(side, c).wait_send()
            rim_send(side, c).wait_send()

    to_both(sent)
    for step in range(1, n_case):
        for c in range(cases):
            for at, which in pieces:
                across(c, step, at, which).wait_send()
    pltpu.make_async_copy(others, others, gsend).wait()


def finish(n_space, s2, e, gath, d, cube, inv, void_v, out, newd, ks, cu, new_v, sem):
    n_case, cases = e.shape[:2]
    planes, rows, lanes = newd.shape
    last = planes + 1
    copies = [
        pltpu.make_async_copy(s2.at[c, :, pl.ds(1, planes)], out.at[c], sem.at[c])
        for c in range(cases)
    ]
    for copy in copies:
        copy.start()

    sums = jnp.sum(gath[...], axis=0)
    lane = lax.broadcasted_iota(jnp.int32, (1, lanes), 1)
    cells = planes * n_space * rows * lanes
    valid = lane < cases * n_case
    scores = (KS_BETA / (3.0 * cells)) * sums
    top = jnp.max(jnp.where(valid, scores, -3.0e38), axis=1, keepdims=True)
    exponent = jnp.where(valid, jnp.exp(jnp.where(valid, scores - top, 0.0)), 0.0)
    total = jnp.sum(exponent, axis=1, keepdims=True)
    weights = exponent / total
    ks[0] = jnp.max((top + jnp.log(total)) / KS_BETA)
    moved = pltpu.roll(sums, lanes // 2, 1)
    scale = jnp.sum(weights * jnp.where(valid, moved, 0.0), axis=1, keepdims=True)
    gain = MOVE_LIMIT / (scale / cells + 1e-06)
    picks = [
        jnp.sum(jnp.where(lane == c, weights, 0.0), axis=1, keepdims=True)
        for c in range(n_case * cases)
    ]

    for j, n in blocks(0, last + 1, 2):
        at = pl.ds(j, n)
        value = picks[0] * e[0, 0, at]
        for c in range(1, n_case * cases):
            value = value + picks[c] * e[c // cases, c % cases, at]
        cu[at] = 1.5 * cube[pl.ds(j + 1, n)] * value

    for j, n in blocks(1, last, 2):
        at = pl.ds(j - 1, n)
        here = cu[pl.ds(j, n)]
        beside = cu[at] + cu[pl.ds(j + 1, n)]
        filtered = inv[pl.ds(j + 1, n)] * (2.0 * here + beside + around(here))
        value = d[pl.ds(j + 1, n)] + (filtered * gain - MOVE_LIMIT)
        value = jnp.minimum(jnp.maximum(value, DENSITY_MIN), 1.0)
        new_v[at] = jnp.where(void_v[at] == 1, DENSITY_MIN, value)

    store = pltpu.make_async_copy(new_v, newd, sem.at[cases])
    store.start()
    for copy in copies:
        copy.wait()
    store.wait()


def solution(mesh):
    n_space, n_case = mesh.shape["space"], mesh.shape["case"]
    members = n_space * n_case

    def body(*args):
        displacement, _, density, _, void_mask = args
        cases, comps, planes, rows, lanes = displacement.shape
        padded = (cases, comps, planes + 2, rows, lanes)
        slab = (planes, rows, lanes)
        thick = (planes + 2, rows, lanes)
        wide = (planes + 4, rows, lanes)
        in_vmem = pl.BlockSpec(memory_space=pltpu.VMEM)
        in_hbm = pl.BlockSpec(memory_space=pltpu.HBM)
        vmem = lambda shape, dtype=F32: pltpu.VMEM(shape, dtype)
        dma = pltpu.SemaphoreType.DMA
        limit = 24 * 2**20
        kept = pl.pallas_call(
            functools.partial(kernel, n_space, n_case),
            out_shape=(
                vmem(padded), vmem((n_case, cases) + thick), vmem((members, 1, lanes)),
                vmem(wide), vmem(wide), vmem(wide), vmem(slab, jnp.int32),
            ),
            in_specs=[in_hbm] * 5,
            out_specs=(in_vmem,) * 7,
            scratch_shapes=[
                vmem(padded), vmem(displacement.shape), vmem(padded), vmem(thick, jnp.int32),
                vmem((planes + 1, rows, lanes)),
                vmem(thick), vmem(thick), vmem(thick), vmem(thick), vmem(thick), vmem(thick),
                vmem(thick), vmem((4, rows, lanes)),
                vmem((cases, 2, 2 * comps, rows, lanes)), vmem((cases, 2, 2 * comps, rows, lanes)),
                vmem((cases, 2, 2, rows, lanes)), vmem((cases, 2, 2, rows, lanes)),
                vmem((2, cases, rows, lanes)), vmem((2 * cases, lanes)),
                dma((2, cases)), dma((3,)), dma((2, 2)), dma((2, 2)),
                dma((2, cases)), dma((2, cases)), dma((2, cases)), dma((2, cases)),
                dma((2, cases)), dma((2, cases)),
                dma((n_case, cases, 3)), dma((n_case, cases, 3)), dma, dma,
                pltpu.SemaphoreType.REGULAR((16,)),
            ],
            compiler_params=pltpu.CompilerParams(
                collective_id=0, has_side_effects=True, vmem_limit_bytes=limit
            ),
        )(*(pltpu.with_memory_space_constraint(arg, pltpu.HBM) for arg in args))
        return pl.pallas_call(
            functools.partial(finish, n_space),
            out_shape=(
                jax.ShapeDtypeStruct(displacement.shape, F32),
                jax.ShapeDtypeStruct(density.shape, F32),
                jax.ShapeDtypeStruct((1,), F32),
            ),
            in_specs=[in_vmem] * 7,
            out_specs=(
                pl.BlockSpec(memory_space=pl.ANY),
                pl.BlockSpec(memory_space=pl.ANY),
                pl.BlockSpec(memory_space=pltpu.SMEM),
            ),
            scratch_shapes=[vmem(thick), vmem(slab), dma((cases + 1,))],
            compiler_params=pltpu.CompilerParams(vmem_limit_bytes=limit),
        )(*kept)

    return jax.shard_map(
        body,
        mesh=mesh,
        in_specs=(
            P(("design", "case"), None, "space", None, None),
            P(("design", "case"), None, "space", None, None),
            P(("design", "space"), None, None),
            P(("design", "space"), None, None),
            P(("design", "space"), None, None),
        ),
        out_specs=(
            P(("design", "case"), None, "space", None, None),
            P(("design", "space"), None, None),
            P("design"),
        ),
        check_vma=False,
    )
```

```python
import functools
import math

import jax
import jax.numpy as jnp
from jax import lax
from jax.experimental import pallas as pl
from jax.experimental.pallas import tpu as pltpu
from jax.sharding import PartitionSpec as P

STIFF_MIN = 0.001
DIAG_SHIFT = 0.5
KS_BETA = 8.0
MOVE_LIMIT = 0.2
DENSITY_MIN = 0.001
STEP_ONE = 1.0 / (1.15 + 0.85 * math.cos(math.pi / 4))
STEP_TWO = 1.0 / (1.15 - 0.85 * math.cos(math.pi / 4))
F32 = jnp.float32
MESH = pl.DeviceIdType.MESH
LO, HI = 0, 1
UP_BIAS, DOWN_BIAS = 1, -1


def loop(start, stop, fn, unroll=1):
    def step(i, carry):
        fn(i)
        return carry

    lax.fori_loop(start, stop, step, 0, unroll=unroll)


def blocks(start, stop, size):
    return [(j, min(size, stop - j)) for j in range(start, stop, size)]


def edges(rows, lanes):
    y_id = lax.broadcasted_iota(jnp.int32, (rows, lanes), 0)
    z_id = lax.broadcasted_iota(jnp.int32, (rows, lanes), 1)
    return y_id == 0, y_id == rows - 1, z_id == 0, z_id == lanes - 1


def next_y(value):
    return pltpu.roll(value, value.shape[-2] - 1, value.ndim - 2)


def prev_y(value):
    return pltpu.roll(value, 1, value.ndim - 2)


def next_z(value):
    return pltpu.roll(value, value.shape[-1] - 1, value.ndim - 1)


def prev_z(value):
    return pltpu.roll(value, 1, value.ndim - 1)


def around(value):
    y_first, y_last, z_first, z_last = edges(*value.shape[-2:])
    return (
        jnp.where(y_last, 0.0, next_y(value)) + jnp.where(y_first, 0.0, prev_y(value))
        + jnp.where(z_last, 0.0, next_z(value)) + jnp.where(z_first, 0.0, prev_z(value))
    )


def kernel(
    n_space, n_case,
    disp, forces, dens, sup, void,
    s2, e, gath, d, cube, inv, void_v,
    v, f, s1, sup_v, kx, kyp, kym, kzp, kzm, keep, rdk, hsum,
    ab, ar, rb, rr, hv, ha, acc, stat,
    load_sem, dens_load, dsend, drecv, vsend, vrecv, asend, arecv, rsend, rrecv,
    psend, precv, hrecv, hsend, csend, crecv, gsend, grecv, known,
):
    cases, comps, planes, rows, lanes = disp.shape
    s = lax.axis_index("space")
    mine = lax.axis_index("case")
    members = n_space * n_case
    me = s * n_case + mine
    has_lo = s > 0
    has_hi = s < n_space - 1
    last = planes + 1
    half = cases // 2
    odd = lax.rem(s, 2) == 1
    even = jnp.logical_not(odd)
    levels = n_space // 2
    sends_by = jnp.where(odd, s + 1 < n_space, s > 0)
    hands_on = jnp.where(odd, s > 2, s + 2 < n_space)

    def by_partner(rises, level):
        up = (cases * (levels - 1 - level)) // max(levels, 1) + UP_BIAS
        down = (cases * (level + 1)) // max(levels, 1) + DOWN_BIAS
        return jnp.clip(jnp.where(rises, up, down), 0, cases)

    by_count = jnp.where(sends_by, by_partner(odd, (s - 1) // 2), 0)
    on_count = jnp.where(hands_on, by_partner(even, jnp.where(odd, s - 2, s) // 2), 0)
    no_lo = 1.0 - has_lo.astype(F32)
    no_hi = 1.0 - has_hi.astype(F32)
    y_first, y_last, z_first, z_last = edges(rows, lanes)

    barrier = pltpu.get_barrier_semaphore()

    def greet(sem, distance):
        @pl.when(s >= distance)
        def _():
            pl.semaphore_signal(
                sem, inc=1, device_id={"space": jnp.maximum(s - distance, 0)}, device_id_type=MESH
            )

        @pl.when(s < n_space - distance)
        def _():
            pl.semaphore_signal(
                sem, inc=1, device_id={"space": jnp.minimum(s + distance, n_space - 1)},
                device_id_type=MESH,
            )

    def greeted(distance):
        return (s >= distance).astype(jnp.int32) + (s < n_space - distance).astype(jnp.int32)

    greet(barrier, 1)
    for step in range(1, n_case):
        pl.semaphore_signal(
            barrier, inc=1, device_id={"case": lax.rem(mine + step, n_case)}, device_id_type=MESH
        )

    distances = []
    while 2 ** len(distances) < n_space:
        distances.append(2 ** len(distances))

    def widen_start(k):
        if k < len(distances):
            greet(known.at[k], distances[k])

    def widen_wait(k):
        if k < len(distances):
            pl.semaphore_wait(known.at[k], greeted(distances[k]))

    own = pl.ds(1, planes)
    d_own = pl.ds(2, planes)
    dens_loads = [
        pltpu.make_async_copy(dens, d.at[d_own], dens_load.at[0]),
        pltpu.make_async_copy(sup, sup_v.at[own], dens_load.at[1]),
        pltpu.make_async_copy(void, void_v, dens_load.at[2]),
    ]
    for copy in dens_loads:
        copy.start()

    def disp_load(c):
        return pltpu.make_async_copy(disp.at[c], v.at[c, :, own], load_sem.at[0, c])

    def force_load(c):
        return pltpu.make_async_copy(forces.at[c], f.at[c], load_sem.at[1, c])

    for c in range(cases):
        disp_load(c).start()
        force_load(c).start()

    for side, absent, wide, at in (
        (LO, s == 0, pl.ds(0, 2), 0), (HI, s == n_space - 1, pl.ds(planes + 2, 2), last)
    ):
        @pl.when(absent)
        def _():
            d[wide] = jnp.zeros((2, rows, lanes), F32)
            sup_v[at] = jnp.ones((rows, lanes), jnp.int32)
            v[:, :, at] = jnp.zeros((cases, comps, rows, lanes), F32)
            ar[:, side] = jnp.zeros((cases, 2 * comps, rows, lanes), F32)
            rr[:, side] = jnp.zeros((cases, 2, rows, lanes), F32)

    pl.semaphore_wait(barrier, greeted(1) + (n_case - 1))

    def remote(src, dst, ssem, rsem, side, distance=1):
        peer = jnp.minimum(s + distance, n_space - 1) if side == HI else jnp.maximum(s - distance, 0)
        return pltpu.make_async_remote_copy(
            src_ref=src, dst_ref=dst, send_sem=ssem, recv_sem=rsem,
            device_id={"space": peer}, device_id_type=MESH,
        )

    def dens_send(side):
        here = pl.ds(planes - 2, 2) if side == HI else pl.ds(0, 2)
        there = pl.ds(0, 2) if side == HI else pl.ds(planes + 2, 2)
        return remote(dens.at[here], d.at[there], dsend.at[side, 0], drecv.at[side, 0], side)

    def sup_send(side):
        here = planes - 1 if side == HI else 0
        there = 0 if side == HI else last
        return remote(sup.at[here], sup_v.at[there], dsend.at[side, 1], drecv.at[side, 1], side)

    def face_send(side, c):
        here = planes - 1 if side == HI else 0
        there = 0 if side == HI else last
        return remote(
            disp.at[c, :, here], v.at[c, :, there], vsend.at[side, c], vrecv.at[side, c], side
        )

    def whole_of(side, c, at_hi):
        return (c >= half) == (side == at_hi)

    def part_send(side, c):
        n = 2 * comps if whole_of(side, c, HI) else comps
        return remote(
            ab.at[c, side, pl.ds(0, n)], ar.at[c, 1 - side, pl.ds(0, n)],
            asend.at[side, c], arecv.at[side, c], side,
        )

    def face_in(side, c):
        here = planes - 1 if side == HI else 0
        return remote(disp.at[c, :, here], hv.at[c], vsend.at[side, c], hrecv.at[0, c], 1 - side)

    def face_on(side, c):
        there = 0 if side == HI else last
        return remote(hv.at[c], v.at[c, :, there], hsend.at[0, c], vrecv.at[side, c], side, 2)

    def part_in(side, c):
        n = 2 * comps if whole_of(side, c, HI) else comps
        return remote(
            ab.at[c, side, pl.ds(0, n)], ha.at[c, pl.ds(0, n)],
            asend.at[side, c], hrecv.at[1, c], 1 - side,
        )

    def part_on(side, c):
        n = 2 * comps if whole_of(side, c, HI) else comps
        return remote(
            ha.at[c, pl.ds(0, n)], ar.at[c, 1 - side, pl.ds(0, n)],
            hsend.at[1, c], arecv.at[side, c], side, 2,
        )

    def send_by(c, inward):
        for side, between in ((HI, odd), (LO, even)):
            @pl.when(jnp.logical_and(between, c < by_count))
            def _():
                inward(side, c).start()

    def send_direct(c, direct):
        for side, has, between in ((HI, has_hi, odd), (LO, has_lo, even)):
            by = jnp.logical_and(between, c < by_count)

            @pl.when(jnp.logical_and(has, jnp.logical_not(by)))
            def _():
                direct(side, c).start()

    def hand_on(c, fn):
        for side, between in ((HI, even), (LO, odd)):
            @pl.when(jnp.logical_and(between, c < on_count))
            def _():
                fn(side)

    order = tuple(reversed(range(cases)))

    def rim_send(side, c):
        n = 2 if whole_of(side, c, LO) else 1
        return remote(
            rb.at[c, side, pl.ds(0, n)], rr.at[c, 1 - side, pl.ds(0, n)],
            rsend.at[side, c], rrecv.at[side, c], side,
        )

    def to_both(fn):
        @pl.when(has_hi)
        def _():
            fn(HI)

        @pl.when(has_lo)
        def _():
            fn(LO)

    def from_both(fn):
        @pl.when(has_lo)
        def _():
            fn(HI)

        @pl.when(has_hi)
        def _():
            fn(LO)

    def first_sends(side):
        dens_send(side).start()
        sup_send(side).start()

    for c in range(cases):
        send_by(c, face_in)
    for c in order:
        send_direct(c, face_send)
    bearer = mine == n_case - 1

    @pl.when(bearer)
    def _():
        to_both(first_sends)

    widen_start(0)

    yz_count = (
        4.0 + 2.0 - y_first.astype(F32) - y_last.astype(F32)
        - z_first.astype(F32) - z_last.astype(F32)
    )
    total_planes = planes * n_space

    def cube_of(j, n=1):
        value = d[pl.ds(j + 1, n)]
        cube[pl.ds(j + 1, n)] = value * value * value

    def inv_of(j, n=1):
        g = s * planes + j - 1 + lax.broadcasted_iota(jnp.int32, (n, rows, lanes), 0)
        x_count = (g > 0).astype(F32) + (g < total_planes - 1).astype(F32)
        inside = jnp.logical_and(g >= 0, g < total_planes)
        value = jnp.where(inside, d[pl.ds(j + 1, n)], 1.0)
        inv[pl.ds(j + 1, n)] = jnp.where(inside, 1.0 / (value * (yz_count + x_count)), 0.0)

    def coefficients(j, n=1):
        at = pl.ds(j, n)
        here = cube[pl.ds(j + 1, n)]
        face_lo = STIFF_MIN + 0.5 * (cube[at] + here)
        face_hi = STIFF_MIN + 0.5 * (here + cube[pl.ds(j + 2, n)])
        y_hi = STIFF_MIN + 0.5 * (here + jnp.where(y_last, 0.0, next_y(here)))
        y_lo = STIFF_MIN + 0.5 * (here + jnp.where(y_first, 0.0, prev_y(here)))
        z_hi = STIFF_MIN + 0.5 * (here + jnp.where(z_last, 0.0, next_z(here)))
        z_lo = STIFF_MIN + 0.5 * (here + jnp.where(z_first, 0.0, prev_z(here)))
        kept = (1 - sup_v[at]).astype(F32)
        diagonal = DIAG_SHIFT + face_hi + face_lo + y_hi + y_lo + z_hi + z_lo
        if j >= 1:
            kx[pl.ds(j - 1, n)] = face_lo
        if j + n <= last:
            kx[at] = face_hi
        kyp[at] = jnp.where(y_last, 0.0, y_hi)
        kym[at] = jnp.where(y_first, 0.0, y_lo)
        kzp[at] = jnp.where(z_last, 0.0, z_hi)
        kzm[at] = jnp.where(z_first, 0.0, z_lo)
        keep[at] = kept
        rdk[at] = kept / diagonal

    def filter_sum(j, n=1):
        here = inv[pl.ds(j + 1, n)]
        total = 2.0 * here + inv[pl.ds(j, n)] + inv[pl.ds(j + 2, n)] + around(here)
        hsum[pl.ds(j, n)] = 1.5 * cube[pl.ds(j + 1, n)] * total

    def in_plane(centre, at):
        total = kyp[at] * next_y(centre) + kym[at] * prev_y(centre)
        return total + kzp[at] * next_z(centre) + kzm[at] * prev_z(centre)

    def settle(centre, total, at, factor):
        return (keep[at] * (1.0 - factor)) * centre + (rdk[at] * factor) * total

    def sweep(src, dst, c, j, n, factor):
        at = pl.ds(j, n)
        centre = src[c, :, at]
        load = f[c, :, pl.ds(j - 1, n)]
        total = load + kx[pl.ds(j - 1, n)] * src[c, :, pl.ds(j - 1, n)]
        total = total + kx[at] * src[c, :, pl.ds(j + 1, n)] + in_plane(centre, at)
        result = settle(centre, total, at, factor)
        dst[c, :, at] = result
        return jnp.sum(jnp.sum(load * result, axis=0), axis=0)

    def energy(c, j, n, low="in", high="in"):
        x_faces, y_faces, z_faces, squares, first, final = [], [], [], [], [], []
        for k in range(comps):
            centre = s2[c, k, pl.ds(j, n)]
            step = centre[1:] - centre[:-1]
            x_faces.append(step * step)
            if low == "end":
                step = centre[:1] * no_lo
            else:
                step = centre[:1] - s2[c, k, pl.ds(j - 1, 1)]
            first.append(step * step)
            if high == "end":
                step = centre[n - 1:] * no_hi
            else:
                step = centre[n - 1:] - s2[c, k, pl.ds(j + n, 1)]
            final.append(step * step)
            step = centre - jnp.where(y_last, 0.0, next_y(centre))
            y_faces.append(step * step)
            step = centre - jnp.where(z_last, 0.0, next_z(centre))
            z_faces.append(step * step)
            squares.append(centre * centre)
        x_faces, y_faces, z_faces, squares, first, final = (
            functools.reduce(lambda a, b: a + b, terms)
            for terms in (x_faces, y_faces, z_faces, squares, first, final)
        )
        value = y_faces + jnp.where(y_first, squares, prev_y(y_faces))
        value = value + z_faces + jnp.where(z_first, squares, prev_z(z_faces))
        value = value + jnp.concatenate([first, x_faces], axis=0)
        value = value + jnp.concatenate([x_faces, final], axis=0)
        e[mine, c, pl.ds(j, n)] = value
        return jnp.sum(value * hsum[pl.ds(j, n)], axis=0), first[0], final[0]

    def side_faces(j):
        here = cube[j + 1]
        kyp[j] = jnp.where(y_last, 0.0, STIFF_MIN + 0.5 * (here + next_y(here)))
        kym[j] = jnp.where(y_first, 0.0, STIFF_MIN + 0.5 * (here + prev_y(here)))
        kzp[j] = jnp.where(z_last, 0.0, STIFF_MIN + 0.5 * (here + next_z(here)))
        kzm[j] = jnp.where(z_first, 0.0, STIFF_MIN + 0.5 * (here + prev_z(here)))

    for copy in dens_loads:
        copy.wait()
    for j, n in blocks(1, last, 2):
        cube_of(j, n)
    for j in (1, planes):
        side_faces(j)
    for j in (2, planes - 1):
        coefficients(j)

    def partial(c, side):
        j = 1 if side == LO else planes
        beyond, face = (2, 1) if side == LO else (planes - 1, planes - 1)
        load = f[c, :, j - 1]
        total = load + kx[face] * v[c, :, beyond] + in_plane(v[c, :, j], j)
        ab[c, side, pl.ds(0, comps)] = total
        sweep(v, s1, c, beyond, 1, STEP_ONE)
        if whole_of(side, c, HI):
            ab[c, side, pl.ds(comps, comps)] = load + kx[face] * s1[c, :, beyond]

    for c in range(cases):
        disp_load(c).wait()
        force_load(c).wait()
        partial(c, LO)
        partial(c, HI)
        send_by(c, part_in)
    for c in order:
        send_direct(c, part_send)

    for j, n in blocks(3, planes - 1, 2):
        coefficients(j, n)

    def interior_one(c):
        for j, n in blocks(3, planes - 1, 2):
            sweep(v, s1, c, j, n, STEP_ONE)

    loop(0, cases, interior_one)
    widen_wait(0)
    widen_start(1)

    def face_hand(side, c):
        face_in(side, c).wait_recv()
        face_on(side, c).start()

    def part_hand(side, c):
        part_in(side, c).wait_recv()
        part_on(side, c).start()

    for c in order:
        hand_on(c, lambda side: face_hand(side, c))

    def first_share(side, step):
        at = pl.ds(0, 2) if side == HI else pl.ds(planes + 2, 2)
        plane = 0 if side == HI else last
        return [
            pltpu.make_async_remote_copy(
                src_ref=ref, dst_ref=ref, send_sem=psend.at[step, side, i],
                recv_sem=precv.at[side, i],
                device_id={"case": lax.rem(mine + step, n_case)}, device_id_type=MESH,
            )
            for i, ref in enumerate((d.at[at], sup_v.at[plane]))
        ]

    def first_pass(side):
        dens_send(side).wait_recv()
        sup_send(side).wait_recv()
        for step in range(1, n_case):
            for copy in first_share(side, step):
                copy.start()

    @pl.when(bearer)
    def _():
        from_both(first_pass)

    def interior_two(c):
        acc[0, c] = sum(sweep(s1, s2, c, j, n, STEP_TWO) for j, n in blocks(3, planes - 1, 2))

    loop(0, cases, interior_two)
    for c in order:
        hand_on(c, lambda side: part_hand(side, c))

    def first_waits(side):
        for copy in first_share(side, 1):
            copy.wait_recv()

    @pl.when(jnp.logical_not(bearer))
    def _():
        from_both(first_waits)

    for j in (-1, last):
        cube_of(j, 2)
        coefficients(j + 1 if j < 0 else planes, 2)

    widen_wait(1)
    widen_start(2)
    for j, n in blocks(-1, planes + 3, 2):
        inv_of(j, n)
    for j, n in blocks(0, last + 1, 2):
        filter_sum(j, n)

    for k in range(2, len(distances)):
        if k > 2:
            widen_start(k)
        widen_wait(k)

    def interior_three(c):
        acc[1, c] = sum(energy(c, j, n)[0] for j, n in blocks(4, planes - 2, 3))

    loop(0, cases, interior_three)

    def across(c, step, at, which):
        return pltpu.make_async_remote_copy(
            src_ref=e.at[mine, c, at], dst_ref=e.at[mine, c, at],
            send_sem=csend.at[step - 1, c, which], recv_sem=crecv.at[step - 1, c, which],
            device_id={"case": lax.rem(mine + step, n_case)}, device_id_type=MESH,
        )

    def across_wait(c, step, at, which):
        there = lax.rem(mine + n_case - step, n_case)
        pltpu.make_async_copy(
            e.at[there, c, at], e.at[there, c, at], crecv.at[step - 1, c, which]
        ).wait()

    pieces = ((pl.ds(2, planes - 2), 0), (pl.ds(0, 2), 1), (pl.ds(planes, 2), 2))

    def finish_edges(c):
        def face_waits(side):
            face_send(side, c).wait_recv()
            part_send(side, c).wait_recv()

        from_both(face_waits)
        for j, beside, face, sums in (
            (1, 0, 0, ab[c, LO]), (planes, last, planes, ab[c, HI]),
            (0, 1, 0, ar[c, LO]), (last, planes, planes, ar[c, HI]),
        ):
            total = sums[:comps] + kx[face] * v[c, :, beside]
            s1[c, :, j] = settle(v[c, :, j], total, j, STEP_ONE)
        part = sweep(s1, s2, c, 1, 2, STEP_TWO)
        acc[0, c] = acc[0, c] + part + sweep(s1, s2, c, planes - 1, 2, STEP_TWO)
        outside, inside, face, side = (0, 1, 0, LO) if c >= half else (last, planes, planes, HI)
        centre = s1[c, :, outside]
        total = ar[c, side, pl.ds(comps, comps)] + kx[face] * s1[c, :, inside]
        s2[c, :, outside] = settle(centre, total + in_plane(centre, outside), outside, STEP_TWO)

        at_lo, first, _ = energy(c, 1, 3, low="in" if c >= half else "end")
        at_hi, _, final = energy(c, planes - 2, 3, high="in" if c < half else "end")
        total = acc[1, c] + at_lo + at_hi
        if c >= half:
            rb[c, LO, 1] = first
            total = total + first * hsum[0]
        else:
            rb[c, HI, 1] = final
            total = total + final * hsum[last]
        rb[c, LO, 0] = e[mine, c, 1]
        rb[c, HI, 0] = e[mine, c, planes]
        acc[1, c] = total
        to_both(lambda side: rim_send(side, c).start())
        for step in range(1, n_case):
            across(c, step, *pieces[0]).start()

    for c in order:
        finish_edges(c)

    def gather_copy(peer):
        return pltpu.make_async_remote_copy(
            src_ref=gath.at[me], dst_ref=gath.at[me], send_sem=gsend, recv_sem=grecv,
            device_id={"space": peer // n_case, "case": lax.rem(peer, n_case)},
            device_id_type=MESH,
        )

    for which in range(2):
        for c in range(cases):
            stat[pl.ds(which * cases + c, 1)] = jnp.sum(acc[which, c], axis=0, keepdims=True)
    row = lax.broadcasted_iota(jnp.int32, (2 * cases, lanes), 0)
    lane = lax.broadcasted_iota(jnp.int32, (2 * cases, lanes), 1)
    place = jnp.where(row < cases, row, row - cases + lanes // 2) + mine * cases
    sums = jnp.sum(stat[...], axis=1, keepdims=True)
    gath[me] = jnp.sum(jnp.where(lane == place, sums, 0.0), axis=0, keepdims=True)
    loop(1, members, lambda step: gather_copy(lax.rem(me + step, members)).start())

    def rim_waits(side):
        for c in range(cases):
            rim_send(side, c).wait_recv()

    from_both(rim_waits)
    for c in range(cases):
        if c >= half:
            e[mine, c, 0] = rr[c, LO, 0] + rb[c, LO, 1]
            e[mine, c, last] = rr[c, HI, 0]
            e[mine, c, planes] = rb[c, HI, 0] + rr[c, HI, 1]
        else:
            e[mine, c, 0] = rr[c, LO, 0]
            e[mine, c, 1] = rb[c, LO, 0] + rr[c, LO, 1]
            e[mine, c, last] = rr[c, HI, 0] + rb[c, HI, 1]
        for step in range(1, n_case):
            across(c, step, *pieces[1]).start()
            across(c, step, *pieces[2]).start()

    others = gath.at[pl.ds(0, members - 1)]
    for step in range(1, n_case):
        for c in range(cases):
            for at, which in pieces:
                across_wait(c, step, at, which)
    pltpu.make_async_copy(others, others, grecv).wait()

    def first_sent(side):
        dens_send(side).wait_send()
        sup_send(side).wait_send()

    def first_passed(side):
        for step in range(1, n_case):
            for copy in first_share(side, step):
                copy.wait_send()

    @pl.when(bearer)
    def _():
        to_both(first_sent)
        from_both(first_passed)

    def sent(side):
        for c in range(cases):
            face_send(side, c).wait_send()
            part_send(side, c).wait_send()
            rim_send(side, c).wait_send()

    to_both(sent)

    def handed(side, c):
        face_on(side, c).wait_send()
        part_on(side, c).wait_send()

    for c in range(cases):
        hand_on(c, lambda side: handed(side, c))
    for step in range(1, n_case):
        for c in range(cases):
            for at, which in pieces:
                across(c, step, at, which).wait_send()
    pltpu.make_async_copy(others, others, gsend).wait()


def finish(
    n_space, s2, e, gath, d, cube, inv, void_v, out, newd, ks, cu, new_v, ks_v, sem
):
    n_case, cases = e.shape[:2]
    planes, rows, lanes = newd.shape
    last = planes + 1
    copies = [
        pltpu.make_async_copy(s2.at[c, :, pl.ds(1, planes)], out.at[c], sem.at[c])
        for c in range(cases)
    ]
    for copy in copies:
        copy.start()

    sums = jnp.sum(gath[...], axis=0)
    lane = lax.broadcasted_iota(jnp.int32, (1, lanes), 1)
    cells = planes * n_space * rows * lanes
    valid = lane < cases * n_case
    scores = (KS_BETA / (3.0 * cells)) * sums
    top = jnp.max(jnp.where(valid, scores, -3.0e38), axis=1, keepdims=True)
    exponent = jnp.where(valid, jnp.exp(jnp.where(valid, scores - top, 0.0)), 0.0)
    total = jnp.sum(exponent, axis=1, keepdims=True)
    weights = exponent / total
    ks_v[0] = jnp.max((top + jnp.log(total)) / KS_BETA)
    score = pltpu.make_async_copy(ks_v, ks, sem.at[cases + 1])
    score.start()
    moved = pltpu.roll(sums, lanes // 2, 1)
    scale = jnp.sum(weights * jnp.where(valid, moved, 0.0), axis=1, keepdims=True)
    gain = MOVE_LIMIT / (scale / cells + 1e-06)
    picks = [
        jnp.sum(jnp.where(lane == c, weights, 0.0), axis=1, keepdims=True)
        for c in range(n_case * cases)
    ]

    for j, n in blocks(0, last + 1, 2):
        at = pl.ds(j, n)
        value = picks[0] * e[0, 0, at]
        for c in range(1, n_case * cases):
            value = value + picks[c] * e[c // cases, c % cases, at]
        cu[at] = 1.5 * cube[pl.ds(j + 1, n)] * value

    for j, n in blocks(1, last, 2):
        at = pl.ds(j - 1, n)
        here = cu[pl.ds(j, n)]
        beside = cu[at] + cu[pl.ds(j + 1, n)]
        filtered = inv[pl.ds(j + 1, n)] * (2.0 * here + beside + around(here))
        value = d[pl.ds(j + 1, n)] + (filtered * gain - MOVE_LIMIT)
        value = jnp.minimum(jnp.maximum(value, DENSITY_MIN), 1.0)
        new_v[at] = jnp.where(void_v[at] == 1, DENSITY_MIN, value)

    store = pltpu.make_async_copy(new_v, newd, sem.at[cases])
    store.start()
    for copy in copies:
        copy.wait()
    store.wait()
    score.wait()


def solution(mesh):
    n_space, n_case = mesh.shape["space"], mesh.shape["case"]
    members = n_space * n_case

    def body(*args):
        displacement, _, density, _, void_mask = args
        cases, comps, planes, rows, lanes = displacement.shape
        padded = (cases, comps, planes + 2, rows, lanes)
        slab = (planes, rows, lanes)
        thick = (planes + 2, rows, lanes)
        wide = (planes + 4, rows, lanes)
        in_vmem = pl.BlockSpec(memory_space=pltpu.VMEM)
        in_hbm = pl.BlockSpec(memory_space=pltpu.HBM)
        vmem = lambda shape, dtype=F32: pltpu.VMEM(shape, dtype)
        dma = pltpu.SemaphoreType.DMA
        limit = 24 * 2**20
        kept = pl.pallas_call(
            functools.partial(kernel, n_space, n_case),
            out_shape=(
                vmem(padded), vmem((n_case, cases) + thick), vmem((members, 1, lanes)),
                vmem(wide), vmem(wide), vmem(wide), vmem(slab, jnp.int32),
            ),
            in_specs=[in_hbm] * 5,
            out_specs=(in_vmem,) * 7,
            scratch_shapes=[
                vmem(padded), vmem(displacement.shape), vmem(padded), vmem(thick, jnp.int32),
                vmem((planes + 1, rows, lanes)),
                vmem(thick), vmem(thick), vmem(thick), vmem(thick), vmem(thick), vmem(thick),
                vmem(thick),
                vmem((cases, 2, 2 * comps, rows, lanes)), vmem((cases, 2, 2 * comps, rows, lanes)),
                vmem((cases, 2, 2, rows, lanes)), vmem((cases, 2, 2, rows, lanes)),
                vmem((cases, comps, rows, lanes)), vmem((cases, 2 * comps, rows, lanes)),
                vmem((2, cases, rows, lanes)), vmem((2 * cases, lanes)),
                dma((2, cases)), dma((3,)), dma((2, 2)), dma((2, 2)),
                dma((2, cases)), dma((2, cases)), dma((2, cases)), dma((2, cases)),
                dma((2, cases)), dma((2, cases)), dma((n_case, 2, 2)), dma((2, 2)),
                dma((2, cases)), dma((2, cases)),
                dma((n_case, cases, 3)), dma((n_case, cases, 3)), dma, dma,
                pltpu.SemaphoreType.REGULAR((16,)),
            ],
            compiler_params=pltpu.CompilerParams(
                collective_id=0, has_side_effects=True, vmem_limit_bytes=limit
            ),
        )(*(pltpu.with_memory_space_constraint(arg, pltpu.HBM) for arg in args))
        return pl.pallas_call(
            functools.partial(finish, n_space),
            out_shape=(
                jax.ShapeDtypeStruct(displacement.shape, F32),
                jax.ShapeDtypeStruct(density.shape, F32),
                jax.ShapeDtypeStruct((1,), F32),
            ),
            in_specs=[in_vmem] * 7,
            out_specs=(
                pl.BlockSpec(memory_space=pl.ANY),
                pl.BlockSpec(memory_space=pl.ANY),
                pl.BlockSpec(memory_space=pl.ANY),
            ),
            scratch_shapes=[vmem(thick), vmem(slab), pltpu.SMEM((1,), F32), dma((cases + 2,))],
            compiler_params=pltpu.CompilerParams(vmem_limit_bytes=limit),
        )(*kept)

    return jax.shard_map(
        body,
        mesh=mesh,
        in_specs=(
            P(("design", "case"), None, "space", None, None),
            P(("design", "case"), None, "space", None, None),
            P(("design", "space"), None, None),
            P(("design", "space"), None, None),
            P(("design", "space"), None, None),
        ),
        out_specs=(
            P(("design", "case"), None, "space", None, None),
            P(("design", "space"), None, None),
            P("design"),
        ),
        check_vma=False,
    )
```

```python
import functools
import math

import jax
import jax.numpy as jnp
from jax import lax
from jax.experimental import pallas as pl
from jax.experimental.pallas import tpu as pltpu
from jax.sharding import PartitionSpec as P

STIFF_MIN = 0.001
DIAG_SHIFT = 0.5
KS_BETA = 8.0
MOVE_LIMIT = 0.2
DENSITY_MIN = 0.001
STEP_ONE = 1.0 / (1.15 + 0.85 * math.cos(math.pi / 4))
STEP_TWO = 1.0 / (1.15 - 0.85 * math.cos(math.pi / 4))
F32 = jnp.float32
MESH = pl.DeviceIdType.MESH
LO, HI = 0, 1
UP_BIAS, DOWN_BIAS = 0, -1


def loop(start, stop, fn, unroll=1):
    def step(i, carry):
        fn(i)
        return carry

    lax.fori_loop(start, stop, step, 0, unroll=unroll)


def blocks(start, stop, size):
    return [(j, min(size, stop - j)) for j in range(start, stop, size)]


def edges(rows, lanes):
    y_id = lax.broadcasted_iota(jnp.int32, (rows, lanes), 0)
    z_id = lax.broadcasted_iota(jnp.int32, (rows, lanes), 1)
    return y_id == 0, y_id == rows - 1, z_id == 0, z_id == lanes - 1


def next_y(value):
    return pltpu.roll(value, value.shape[-2] - 1, value.ndim - 2)


def prev_y(value):
    return pltpu.roll(value, 1, value.ndim - 2)


def next_z(value):
    return pltpu.roll(value, value.shape[-1] - 1, value.ndim - 1)


def prev_z(value):
    return pltpu.roll(value, 1, value.ndim - 1)


def around(value):
    y_first, y_last, z_first, z_last = edges(*value.shape[-2:])
    return (
        jnp.where(y_last, 0.0, next_y(value)) + jnp.where(y_first, 0.0, prev_y(value))
        + jnp.where(z_last, 0.0, next_z(value)) + jnp.where(z_first, 0.0, prev_z(value))
    )


def kernel(
    n_space, n_case,
    disp, forces, dens, sup, void,
    s2, e, gath, d, cube, inv, void_v,
    v, f, s1, sup_v, kx, kyp, kym, kzp, kzm, keep, rdk, hsum,
    ab, ar, rb, rr, hv, ha, acc, stat,
    load_sem, dens_load, dsend, drecv, vsend, vrecv, asend, arecv, rsend, rrecv,
    psend, precv, hrecv, hsend, csend, crecv, gsend, grecv, known,
):
    cases, comps, planes, rows, lanes = disp.shape
    s = lax.axis_index("space")
    mine = lax.axis_index("case")
    members = n_space * n_case
    me = s * n_case + mine
    has_lo = s > 0
    has_hi = s < n_space - 1
    last = planes + 1
    half = cases // 2
    odd = lax.rem(s, 2) == 1
    even = jnp.logical_not(odd)
    levels = n_space // 2
    sends_by = jnp.where(odd, s + 1 < n_space, s > 0)
    hands_on = jnp.where(odd, s > 2, s + 2 < n_space)

    def by_partner(rises, level):
        up = (cases * (levels - 1 - level)) // max(levels, 1) + UP_BIAS
        down = (cases * (level + 1)) // max(levels, 1) + DOWN_BIAS
        return jnp.clip(jnp.where(rises, up, down), 0, cases)

    by_count = jnp.where(sends_by, by_partner(odd, (s - 1) // 2), 0)
    on_count = jnp.where(hands_on, by_partner(even, jnp.where(odd, s - 2, s) // 2), 0)
    no_lo = 1.0 - has_lo.astype(F32)
    no_hi = 1.0 - has_hi.astype(F32)
    y_first, y_last, z_first, z_last = edges(rows, lanes)

    barrier = pltpu.get_barrier_semaphore()

    def greet(sem, distance):
        @pl.when(s >= distance)
        def _():
            pl.semaphore_signal(
                sem, inc=1, device_id={"space": jnp.maximum(s - distance, 0)}, device_id_type=MESH
            )

        @pl.when(s < n_space - distance)
        def _():
            pl.semaphore_signal(
                sem, inc=1, device_id={"space": jnp.minimum(s + distance, n_space - 1)},
                device_id_type=MESH,
            )

    def greeted(distance):
        return (s >= distance).astype(jnp.int32) + (s < n_space - distance).astype(jnp.int32)

    greet(barrier, 1)
    for step in range(1, n_case):
        pl.semaphore_signal(
            barrier, inc=1, device_id={"case": lax.rem(mine + step, n_case)}, device_id_type=MESH
        )

    distances = []
    while 2 ** len(distances) < n_space:
        distances.append(2 ** len(distances))

    def widen_start(k):
        if k < len(distances):
            greet(known.at[k], distances[k])

    def widen_wait(k):
        if k < len(distances):
            pl.semaphore_wait(known.at[k], greeted(distances[k]))

    own = pl.ds(1, planes)
    d_own = pl.ds(2, planes)
    dens_loads = [
        pltpu.make_async_copy(dens, d.at[d_own], dens_load.at[0]),
        pltpu.make_async_copy(sup, sup_v.at[own], dens_load.at[1]),
        pltpu.make_async_copy(void, void_v, dens_load.at[2]),
    ]
    for copy in dens_loads:
        copy.start()

    def disp_load(c):
        return pltpu.make_async_copy(disp.at[c], v.at[c, :, own], load_sem.at[0, c])

    def force_load(c):
        return pltpu.make_async_copy(forces.at[c], f.at[c], load_sem.at[1, c])

    for c in range(cases):
        disp_load(c).start()
        force_load(c).start()

    for side, absent, wide, at in (
        (LO, s == 0, pl.ds(0, 2), 0), (HI, s == n_space - 1, pl.ds(planes + 2, 2), last)
    ):
        @pl.when(absent)
        def _():
            d[wide] = jnp.zeros((2, rows, lanes), F32)
            sup_v[at] = jnp.ones((rows, lanes), jnp.int32)
            v[:, :, at] = jnp.zeros((cases, comps, rows, lanes), F32)
            ar[:, side] = jnp.zeros((cases, 2 * comps, rows, lanes), F32)
            rr[:, side] = jnp.zeros((cases, 2, rows, lanes), F32)

    pl.semaphore_wait(barrier, greeted(1) + (n_case - 1))

    def remote(src, dst, ssem, rsem, side, distance=1):
        peer = jnp.minimum(s + distance, n_space - 1) if side == HI else jnp.maximum(s - distance, 0)
        return pltpu.make_async_remote_copy(
            src_ref=src, dst_ref=dst, send_sem=ssem, recv_sem=rsem,
            device_id={"space": peer}, device_id_type=MESH,
        )

    def dens_send(side):
        here = pl.ds(planes - 2, 2) if side == HI else pl.ds(0, 2)
        there = pl.ds(0, 2) if side == HI else pl.ds(planes + 2, 2)
        return remote(dens.at[here], d.at[there], dsend.at[side, 0], drecv.at[side, 0], side)

    def sup_send(side):
        here = planes - 1 if side == HI else 0
        there = 0 if side == HI else last
        return remote(sup.at[here], sup_v.at[there], dsend.at[side, 1], drecv.at[side, 1], side)

    def face_send(side, c):
        here = planes - 1 if side == HI else 0
        there = 0 if side == HI else last
        return remote(
            disp.at[c, :, here], v.at[c, :, there], vsend.at[side, c], vrecv.at[side, c], side
        )

    def whole_of(side, c, at_hi):
        return (c >= half) == (side == at_hi)

    def part_send(side, c):
        n = 2 * comps if whole_of(side, c, HI) else comps
        return remote(
            ab.at[c, side, pl.ds(0, n)], ar.at[c, 1 - side, pl.ds(0, n)],
            asend.at[side, c], arecv.at[side, c], side,
        )

    def face_in(side, c):
        here = planes - 1 if side == HI else 0
        return remote(disp.at[c, :, here], hv.at[c], vsend.at[side, c], hrecv.at[0, c], 1 - side)

    def face_on(side, c):
        there = 0 if side == HI else last
        return remote(hv.at[c], v.at[c, :, there], hsend.at[0, c], vrecv.at[side, c], side, 2)

    def part_in(side, c):
        n = 2 * comps if whole_of(side, c, HI) else comps
        return remote(
            ab.at[c, side, pl.ds(0, n)], ha.at[c, pl.ds(0, n)],
            asend.at[side, c], hrecv.at[1, c], 1 - side,
        )

    def part_on(side, c):
        n = 2 * comps if whole_of(side, c, HI) else comps
        return remote(
            ha.at[c, pl.ds(0, n)], ar.at[c, 1 - side, pl.ds(0, n)],
            hsend.at[1, c], arecv.at[side, c], side, 2,
        )

    def send_by(c, inward):
        for side, between in ((HI, odd), (LO, even)):
            @pl.when(jnp.logical_and(between, c < by_count))
            def _():
                inward(side, c).start()

    def send_direct(c, direct):
        for side, has, between in ((HI, has_hi, odd), (LO, has_lo, even)):
            by = jnp.logical_and(between, c < by_count)

            @pl.when(jnp.logical_and(has, jnp.logical_not(by)))
            def _():
                direct(side, c).start()

    def hand_on(c, fn):
        for side, between in ((HI, even), (LO, odd)):
            @pl.when(jnp.logical_and(between, c < on_count))
            def _():
                fn(side)

    order = tuple(reversed(range(cases)))

    def rim_send(side, c):
        n = 2 if whole_of(side, c, LO) else 1
        return remote(
            rb.at[c, side, pl.ds(0, n)], rr.at[c, 1 - side, pl.ds(0, n)],
            rsend.at[side, c], rrecv.at[side, c], side,
        )

    def to_both(fn):
        @pl.when(has_hi)
        def _():
            fn(HI)

        @pl.when(has_lo)
        def _():
            fn(LO)

    def from_both(fn):
        @pl.when(has_lo)
        def _():
            fn(HI)

        @pl.when(has_hi)
        def _():
            fn(LO)

    def first_sends(side):
        dens_send(side).start()
        sup_send(side).start()

    for c in range(cases):
        send_by(c, face_in)
    for c in order:
        send_direct(c, face_send)
    bearer = mine == n_case - 1

    @pl.when(bearer)
    def _():
        to_both(first_sends)

    widen_start(0)

    yz_count = (
        4.0 + 2.0 - y_first.astype(F32) - y_last.astype(F32)
        - z_first.astype(F32) - z_last.astype(F32)
    )
    total_planes = planes * n_space

    def cube_of(j, n=1):
        value = d[pl.ds(j + 1, n)]
        cube[pl.ds(j + 1, n)] = value * value * value

    def inv_of(j, n=1):
        g = s * planes + j - 1 + lax.broadcasted_iota(jnp.int32, (n, rows, lanes), 0)
        x_count = (g > 0).astype(F32) + (g < total_planes - 1).astype(F32)
        inside = jnp.logical_and(g >= 0, g < total_planes)
        value = jnp.where(inside, d[pl.ds(j + 1, n)], 1.0)
        inv[pl.ds(j + 1, n)] = jnp.where(inside, 1.0 / (value * (yz_count + x_count)), 0.0)

    def coefficients(j, n=1):
        at = pl.ds(j, n)
        here = cube[pl.ds(j + 1, n)]
        face_lo = STIFF_MIN + 0.5 * (cube[at] + here)
        face_hi = STIFF_MIN + 0.5 * (here + cube[pl.ds(j + 2, n)])
        y_hi = STIFF_MIN + 0.5 * (here + jnp.where(y_last, 0.0, next_y(here)))
        y_lo = STIFF_MIN + 0.5 * (here + jnp.where(y_first, 0.0, prev_y(here)))
        z_hi = STIFF_MIN + 0.5 * (here + jnp.where(z_last, 0.0, next_z(here)))
        z_lo = STIFF_MIN + 0.5 * (here + jnp.where(z_first, 0.0, prev_z(here)))
        kept = (1 - sup_v[at]).astype(F32)
        diagonal = DIAG_SHIFT + face_hi + face_lo + y_hi + y_lo + z_hi + z_lo
        if j >= 1:
            kx[pl.ds(j - 1, n)] = face_lo
        if j + n <= last:
            kx[at] = face_hi
        kyp[at] = jnp.where(y_last, 0.0, y_hi)
        kym[at] = jnp.where(y_first, 0.0, y_lo)
        kzp[at] = jnp.where(z_last, 0.0, z_hi)
        kzm[at] = jnp.where(z_first, 0.0, z_lo)
        keep[at] = kept
        rdk[at] = kept / diagonal

    def filter_sum(j, n=1):
        here = inv[pl.ds(j + 1, n)]
        total = 2.0 * here + inv[pl.ds(j, n)] + inv[pl.ds(j + 2, n)] + around(here)
        hsum[pl.ds(j, n)] = 1.5 * cube[pl.ds(j + 1, n)] * total

    def in_plane(centre, at):
        total = kyp[at] * next_y(centre) + kym[at] * prev_y(centre)
        return total + kzp[at] * next_z(centre) + kzm[at] * prev_z(centre)

    def settle(centre, total, at, factor):
        return (keep[at] * (1.0 - factor)) * centre + (rdk[at] * factor) * total

    def sweep(src, dst, c, j, n, factor):
        at = pl.ds(j, n)
        centre = src[c, :, at]
        load = f[c, :, pl.ds(j - 1, n)]
        total = load + kx[pl.ds(j - 1, n)] * src[c, :, pl.ds(j - 1, n)]
        total = total + kx[at] * src[c, :, pl.ds(j + 1, n)] + in_plane(centre, at)
        result = settle(centre, total, at, factor)
        dst[c, :, at] = result
        return jnp.sum(jnp.sum(load * result, axis=0), axis=0)

    def energy(c, j, n, low="in", high="in"):
        x_faces, y_faces, z_faces, squares, first, final = [], [], [], [], [], []
        for k in range(comps):
            centre = s2[c, k, pl.ds(j, n)]
            step = centre[1:] - centre[:-1]
            x_faces.append(step * step)
            if low == "end":
                step = centre[:1] * no_lo
            else:
                step = centre[:1] - s2[c, k, pl.ds(j - 1, 1)]
            first.append(step * step)
            if high == "end":
                step = centre[n - 1:] * no_hi
            else:
                step = centre[n - 1:] - s2[c, k, pl.ds(j + n, 1)]
            final.append(step * step)
            step = centre - jnp.where(y_last, 0.0, next_y(centre))
            y_faces.append(step * step)
            step = centre - jnp.where(z_last, 0.0, next_z(centre))
            z_faces.append(step * step)
            squares.append(centre * centre)
        x_faces, y_faces, z_faces, squares, first, final = (
            functools.reduce(lambda a, b: a + b, terms)
            for terms in (x_faces, y_faces, z_faces, squares, first, final)
        )
        value = y_faces + jnp.where(y_first, squares, prev_y(y_faces))
        value = value + z_faces + jnp.where(z_first, squares, prev_z(z_faces))
        value = value + jnp.concatenate([first, x_faces], axis=0)
        value = value + jnp.concatenate([x_faces, final], axis=0)
        e[mine, c, pl.ds(j, n)] = value
        return jnp.sum(value * hsum[pl.ds(j, n)], axis=0), first[0], final[0]

    def side_faces(j):
        here = cube[j + 1]
        kyp[j] = jnp.where(y_last, 0.0, STIFF_MIN + 0.5 * (here + next_y(here)))
        kym[j] = jnp.where(y_first, 0.0, STIFF_MIN + 0.5 * (here + prev_y(here)))
        kzp[j] = jnp.where(z_last, 0.0, STIFF_MIN + 0.5 * (here + next_z(here)))
        kzm[j] = jnp.where(z_first, 0.0, STIFF_MIN + 0.5 * (here + prev_z(here)))

    for copy in dens_loads:
        copy.wait()
    for j, n in blocks(1, last, 2):
        cube_of(j, n)
    for j in (1, planes):
        side_faces(j)
    for j in (2, planes - 1):
        coefficients(j)

    def partial(c, side):
        j = 1 if side == LO else planes
        beyond, face = (2, 1) if side == LO else (planes - 1, planes - 1)
        load = f[c, :, j - 1]
        total = load + kx[face] * v[c, :, beyond] + in_plane(v[c, :, j], j)
        ab[c, side, pl.ds(0, comps)] = total
        sweep(v, s1, c, beyond, 1, STEP_ONE)
        if whole_of(side, c, HI):
            ab[c, side, pl.ds(comps, comps)] = load + kx[face] * s1[c, :, beyond]

    for c in range(cases):
        disp_load(c).wait()
        force_load(c).wait()
        partial(c, LO)
        partial(c, HI)
        send_by(c, part_in)
    for c in order:
        send_direct(c, part_send)

    for j, n in blocks(3, planes - 1, 2):
        coefficients(j, n)

    def interior_one(c):
        for j, n in blocks(3, planes - 1, 2):
            sweep(v, s1, c, j, n, STEP_ONE)

    loop(0, cases, interior_one)
    widen_wait(0)
    widen_start(1)

    def face_hand(side, c):
        face_in(side, c).wait_recv()
        face_on(side, c).start()

    def part_hand(side, c):
        part_in(side, c).wait_recv()
        part_on(side, c).start()

    for c in order:
        hand_on(c, lambda side: face_hand(side, c))

    def first_share(side, step):
        at = pl.ds(0, 2) if side == HI else pl.ds(planes + 2, 2)
        plane = 0 if side == HI else last
        return [
            pltpu.make_async_remote_copy(
                src_ref=ref, dst_ref=ref, send_sem=psend.at[step, side, i],
                recv_sem=precv.at[side, i],
                device_id={"case": lax.rem(mine + step, n_case)}, device_id_type=MESH,
            )
            for i, ref in enumerate((d.at[at], sup_v.at[plane]))
        ]

    def first_pass(side):
        dens_send(side).wait_recv()
        sup_send(side).wait_recv()
        for step in range(1, n_case):
            for copy in first_share(side, step):
                copy.start()

    @pl.when(bearer)
    def _():
        from_both(first_pass)

    def interior_two(c):
        acc[0, c] = sum(sweep(s1, s2, c, j, n, STEP_TWO) for j, n in blocks(3, planes - 1, 2))

    loop(0, cases, interior_two)
    for c in order:
        hand_on(c, lambda side: part_hand(side, c))

    def first_waits(side):
        for copy in first_share(side, 1):
            copy.wait_recv()

    @pl.when(jnp.logical_not(bearer))
    def _():
        from_both(first_waits)

    for j in (-1, last):
        cube_of(j, 2)
        coefficients(j + 1 if j < 0 else planes, 2)

    widen_wait(1)
    widen_start(2)
    for j, n in blocks(-1, planes + 3, 2):
        inv_of(j, n)
    for j, n in blocks(0, last + 1, 2):
        filter_sum(j, n)

    for k in range(2, len(distances)):
        if k > 2:
            widen_start(k)
        widen_wait(k)

    def interior_three(c):
        acc[1, c] = sum(energy(c, j, n)[0] for j, n in blocks(4, planes - 2, 3))

    loop(0, cases, interior_three)

    def across(c, step, at, which):
        return pltpu.make_async_remote_copy(
            src_ref=e.at[mine, c, at], dst_ref=e.at[mine, c, at],
            send_sem=csend.at[step - 1, c, which], recv_sem=crecv.at[step - 1, c, which],
            device_id={"case": lax.rem(mine + step, n_case)}, device_id_type=MESH,
        )

    def across_wait(c, step, at, which):
        there = lax.rem(mine + n_case - step, n_case)
        pltpu.make_async_copy(
            e.at[there, c, at], e.at[there, c, at], crecv.at[step - 1, c, which]
        ).wait()

    pieces = ((pl.ds(2, planes - 2), 0), (pl.ds(0, 2), 1), (pl.ds(planes, 2), 2))

    def finish_edges(c):
        def face_waits(side):
            face_send(side, c).wait_recv()
            part_send(side, c).wait_recv()

        from_both(face_waits)
        for j, beside, face, sums in (
            (1, 0, 0, ab[c, LO]), (planes, last, planes, ab[c, HI]),
            (0, 1, 0, ar[c, LO]), (last, planes, planes, ar[c, HI]),
        ):
            total = sums[:comps] + kx[face] * v[c, :, beside]
            s1[c, :, j] = settle(v[c, :, j], total, j, STEP_ONE)
        part = sweep(s1, s2, c, 1, 2, STEP_TWO)
        acc[0, c] = acc[0, c] + part + sweep(s1, s2, c, planes - 1, 2, STEP_TWO)
        outside, inside, face, side = (0, 1, 0, LO) if c >= half else (last, planes, planes, HI)
        centre = s1[c, :, outside]
        total = ar[c, side, pl.ds(comps, comps)] + kx[face] * s1[c, :, inside]
        s2[c, :, outside] = settle(centre, total + in_plane(centre, outside), outside, STEP_TWO)

        at_lo, first, _ = energy(c, 1, 3, low="in" if c >= half else "end")
        at_hi, _, final = energy(c, planes - 2, 3, high="in" if c < half else "end")
        total = acc[1, c] + at_lo + at_hi
        if c >= half:
            rb[c, LO, 1] = first
            total = total + first * hsum[0]
        else:
            rb[c, HI, 1] = final
            total = total + final * hsum[last]
        rb[c, LO, 0] = e[mine, c, 1]
        rb[c, HI, 0] = e[mine, c, planes]
        acc[1, c] = total
        to_both(lambda side: rim_send(side, c).start())
        for step in range(1, n_case):
            across(c, step, *pieces[0]).start()

    for c in order:
        finish_edges(c)

    def gather_copy(peer):
        return pltpu.make_async_remote_copy(
            src_ref=gath.at[me], dst_ref=gath.at[me], send_sem=gsend, recv_sem=grecv,
            device_id={"space": peer // n_case, "case": lax.rem(peer, n_case)},
            device_id_type=MESH,
        )

    for which in range(2):
        for c in range(cases):
            stat[pl.ds(which * cases + c, 1)] = jnp.sum(acc[which, c], axis=0, keepdims=True)
    row = lax.broadcasted_iota(jnp.int32, (2 * cases, lanes), 0)
    lane = lax.broadcasted_iota(jnp.int32, (2 * cases, lanes), 1)
    place = jnp.where(row < cases, row, row - cases + lanes // 2) + mine * cases
    sums = jnp.sum(stat[...], axis=1, keepdims=True)
    gath[me] = jnp.sum(jnp.where(lane == place, sums, 0.0), axis=0, keepdims=True)
    loop(1, members, lambda step: gather_copy(lax.rem(me + step, members)).start())

    def rim_waits(side):
        for c in range(cases):
            rim_send(side, c).wait_recv()

    from_both(rim_waits)
    for c in range(cases):
        if c >= half:
            e[mine, c, 0] = rr[c, LO, 0] + rb[c, LO, 1]
            e[mine, c, last] = rr[c, HI, 0]
            e[mine, c, planes] = rb[c, HI, 0] + rr[c, HI, 1]
        else:
            e[mine, c, 0] = rr[c, LO, 0]
            e[mine, c, 1] = rb[c, LO, 0] + rr[c, LO, 1]
            e[mine, c, last] = rr[c, HI, 0] + rb[c, HI, 1]
        for step in range(1, n_case):
            across(c, step, *pieces[1]).start()
            across(c, step, *pieces[2]).start()

    others = gath.at[pl.ds(0, members - 1)]
    for step in range(1, n_case):
        for c in range(cases):
            for at, which in pieces:
                across_wait(c, step, at, which)
    pltpu.make_async_copy(others, others, grecv).wait()

    def first_sent(side):
        dens_send(side).wait_send()
        sup_send(side).wait_send()

    def first_passed(side):
        for step in range(1, n_case):
            for copy in first_share(side, step):
                copy.wait_send()

    @pl.when(bearer)
    def _():
        to_both(first_sent)
        from_both(first_passed)

    def sent(side):
        for c in range(cases):
            face_send(side, c).wait_send()
            part_send(side, c).wait_send()
            rim_send(side, c).wait_send()

    to_both(sent)

    def handed(side, c):
        face_on(side, c).wait_send()
        part_on(side, c).wait_send()

    for c in range(cases):
        hand_on(c, lambda side: handed(side, c))
    for step in range(1, n_case):
        for c in range(cases):
            for at, which in pieces:
                across(c, step, at, which).wait_send()
    pltpu.make_async_copy(others, others, gsend).wait()


def finish(
    n_space, s2, e, gath, d, cube, inv, void_v, out, newd, ks, cu, new_v, ks_v, sem
):
    n_case, cases = e.shape[:2]
    planes, rows, lanes = newd.shape
    last = planes + 1
    copies = [
        pltpu.make_async_copy(s2.at[c, :, pl.ds(1, planes)], out.at[c], sem.at[c])
        for c in range(cases)
    ]
    for copy in copies:
        copy.start()

    sums = jnp.sum(gath[...], axis=0)
    lane = lax.broadcasted_iota(jnp.int32, (1, lanes), 1)
    cells = planes * n_space * rows * lanes
    valid = lane < cases * n_case
    scores = (KS_BETA / (3.0 * cells)) * sums
    top = jnp.max(jnp.where(valid, scores, -3.0e38), axis=1, keepdims=True)
    exponent = jnp.where(valid, jnp.exp(jnp.where(valid, scores - top, 0.0)), 0.0)
    total = jnp.sum(exponent, axis=1, keepdims=True)
    weights = exponent / total
    ks_v[0] = jnp.max((top + jnp.log(total)) / KS_BETA)
    score = pltpu.make_async_copy(ks_v, ks, sem.at[cases + 1])
    score.start()
    moved = pltpu.roll(sums, lanes // 2, 1)
    scale = jnp.sum(weights * jnp.where(valid, moved, 0.0), axis=1, keepdims=True)
    gain = MOVE_LIMIT / (scale / cells + 1e-06)
    picks = [
        jnp.sum(jnp.where(lane == c, weights, 0.0), axis=1, keepdims=True)
        for c in range(n_case * cases)
    ]

    for j, n in blocks(0, last + 1, 2):
        at = pl.ds(j, n)
        value = picks[0] * e[0, 0, at]
        for c in range(1, n_case * cases):
            value = value + picks[c] * e[c // cases, c % cases, at]
        cu[at] = 1.5 * cube[pl.ds(j + 1, n)] * value

    for j, n in blocks(1, last, 2):
        at = pl.ds(j - 1, n)
        here = cu[pl.ds(j, n)]
        beside = cu[at] + cu[pl.ds(j + 1, n)]
        filtered = inv[pl.ds(j + 1, n)] * (2.0 * here + beside + around(here))
        value = d[pl.ds(j + 1, n)] + (filtered * gain - MOVE_LIMIT)
        value = jnp.minimum(jnp.maximum(value, DENSITY_MIN), 1.0)
        new_v[at] = jnp.where(void_v[at] == 1, DENSITY_MIN, value)

    store = pltpu.make_async_copy(new_v, newd, sem.at[cases])
    store.start()
    for copy in copies:
        copy.wait()
    store.wait()
    score.wait()


def solution(mesh):
    n_space, n_case = mesh.shape["space"], mesh.shape["case"]
    members = n_space * n_case

    def body(*args):
        displacement, _, density, _, void_mask = args
        cases, comps, planes, rows, lanes = displacement.shape
        padded = (cases, comps, planes + 2, rows, lanes)
        slab = (planes, rows, lanes)
        thick = (planes + 2, rows, lanes)
        wide = (planes + 4, rows, lanes)
        in_vmem = pl.BlockSpec(memory_space=pltpu.VMEM)
        in_hbm = pl.BlockSpec(memory_space=pltpu.HBM)
        vmem = lambda shape, dtype=F32: pltpu.VMEM(shape, dtype)
        dma = pltpu.SemaphoreType.DMA
        limit = 24 * 2**20
        kept = pl.pallas_call(
            functools.partial(kernel, n_space, n_case),
            out_shape=(
                vmem(padded), vmem((n_case, cases) + thick), vmem((members, 1, lanes)),
                vmem(wide), vmem(wide), vmem(wide), vmem(slab, jnp.int32),
            ),
            in_specs=[in_hbm] * 5,
            out_specs=(in_vmem,) * 7,
            scratch_shapes=[
                vmem(padded), vmem(displacement.shape), vmem(padded), vmem(thick, jnp.int32),
                vmem((planes + 1, rows, lanes)),
                vmem(thick), vmem(thick), vmem(thick), vmem(thick), vmem(thick), vmem(thick),
                vmem(thick),
                vmem((cases, 2, 2 * comps, rows, lanes)), vmem((cases, 2, 2 * comps, rows, lanes)),
                vmem((cases, 2, 2, rows, lanes)), vmem((cases, 2, 2, rows, lanes)),
                vmem((cases, comps, rows, lanes)), vmem((cases, 2 * comps, rows, lanes)),
                vmem((2, cases, rows, lanes)), vmem((2 * cases, lanes)),
                dma((2, cases)), dma((3,)), dma((2, 2)), dma((2, 2)),
                dma((2, cases)), dma((2, cases)), dma((2, cases)), dma((2, cases)),
                dma((2, cases)), dma((2, cases)), dma((n_case, 2, 2)), dma((2, 2)),
                dma((2, cases)), dma((2, cases)),
                dma((n_case, cases, 3)), dma((n_case, cases, 3)), dma, dma,
                pltpu.SemaphoreType.REGULAR((16,)),
            ],
            compiler_params=pltpu.CompilerParams(
                collective_id=0, has_side_effects=True, vmem_limit_bytes=limit
            ),
        )(*(pltpu.with_memory_space_constraint(arg, pltpu.HBM) for arg in args))
        return pl.pallas_call(
            functools.partial(finish, n_space),
            out_shape=(
                jax.ShapeDtypeStruct(displacement.shape, F32),
                jax.ShapeDtypeStruct(density.shape, F32),
                jax.ShapeDtypeStruct((1,), F32),
            ),
            in_specs=[in_vmem] * 7,
            out_specs=(
                pl.BlockSpec(memory_space=pl.ANY),
                pl.BlockSpec(memory_space=pl.ANY),
                pl.BlockSpec(memory_space=pl.ANY),
            ),
            scratch_shapes=[vmem(thick), vmem(slab), pltpu.SMEM((1,), F32), dma((cases + 2,))],
            compiler_params=pltpu.CompilerParams(vmem_limit_bytes=limit),
        )(*kept)

    return jax.shard_map(
        body,
        mesh=mesh,
        in_specs=(
            P(("design", "case"), None, "space", None, None),
            P(("design", "case"), None, "space", None, None),
            P(("design", "space"), None, None),
            P(("design", "space"), None, None),
            P(("design", "space"), None, None),
        ),
        out_specs=(
            P(("design", "case"), None, "space", None, None),
            P(("design", "space"), None, None),
            P("design"),
        ),
        check_vma=False,
    )
```

```python
import functools
import math

import jax
import jax.numpy as jnp
from jax import lax
from jax.experimental import pallas as pl
from jax.experimental.pallas import tpu as pltpu
from jax.sharding import PartitionSpec as P

STIFF_MIN = 0.001
DIAG_SHIFT = 0.5
KS_BETA = 8.0
MOVE_LIMIT = 0.2
DENSITY_MIN = 0.001
STEP_ONE = 1.0 / (1.15 + 0.85 * math.cos(math.pi / 4))
STEP_TWO = 1.0 / (1.15 - 0.85 * math.cos(math.pi / 4))
F32 = jnp.float32
MESH = pl.DeviceIdType.MESH
LO, HI = 0, 1
DOWN_LESS = (2, 1)


def loop(start, stop, fn, unroll=1):
    def step(i, carry):
        fn(i)
        return carry

    lax.fori_loop(start, stop, step, 0, unroll=unroll)


def blocks(start, stop, size):
    return [(j, min(size, stop - j)) for j in range(start, stop, size)]


def edges(rows, lanes):
    y_id = lax.broadcasted_iota(jnp.int32, (rows, lanes), 0)
    z_id = lax.broadcasted_iota(jnp.int32, (rows, lanes), 1)
    return y_id == 0, y_id == rows - 1, z_id == 0, z_id == lanes - 1


def next_y(value):
    return pltpu.roll(value, value.shape[-2] - 1, value.ndim - 2)


def prev_y(value):
    return pltpu.roll(value, 1, value.ndim - 2)


def next_z(value):
    return pltpu.roll(value, value.shape[-1] - 1, value.ndim - 1)


def prev_z(value):
    return pltpu.roll(value, 1, value.ndim - 1)


def around(value):
    y_first, y_last, z_first, z_last = edges(*value.shape[-2:])
    return (
        jnp.where(y_last, 0.0, next_y(value)) + jnp.where(y_first, 0.0, prev_y(value))
        + jnp.where(z_last, 0.0, next_z(value)) + jnp.where(z_first, 0.0, prev_z(value))
    )


def kernel(
    n_space, n_case,
    disp, forces, dens, sup, void,
    s2, e, gath, d, cube, inv, void_v,
    v, f, s1, sup_v, kx, kyp, kym, kzp, kzm, keep, rdk, hsum,
    ab, ar, rb, rr, hv, ha, hb, acc, stat,
    load_sem, dens_load, dsend, drecv, vsend, vrecv, asend, arecv, rsend, rrecv,
    psend, precv, hrecv, hsend, csend, crecv, gsend, grecv, known,
):
    cases, comps, planes, rows, lanes = disp.shape
    s = lax.axis_index("space")
    mine = lax.axis_index("case")
    members = n_space * n_case
    me = s * n_case + mine
    has_lo = s > 0
    has_hi = s < n_space - 1
    last = planes + 1
    half = cases // 2
    odd = lax.rem(s, 2) == 1
    even = jnp.logical_not(odd)
    levels = n_space // 2
    sends_by = jnp.where(odd, s + 1 < n_space, s > 0)
    hands_on = jnp.where(odd, s > 2, s + 2 < n_space)

    less = jnp.where(mine == 0, DOWN_LESS[0], DOWN_LESS[1])

    def by_partner(rises, level):
        up = (cases * (levels - 1 - level)) // max(levels, 1)
        down = (cases * (level + 1)) // max(levels, 1) - less
        return jnp.clip(jnp.where(rises, up, down), 0, cases)

    by_count = jnp.where(sends_by, by_partner(odd, (s - 1) // 2), 0)
    on_count = jnp.where(hands_on, by_partner(even, jnp.where(odd, s - 2, s) // 2), 0)
    no_lo = 1.0 - has_lo.astype(F32)
    no_hi = 1.0 - has_hi.astype(F32)
    y_first, y_last, z_first, z_last = edges(rows, lanes)

    barrier = pltpu.get_barrier_semaphore()

    def greet(sem, distance):
        @pl.when(s >= distance)
        def _():
            pl.semaphore_signal(
                sem, inc=1, device_id={"space": jnp.maximum(s - distance, 0)}, device_id_type=MESH
            )

        @pl.when(s < n_space - distance)
        def _():
            pl.semaphore_signal(
                sem, inc=1, device_id={"space": jnp.minimum(s + distance, n_space - 1)},
                device_id_type=MESH,
            )

    def greeted(distance):
        return (s >= distance).astype(jnp.int32) + (s < n_space - distance).astype(jnp.int32)

    greet(barrier, 1)
    for step in range(1, n_case):
        pl.semaphore_signal(
            barrier, inc=1, device_id={"case": lax.rem(mine + step, n_case)}, device_id_type=MESH
        )

    distances = []
    while 2 ** len(distances) < n_space:
        distances.append(2 ** len(distances))

    def widen_start(k):
        if k < len(distances):
            greet(known.at[k], distances[k])

    def widen_wait(k):
        if k < len(distances):
            pl.semaphore_wait(known.at[k], greeted(distances[k]))

    own = pl.ds(1, planes)
    d_own = pl.ds(2, planes)
    dens_loads = [
        pltpu.make_async_copy(dens, d.at[d_own], dens_load.at[0]),
        pltpu.make_async_copy(sup, sup_v.at[own], dens_load.at[1]),
        pltpu.make_async_copy(void, void_v, dens_load.at[2]),
    ]
    for copy in dens_loads:
        copy.start()

    def disp_load(c):
        return pltpu.make_async_copy(disp.at[c], v.at[c, :, own], load_sem.at[0, c])

    def force_load(c):
        return pltpu.make_async_copy(forces.at[c], f.at[c], load_sem.at[1, c])

    for c in range(cases):
        disp_load(c).start()
        force_load(c).start()

    for side, absent, wide, at in (
        (LO, s == 0, pl.ds(0, 2), 0), (HI, s == n_space - 1, pl.ds(planes + 2, 2), last)
    ):
        @pl.when(absent)
        def _():
            d[wide] = jnp.zeros((2, rows, lanes), F32)
            sup_v[at] = jnp.ones((rows, lanes), jnp.int32)
            v[:, :, at] = jnp.zeros((cases, comps, rows, lanes), F32)
            ar[:, side] = jnp.zeros((cases, 2 * comps, rows, lanes), F32)
            rr[:, side] = jnp.zeros((cases, 2, rows, lanes), F32)

    pl.semaphore_wait(barrier, greeted(1) + (n_case - 1))

    def remote(src, dst, ssem, rsem, side, distance=1):
        peer = jnp.minimum(s + distance, n_space - 1) if side == HI else jnp.maximum(s - distance, 0)
        return pltpu.make_async_remote_copy(
            src_ref=src, dst_ref=dst, send_sem=ssem, recv_sem=rsem,
            device_id={"space": peer}, device_id_type=MESH,
        )

    def dens_send(side):
        here = pl.ds(planes - 2, 2) if side == HI else pl.ds(0, 2)
        there = pl.ds(0, 2) if side == HI else pl.ds(planes + 2, 2)
        return remote(dens.at[here], d.at[there], dsend.at[side, 0], drecv.at[side, 0], side)

    def sup_send(side):
        here = planes - 1 if side == HI else 0
        there = 0 if side == HI else last
        return remote(sup.at[here], sup_v.at[there], dsend.at[side, 1], drecv.at[side, 1], side)

    def face_send(side, c):
        here = planes - 1 if side == HI else 0
        there = 0 if side == HI else last
        return remote(
            disp.at[c, :, here], v.at[c, :, there], vsend.at[side, c], vrecv.at[side, c], side
        )

    def whole_of(side, c, at_hi):
        return (c >= half) == (side == at_hi)

    def part_send(side, c):
        n = 2 * comps if whole_of(side, c, HI) else comps
        return remote(
            ab.at[c, side, pl.ds(0, n)], ar.at[c, 1 - side, pl.ds(0, n)],
            asend.at[side, c], arecv.at[side, c], side,
        )

    def face_in(side, c):
        here = planes - 1 if side == HI else 0
        return remote(disp.at[c, :, here], hv.at[c], vsend.at[side, c], hrecv.at[0, c], 1 - side)

    def face_on(side, c):
        there = 0 if side == HI else last
        return remote(hv.at[c], v.at[c, :, there], hsend.at[0, c], vrecv.at[side, c], side, 2)

    def part_in(side, c):
        n = 2 * comps if whole_of(side, c, HI) else comps
        return remote(
            ab.at[c, side, pl.ds(0, n)], ha.at[c, pl.ds(0, n)],
            asend.at[side, c], hrecv.at[1, c], 1 - side,
        )

    def part_on(side, c):
        n = 2 * comps if whole_of(side, c, HI) else comps
        return remote(
            ha.at[c, pl.ds(0, n)], ar.at[c, 1 - side, pl.ds(0, n)],
            hsend.at[1, c], arecv.at[side, c], side, 2,
        )

    def send_by(c, inward):
        for side, between in ((HI, odd), (LO, even)):
            @pl.when(jnp.logical_and(between, c < by_count))
            def _():
                inward(side, c).start()

    def send_direct(c, direct):
        for side, has, between in ((HI, has_hi, odd), (LO, has_lo, even)):
            by = jnp.logical_and(between, c < by_count)

            @pl.when(jnp.logical_and(has, jnp.logical_not(by)))
            def _():
                direct(side, c).start()

    def hand_on(c, fn):
        for side, between in ((HI, even), (LO, odd)):
            @pl.when(jnp.logical_and(between, c < on_count))
            def _():
                fn(side)

    order = tuple(reversed(range(cases)))

    def rim_send(side, c):
        n = 2 if whole_of(side, c, LO) else 1
        return remote(
            rb.at[c, side, pl.ds(0, n)], rr.at[c, 1 - side, pl.ds(0, n)],
            rsend.at[side, c], rrecv.at[side, c], side,
        )

    def to_both(fn):
        @pl.when(has_hi)
        def _():
            fn(HI)

        @pl.when(has_lo)
        def _():
            fn(LO)

    def from_both(fn):
        @pl.when(has_lo)
        def _():
            fn(HI)

        @pl.when(has_hi)
        def _():
            fn(LO)

    def first_sends(side):
        dens_send(side).start()
        sup_send(side).start()

    for c in range(cases):
        send_by(c, face_in)
    for c in order:
        send_direct(c, face_send)
    bearer = mine == n_case - 1

    @pl.when(bearer)
    def _():
        to_both(first_sends)

    widen_start(0)

    yz_count = (
        4.0 + 2.0 - y_first.astype(F32) - y_last.astype(F32)
        - z_first.astype(F32) - z_last.astype(F32)
    )
    total_planes = planes * n_space

    def cube_of(j, n=1):
        value = d[pl.ds(j + 1, n)]
        cube[pl.ds(j + 1, n)] = value * value * value

    def inv_of(j, n=1):
        g = s * planes + j - 1 + lax.broadcasted_iota(jnp.int32, (n, rows, lanes), 0)
        x_count = (g > 0).astype(F32) + (g < total_planes - 1).astype(F32)
        inside = jnp.logical_and(g >= 0, g < total_planes)
        value = jnp.where(inside, d[pl.ds(j + 1, n)], 1.0)
        inv[pl.ds(j + 1, n)] = jnp.where(inside, 1.0 / (value * (yz_count + x_count)), 0.0)

    def coefficients(j, n=1):
        at = pl.ds(j, n)
        here = cube[pl.ds(j + 1, n)]
        face_lo = STIFF_MIN + 0.5 * (cube[at] + here)
        face_hi = STIFF_MIN + 0.5 * (here + cube[pl.ds(j + 2, n)])
        y_hi = STIFF_MIN + 0.5 * (here + jnp.where(y_last, 0.0, next_y(here)))
        y_lo = STIFF_MIN + 0.5 * (here + jnp.where(y_first, 0.0, prev_y(here)))
        z_hi = STIFF_MIN + 0.5 * (here + jnp.where(z_last, 0.0, next_z(here)))
        z_lo = STIFF_MIN + 0.5 * (here + jnp.where(z_first, 0.0, prev_z(here)))
        kept = (1 - sup_v[at]).astype(F32)
        diagonal = DIAG_SHIFT + face_hi + face_lo + y_hi + y_lo + z_hi + z_lo
        if j >= 1:
            kx[pl.ds(j - 1, n)] = face_lo
        if j + n <= last:
            kx[at] = face_hi
        kyp[at] = jnp.where(y_last, 0.0, y_hi)
        kym[at] = jnp.where(y_first, 0.0, y_lo)
        kzp[at] = jnp.where(z_last, 0.0, z_hi)
        kzm[at] = jnp.where(z_first, 0.0, z_lo)
        keep[at] = kept
        rdk[at] = kept / diagonal

    def filter_sum(j, n=1):
        here = inv[pl.ds(j + 1, n)]
        total = 2.0 * here + inv[pl.ds(j, n)] + inv[pl.ds(j + 2, n)] + around(here)
        hsum[pl.ds(j, n)] = 1.5 * cube[pl.ds(j + 1, n)] * total

    def in_plane(centre, at):
        total = kyp[at] * next_y(centre) + kym[at] * prev_y(centre)
        return total + kzp[at] * next_z(centre) + kzm[at] * prev_z(centre)

    def settle(centre, total, at, factor):
        return (keep[at] * (1.0 - factor)) * centre + (rdk[at] * factor) * total

    def sweep(src, dst, c, j, n, factor):
        at = pl.ds(j, n)
        centre = src[c, :, at]
        load = f[c, :, pl.ds(j - 1, n)]
        total = load + kx[pl.ds(j - 1, n)] * src[c, :, pl.ds(j - 1, n)]
        total = total + kx[at] * src[c, :, pl.ds(j + 1, n)] + in_plane(centre, at)
        result = settle(centre, total, at, factor)
        dst[c, :, at] = result
        return jnp.sum(jnp.sum(load * result, axis=0), axis=0)

    def energy(c, j, n, low="in", high="in"):
        x_faces, y_faces, z_faces, squares, first, final = [], [], [], [], [], []
        for k in range(comps):
            centre = s2[c, k, pl.ds(j, n)]
            step = centre[1:] - centre[:-1]
            x_faces.append(step * step)
            if low == "none":
                step = jnp.zeros((1, rows, lanes), F32)
            elif low == "end":
                step = centre[:1] * no_lo
            else:
                step = centre[:1] - s2[c, k, pl.ds(j - 1, 1)]
            first.append(step * step)
            if high == "none":
                step = jnp.zeros((1, rows, lanes), F32)
            elif high == "end":
                step = centre[n - 1:] * no_hi
            else:
                step = centre[n - 1:] - s2[c, k, pl.ds(j + n, 1)]
            final.append(step * step)
            step = centre - jnp.where(y_last, 0.0, next_y(centre))
            y_faces.append(step * step)
            step = centre - jnp.where(z_last, 0.0, next_z(centre))
            z_faces.append(step * step)
            squares.append(centre * centre)
        x_faces, y_faces, z_faces, squares, first, final = (
            functools.reduce(lambda a, b: a + b, terms)
            for terms in (x_faces, y_faces, z_faces, squares, first, final)
        )
        value = y_faces + jnp.where(y_first, squares, prev_y(y_faces))
        value = value + z_faces + jnp.where(z_first, squares, prev_z(z_faces))
        value = value + jnp.concatenate([first, x_faces], axis=0)
        value = value + jnp.concatenate([x_faces, final], axis=0)
        e[mine, c, pl.ds(j, n)] = value
        return jnp.sum(value * hsum[pl.ds(j, n)], axis=0), first[0], final[0]

    def side_faces(j):
        here = cube[j + 1]
        kyp[j] = jnp.where(y_last, 0.0, STIFF_MIN + 0.5 * (here + next_y(here)))
        kym[j] = jnp.where(y_first, 0.0, STIFF_MIN + 0.5 * (here + prev_y(here)))
        kzp[j] = jnp.where(z_last, 0.0, STIFF_MIN + 0.5 * (here + next_z(here)))
        kzm[j] = jnp.where(z_first, 0.0, STIFF_MIN + 0.5 * (here + prev_z(here)))

    for copy in dens_loads:
        copy.wait()
    for j, n in blocks(1, last, 2):
        cube_of(j, n)
    for j in (1, planes):
        side_faces(j)
    for j in (2, planes - 1):
        coefficients(j)

    def partial(c, side):
        j = 1 if side == LO else planes
        beyond, face = (2, 1) if side == LO else (planes - 1, planes - 1)
        load = f[c, :, j - 1]
        total = load + kx[face] * v[c, :, beyond] + in_plane(v[c, :, j], j)
        ab[c, side, pl.ds(0, comps)] = total
        sweep(v, s1, c, beyond, 1, STEP_ONE)
        if whole_of(side, c, HI):
            ab[c, side, pl.ds(comps, comps)] = load + kx[face] * s1[c, :, beyond]

    for c in range(cases):
        disp_load(c).wait()
        force_load(c).wait()
        partial(c, LO)
        partial(c, HI)
        send_by(c, part_in)
    for c in order:
        send_direct(c, part_send)

    for j, n in blocks(3, planes - 1, 2):
        coefficients(j, n)

    def interior_one(c):
        for j, n in blocks(3, planes - 1, 2):
            sweep(v, s1, c, j, n, STEP_ONE)

    loop(0, cases, interior_one)
    widen_wait(0)
    widen_start(1)

    def face_hand(side, c):
        face_in(side, c).wait_recv()
        face_on(side, c).start()

    def part_hand(side, c):
        part_in(side, c).wait_recv()
        part_on(side, c).start()

    for c in order:
        hand_on(c, lambda side: face_hand(side, c))

    def first_share(side, step):
        at = pl.ds(0, 2) if side == HI else pl.ds(planes + 2, 2)
        plane = 0 if side == HI else last
        return [
            pltpu.make_async_remote_copy(
                src_ref=ref, dst_ref=ref, send_sem=psend.at[step, side, i],
                recv_sem=precv.at[side, i],
                device_id={"case": lax.rem(mine + step, n_case)}, device_id_type=MESH,
            )
            for i, ref in enumerate((d.at[at], sup_v.at[plane]))
        ]

    def first_pass(side):
        dens_send(side).wait_recv()
        sup_send(side).wait_recv()
        for step in range(1, n_case):
            for copy in first_share(side, step):
                copy.start()

    @pl.when(bearer)
    def _():
        from_both(first_pass)

    def interior_two(c):
        acc[0, c] = sum(sweep(s1, s2, c, j, n, STEP_TWO) for j, n in blocks(3, planes - 1, 2))

    loop(0, cases, interior_two)
    for c in order:
        hand_on(c, lambda side: part_hand(side, c))

    def first_waits(side):
        for copy in first_share(side, 1):
            copy.wait_recv()

    @pl.when(jnp.logical_not(bearer))
    def _():
        from_both(first_waits)

    for j in (-1, last):
        cube_of(j, 2)
        coefficients(j + 1 if j < 0 else planes, 2)

    widen_wait(1)
    widen_start(2)
    for j, n in blocks(-1, planes + 3, 2):
        inv_of(j, n)
    for j, n in blocks(0, last + 1, 2):
        filter_sum(j, n)

    for k in range(2, len(distances)):
        if k > 2:
            widen_start(k)
        widen_wait(k)

    def interior_three(c):
        inside = blocks(3, planes - 1, 4)
        acc[1, c] = sum(
            energy(
                c, j, n, low="none" if j == inside[0][0] else "in",
                high="none" if j == inside[-1][0] else "in",
            )[0]
            for j, n in inside
        )
        for side, j, inner, face in ((LO, 2, 3, 2), (HI, planes - 1, planes - 2, planes - 2)):
            total = f[c, :, j - 1] + kx[face] * s1[c, :, inner]
            hb[c, side] = total + in_plane(s1[c, :, j], j)

    loop(0, cases, interior_three)

    def across(c, step, at, which):
        return pltpu.make_async_remote_copy(
            src_ref=e.at[mine, c, at], dst_ref=e.at[mine, c, at],
            send_sem=csend.at[step - 1, c, which], recv_sem=crecv.at[step - 1, c, which],
            device_id={"case": lax.rem(mine + step, n_case)}, device_id_type=MESH,
        )

    def across_wait(c, step, at, which):
        there = lax.rem(mine + n_case - step, n_case)
        pltpu.make_async_copy(
            e.at[there, c, at], e.at[there, c, at], crecv.at[step - 1, c, which]
        ).wait()

    pieces = ((pl.ds(2, planes - 2), 0), (pl.ds(0, 2), 1), (pl.ds(planes, 2), 2))

    def finish_edges(c):
        def face_waits(side):
            face_send(side, c).wait_recv()
            part_send(side, c).wait_recv()

        from_both(face_waits)
        for j, beside, face, sums in (
            (1, 0, 0, ab[c, LO]), (planes, last, planes, ab[c, HI]),
            (0, 1, 0, ar[c, LO]), (last, planes, planes, ar[c, HI]),
        ):
            total = sums[:comps] + kx[face] * v[c, :, beside]
            s1[c, :, j] = settle(v[c, :, j], total, j, STEP_ONE)
        part = acc[0, c]
        for side, j, outer, face in ((LO, 2, 1, 1), (HI, planes - 1, planes, planes - 1)):
            total = hb[c, side] + kx[face] * s1[c, :, outer]
            result = settle(s1[c, :, j], total, j, STEP_TWO)
            s2[c, :, j] = result
            part = part + jnp.sum(f[c, :, j - 1] * result, axis=0)
            part = part + sweep(s1, s2, c, outer, 1, STEP_TWO)
        acc[0, c] = part
        outside, inside, face, side = (0, 1, 0, LO) if c >= half else (last, planes, planes, HI)
        centre = s1[c, :, outside]
        total = ar[c, side, pl.ds(comps, comps)] + kx[face] * s1[c, :, inside]
        s2[c, :, outside] = settle(centre, total + in_plane(centre, outside), outside, STEP_TWO)

        at_lo, first, near = energy(c, 1, 2, low="in" if c >= half else "end")
        at_hi, far, final = energy(c, planes - 1, 2, high="in" if c < half else "end")
        e[mine, c, 3] = e[mine, c, 3] + near
        e[mine, c, planes - 2] = e[mine, c, planes - 2] + far
        total = acc[1, c] + at_lo + at_hi + near * hsum[3] + far * hsum[planes - 2]
        if c >= half:
            rb[c, LO, 1] = first
            total = total + first * hsum[0]
        else:
            rb[c, HI, 1] = final
            total = total + final * hsum[last]
        rb[c, LO, 0] = e[mine, c, 1]
        rb[c, HI, 0] = e[mine, c, planes]
        acc[1, c] = total
        to_both(lambda side: rim_send(side, c).start())
        for step in range(1, n_case):
            across(c, step, *pieces[0]).start()

    for c in order:
        finish_edges(c)

    def gather_copy(peer):
        return pltpu.make_async_remote_copy(
            src_ref=gath.at[me], dst_ref=gath.at[me], send_sem=gsend, recv_sem=grecv,
            device_id={"space": peer // n_case, "case": lax.rem(peer, n_case)},
            device_id_type=MESH,
        )

    for which in range(2):
        for c in range(cases):
            stat[pl.ds(which * cases + c, 1)] = jnp.sum(acc[which, c], axis=0, keepdims=True)
    row = lax.broadcasted_iota(jnp.int32, (2 * cases, lanes), 0)
    lane = lax.broadcasted_iota(jnp.int32, (2 * cases, lanes), 1)
    place = jnp.where(row < cases, row, row - cases + lanes // 2) + mine * cases
    sums = jnp.sum(stat[...], axis=1, keepdims=True)
    gath[me] = jnp.sum(jnp.where(lane == place, sums, 0.0), axis=0, keepdims=True)
    loop(1, members, lambda step: gather_copy(lax.rem(me + step, members)).start())

    def rim_waits(side):
        for c in range(cases):
            rim_send(side, c).wait_recv()

    from_both(rim_waits)
    for c in range(cases):
        if c >= half:
            e[mine, c, 0] = rr[c, LO, 0] + rb[c, LO, 1]
            e[mine, c, last] = rr[c, HI, 0]
            e[mine, c, planes] = rb[c, HI, 0] + rr[c, HI, 1]
        else:
            e[mine, c, 0] = rr[c, LO, 0]
            e[mine, c, 1] = rb[c, LO, 0] + rr[c, LO, 1]
            e[mine, c, last] = rr[c, HI, 0] + rb[c, HI, 1]
        for step in range(1, n_case):
            across(c, step, *pieces[1]).start()
            across(c, step, *pieces[2]).start()

    others = gath.at[pl.ds(0, members - 1)]
    for step in range(1, n_case):
        for c in range(cases):
            for at, which in pieces:
                across_wait(c, step, at, which)
    pltpu.make_async_copy(others, others, grecv).wait()

    def first_sent(side):
        dens_send(side).wait_send()
        sup_send(side).wait_send()

    def first_passed(side):
        for step in range(1, n_case):
            for copy in first_share(side, step):
                copy.wait_send()

    @pl.when(bearer)
    def _():
        to_both(first_sent)
        from_both(first_passed)

    def sent(side):
        for c in range(cases):
            face_send(side, c).wait_send()
            part_send(side, c).wait_send()
            rim_send(side, c).wait_send()

    to_both(sent)

    def handed(side, c):
        face_on(side, c).wait_send()
        part_on(side, c).wait_send()

    for c in range(cases):
        hand_on(c, lambda side: handed(side, c))
    for step in range(1, n_case):
        for c in range(cases):
            for at, which in pieces:
                across(c, step, at, which).wait_send()
    pltpu.make_async_copy(others, others, gsend).wait()


def finish(
    n_space, s2, e, gath, d, cube, inv, void_v, out, newd, ks, cu, new_v, ks_v, sem
):
    n_case, cases = e.shape[:2]
    planes, rows, lanes = newd.shape
    last = planes + 1
    copies = [
        pltpu.make_async_copy(s2.at[c, :, pl.ds(1, planes)], out.at[c], sem.at[c])
        for c in range(cases)
    ]
    for copy in copies:
        copy.start()

    sums = jnp.sum(gath[...], axis=0)
    lane = lax.broadcasted_iota(jnp.int32, (1, lanes), 1)
    cells = planes * n_space * rows * lanes
    valid = lane < cases * n_case
    scores = (KS_BETA / (3.0 * cells)) * sums
    top = jnp.max(jnp.where(valid, scores, -3.0e38), axis=1, keepdims=True)
    exponent = jnp.where(valid, jnp.exp(jnp.where(valid, scores - top, 0.0)), 0.0)
    total = jnp.sum(exponent, axis=1, keepdims=True)
    weights = exponent / total
    ks_v[0] = jnp.max((top + jnp.log(total)) / KS_BETA)
    score = pltpu.make_async_copy(ks_v, ks, sem.at[cases + 1])
    score.start()
    moved = pltpu.roll(sums, lanes // 2, 1)
    scale = jnp.sum(weights * jnp.where(valid, moved, 0.0), axis=1, keepdims=True)
    gain = MOVE_LIMIT / (scale / cells + 1e-06)
    picks = [
        jnp.sum(jnp.where(lane == c, weights, 0.0), axis=1, keepdims=True)
        for c in range(n_case * cases)
    ]

    for j, n in blocks(0, last + 1, 2):
        at = pl.ds(j, n)
        value = picks[0] * e[0, 0, at]
        for c in range(1, n_case * cases):
            value = value + picks[c] * e[c // cases, c % cases, at]
        cu[at] = 1.5 * cube[pl.ds(j + 1, n)] * value

    for j, n in blocks(1, last, 2):
        at = pl.ds(j - 1, n)
        here = cu[pl.ds(j, n)]
        beside = cu[at] + cu[pl.ds(j + 1, n)]
        filtered = inv[pl.ds(j + 1, n)] * (2.0 * here + beside + around(here))
        value = d[pl.ds(j + 1, n)] + (filtered * gain - MOVE_LIMIT)
        value = jnp.minimum(jnp.maximum(value, DENSITY_MIN), 1.0)
        new_v[at] = jnp.where(void_v[at] == 1, DENSITY_MIN, value)

    store = pltpu.make_async_copy(new_v, newd, sem.at[cases])
    store.start()
    for copy in copies:
        copy.wait()
    store.wait()
    score.wait()


def solution(mesh):
    n_space, n_case = mesh.shape["space"], mesh.shape["case"]
    members = n_space * n_case

    def body(*args):
        displacement, _, density, _, void_mask = args
        cases, comps, planes, rows, lanes = displacement.shape
        padded = (cases, comps, planes + 2, rows, lanes)
        slab = (planes, rows, lanes)
        thick = (planes + 2, rows, lanes)
        wide = (planes + 4, rows, lanes)
        in_vmem = pl.BlockSpec(memory_space=pltpu.VMEM)
        in_hbm = pl.BlockSpec(memory_space=pltpu.HBM)
        vmem = lambda shape, dtype=F32: pltpu.VMEM(shape, dtype)
        dma = pltpu.SemaphoreType.DMA
        limit = 24 * 2**20
        kept = pl.pallas_call(
            functools.partial(kernel, n_space, n_case),
            out_shape=(
                vmem(padded), vmem((n_case, cases) + thick), vmem((members, 1, lanes)),
                vmem(wide), vmem(wide), vmem(wide), vmem(slab, jnp.int32),
            ),
            in_specs=[in_hbm] * 5,
            out_specs=(in_vmem,) * 7,
            scratch_shapes=[
                vmem(padded), vmem(displacement.shape), vmem(padded), vmem(thick, jnp.int32),
                vmem((planes + 1, rows, lanes)),
                vmem(thick), vmem(thick), vmem(thick), vmem(thick), vmem(thick), vmem(thick),
                vmem(thick),
                vmem((cases, 2, 2 * comps, rows, lanes)), vmem((cases, 2, 2 * comps, rows, lanes)),
                vmem((cases, 2, 2, rows, lanes)), vmem((cases, 2, 2, rows, lanes)),
                vmem((cases, comps, rows, lanes)), vmem((cases, 2 * comps, rows, lanes)),
                vmem((cases, 2, comps, rows, lanes)),
                vmem((2, cases, rows, lanes)), vmem((2 * cases, lanes)),
                dma((2, cases)), dma((3,)), dma((2, 2)), dma((2, 2)),
                dma((2, cases)), dma((2, cases)), dma((2, cases)), dma((2, cases)),
                dma((2, cases)), dma((2, cases)), dma((n_case, 2, 2)), dma((2, 2)),
                dma((2, cases)), dma((2, cases)),
                dma((n_case, cases, 3)), dma((n_case, cases, 3)), dma, dma,
                pltpu.SemaphoreType.REGULAR((16,)),
            ],
            compiler_params=pltpu.CompilerParams(
                collective_id=0, has_side_effects=True, vmem_limit_bytes=limit
            ),
        )(*(pltpu.with_memory_space_constraint(arg, pltpu.HBM) for arg in args))
        return pl.pallas_call(
            functools.partial(finish, n_space),
            out_shape=(
                jax.ShapeDtypeStruct(displacement.shape, F32),
                jax.ShapeDtypeStruct(density.shape, F32),
                jax.ShapeDtypeStruct((1,), F32),
            ),
            in_specs=[in_vmem] * 7,
            out_specs=(
                pl.BlockSpec(memory_space=pl.ANY),
                pl.BlockSpec(memory_space=pl.ANY),
                pl.BlockSpec(memory_space=pl.ANY),
            ),
            scratch_shapes=[vmem(thick), vmem(slab), pltpu.SMEM((1,), F32), dma((cases + 2,))],
            compiler_params=pltpu.CompilerParams(vmem_limit_bytes=limit),
        )(*kept)

    return jax.shard_map(
        body,
        mesh=mesh,
        in_specs=(
            P(("design", "case"), None, "space", None, None),
            P(("design", "case"), None, "space", None, None),
            P(("design", "space"), None, None),
            P(("design", "space"), None, None),
            P(("design", "space"), None, None),
        ),
        out_specs=(
            P(("design", "case"), None, "space", None, None),
            P(("design", "space"), None, None),
            P("design"),
        ),
        check_vma=False,
    )
```

```python
import functools
import math

import jax
import jax.numpy as jnp
from jax import lax
from jax.experimental import pallas as pl
from jax.experimental.pallas import tpu as pltpu
from jax.sharding import PartitionSpec as P

STIFF_MIN = 0.001
DIAG_SHIFT = 0.5
KS_BETA = 8.0
MOVE_LIMIT = 0.2
DENSITY_MIN = 0.001
STEP_ONE = 1.0 / (1.15 + 0.85 * math.cos(math.pi / 4))
STEP_TWO = 1.0 / (1.15 - 0.85 * math.cos(math.pi / 4))
F32 = jnp.float32
MESH = pl.DeviceIdType.MESH
LO, HI = 0, 1
UP_MORE, DOWN_LESS = (0, 1), (2, 1)


def loop(start, stop, fn, unroll=1):
    def step(i, carry):
        fn(i)
        return carry

    lax.fori_loop(start, stop, step, 0, unroll=unroll)


def blocks(start, stop, size):
    return [(j, min(size, stop - j)) for j in range(start, stop, size)]


def edges(rows, lanes):
    y_id = lax.broadcasted_iota(jnp.int32, (rows, lanes), 0)
    z_id = lax.broadcasted_iota(jnp.int32, (rows, lanes), 1)
    return y_id == 0, y_id == rows - 1, z_id == 0, z_id == lanes - 1


def next_y(value):
    return pltpu.roll(value, value.shape[-2] - 1, value.ndim - 2)


def prev_y(value):
    return pltpu.roll(value, 1, value.ndim - 2)


def next_z(value):
    return pltpu.roll(value, value.shape[-1] - 1, value.ndim - 1)


def prev_z(value):
    return pltpu.roll(value, 1, value.ndim - 1)


def around(value):
    y_first, y_last, z_first, z_last = edges(*value.shape[-2:])
    return (
        jnp.where(y_last, 0.0, next_y(value)) + jnp.where(y_first, 0.0, prev_y(value))
        + jnp.where(z_last, 0.0, next_z(value)) + jnp.where(z_first, 0.0, prev_z(value))
    )


def kernel(
    n_space, n_case,
    disp, forces, dens, sup, void,
    s2, e, gath, d, cube, inv, void_v,
    v, f, s1, sup_v, kx, kyp, kym, kzp, kzm, keep, rdk, hsum,
    ab, ar, rb, rr, hv, ha, hb, acc, stat,
    load_sem, dens_load, dsend, drecv, vsend, vrecv, asend, arecv, rsend, rrecv,
    psend, precv, hrecv, hsend, csend, crecv, gsend, grecv, known,
):
    cases, comps, planes, rows, lanes = disp.shape
    s = lax.axis_index("space")
    mine = lax.axis_index("case")
    members = n_space * n_case
    me = s * n_case + mine
    has_lo = s > 0
    has_hi = s < n_space - 1
    last = planes + 1
    half = cases // 2
    odd = lax.rem(s, 2) == 1
    even = jnp.logical_not(odd)
    levels = n_space // 2
    sends_by = jnp.where(odd, s + 1 < n_space, s > 0)
    hands_on = jnp.where(odd, s > 2, s + 2 < n_space)

    more = jnp.where(mine == 0, UP_MORE[0], UP_MORE[1])
    less = jnp.where(mine == 0, DOWN_LESS[0], DOWN_LESS[1])

    def by_partner(rises, level):
        up = (cases * (levels - 1 - level)) // max(levels, 1) + more
        down = (cases * (level + 1)) // max(levels, 1) - less
        return jnp.clip(jnp.where(rises, up, down), 0, cases)

    by_count = jnp.where(sends_by, by_partner(odd, (s - 1) // 2), 0)
    on_count = jnp.where(hands_on, by_partner(even, jnp.where(odd, s - 2, s) // 2), 0)
    no_lo = 1.0 - has_lo.astype(F32)
    no_hi = 1.0 - has_hi.astype(F32)
    y_first, y_last, z_first, z_last = edges(rows, lanes)

    barrier = pltpu.get_barrier_semaphore()

    def greet(sem, distance):
        @pl.when(s >= distance)
        def _():
            pl.semaphore_signal(
                sem, inc=1, device_id={"space": jnp.maximum(s - distance, 0)}, device_id_type=MESH
            )

        @pl.when(s < n_space - distance)
        def _():
            pl.semaphore_signal(
                sem, inc=1, device_id={"space": jnp.minimum(s + distance, n_space - 1)},
                device_id_type=MESH,
            )

    def greeted(distance):
        return (s >= distance).astype(jnp.int32) + (s < n_space - distance).astype(jnp.int32)

    greet(barrier, 1)
    for step in range(1, n_case):
        pl.semaphore_signal(
            barrier, inc=1, device_id={"case": lax.rem(mine + step, n_case)}, device_id_type=MESH
        )

    distances = []
    while 2 ** len(distances) < n_space:
        distances.append(2 ** len(distances))

    def widen_start(k):
        if k < len(distances):
            greet(known.at[k], distances[k])

    def widen_wait(k):
        if k < len(distances):
            pl.semaphore_wait(known.at[k], greeted(distances[k]))

    own = pl.ds(1, planes)
    d_own = pl.ds(2, planes)
    dens_loads = [
        pltpu.make_async_copy(dens, d.at[d_own], dens_load.at[0]),
        pltpu.make_async_copy(sup, sup_v.at[own], dens_load.at[1]),
        pltpu.make_async_copy(void, void_v, dens_load.at[2]),
    ]
    for copy in dens_loads:
        copy.start()

    def disp_load(c):
        return pltpu.make_async_copy(disp.at[c], v.at[c, :, own], load_sem.at[0, c])

    def force_load(c):
        return pltpu.make_async_copy(forces.at[c], f.at[c], load_sem.at[1, c])

    for c in range(cases):
        disp_load(c).start()
        force_load(c).start()

    for side, absent, wide, at in (
        (LO, s == 0, pl.ds(0, 2), 0), (HI, s == n_space - 1, pl.ds(planes + 2, 2), last)
    ):
        @pl.when(absent)
        def _():
            d[wide] = jnp.zeros((2, rows, lanes), F32)
            sup_v[at] = jnp.ones((rows, lanes), jnp.int32)
            v[:, :, at] = jnp.zeros((cases, comps, rows, lanes), F32)
            ar[:, side] = jnp.zeros((cases, 2 * comps, rows, lanes), F32)
            rr[:, side] = jnp.zeros((cases, 2, rows, lanes), F32)

    pl.semaphore_wait(barrier, greeted(1) + (n_case - 1))

    def remote(src, dst, ssem, rsem, side, distance=1):
        peer = jnp.minimum(s + distance, n_space - 1) if side == HI else jnp.maximum(s - distance, 0)
        return pltpu.make_async_remote_copy(
            src_ref=src, dst_ref=dst, send_sem=ssem, recv_sem=rsem,
            device_id={"space": peer}, device_id_type=MESH,
        )

    def dens_send(side):
        here = pl.ds(planes - 2, 2) if side == HI else pl.ds(0, 2)
        there = pl.ds(0, 2) if side == HI else pl.ds(planes + 2, 2)
        return remote(dens.at[here], d.at[there], dsend.at[side, 0], drecv.at[side, 0], side)

    def sup_send(side):
        here = planes - 1 if side == HI else 0
        there = 0 if side == HI else last
        return remote(sup.at[here], sup_v.at[there], dsend.at[side, 1], drecv.at[side, 1], side)

    def face_send(side, c):
        here = planes - 1 if side == HI else 0
        there = 0 if side == HI else last
        return remote(
            disp.at[c, :, here], v.at[c, :, there], vsend.at[side, c], vrecv.at[side, c], side
        )

    def whole_of(side, c, at_hi):
        return (c >= half) == (side == at_hi)

    def part_send(side, c):
        n = 2 * comps if whole_of(side, c, HI) else comps
        return remote(
            ab.at[c, side, pl.ds(0, n)], ar.at[c, 1 - side, pl.ds(0, n)],
            asend.at[side, c], arecv.at[side, c], side,
        )

    def face_in(side, c):
        here = planes - 1 if side == HI else 0
        return remote(disp.at[c, :, here], hv.at[c], vsend.at[side, c], hrecv.at[0, c], 1 - side)

    def face_on(side, c):
        there = 0 if side == HI else last
        return remote(hv.at[c], v.at[c, :, there], hsend.at[0, c], vrecv.at[side, c], side, 2)

    def part_in(side, c):
        n = 2 * comps if whole_of(side, c, HI) else comps
        return remote(
            ab.at[c, side, pl.ds(0, n)], ha.at[c, pl.ds(0, n)],
            asend.at[side, c], hrecv.at[1, c], 1 - side,
        )

    def part_on(side, c):
        n = 2 * comps if whole_of(side, c, HI) else comps
        return remote(
            ha.at[c, pl.ds(0, n)], ar.at[c, 1 - side, pl.ds(0, n)],
            hsend.at[1, c], arecv.at[side, c], side, 2,
        )

    def send_by(c, inward):
        for side, between in ((HI, odd), (LO, even)):
            @pl.when(jnp.logical_and(between, c < by_count))
            def _():
                inward(side, c).start()

    def send_direct(c, direct):
        for side, has, between in ((HI, has_hi, odd), (LO, has_lo, even)):
            by = jnp.logical_and(between, c < by_count)

            @pl.when(jnp.logical_and(has, jnp.logical_not(by)))
            def _():
                direct(side, c).start()

    def hand_on(c, fn):
        for side, between in ((HI, even), (LO, odd)):
            @pl.when(jnp.logical_and(between, c < on_count))
            def _():
                fn(side)

    order = tuple(reversed(range(cases)))

    def rim_send(side, c):
        n = 2 if whole_of(side, c, LO) else 1
        return remote(
            rb.at[c, side, pl.ds(0, n)], rr.at[c, 1 - side, pl.ds(0, n)],
            rsend.at[side, c], rrecv.at[side, c], side,
        )

    def to_both(fn):
        @pl.when(has_hi)
        def _():
            fn(HI)

        @pl.when(has_lo)
        def _():
            fn(LO)

    def from_both(fn):
        @pl.when(has_lo)
        def _():
            fn(HI)

        @pl.when(has_hi)
        def _():
            fn(LO)

    def first_sends(side):
        dens_send(side).start()
        sup_send(side).start()

    for c in range(cases):
        send_by(c, face_in)
    for c in order:
        send_direct(c, face_send)
    bearer = mine == n_case - 1

    @pl.when(bearer)
    def _():
        to_both(first_sends)

    widen_start(0)

    yz_count = (
        4.0 + 2.0 - y_first.astype(F32) - y_last.astype(F32)
        - z_first.astype(F32) - z_last.astype(F32)
    )
    total_planes = planes * n_space

    def cube_of(j, n=1):
        value = d[pl.ds(j + 1, n)]
        cube[pl.ds(j + 1, n)] = value * value * value

    def inv_of(j, n=1):
        g = s * planes + j - 1 + lax.broadcasted_iota(jnp.int32, (n, rows, lanes), 0)
        x_count = (g > 0).astype(F32) + (g < total_planes - 1).astype(F32)
        inside = jnp.logical_and(g >= 0, g < total_planes)
        value = jnp.where(inside, d[pl.ds(j + 1, n)], 1.0)
        inv[pl.ds(j + 1, n)] = jnp.where(inside, 1.0 / (value * (yz_count + x_count)), 0.0)

    def coefficients(j, n=1):
        at = pl.ds(j, n)
        here = cube[pl.ds(j + 1, n)]
        face_lo = STIFF_MIN + 0.5 * (cube[at] + here)
        face_hi = STIFF_MIN + 0.5 * (here + cube[pl.ds(j + 2, n)])
        y_hi = STIFF_MIN + 0.5 * (here + jnp.where(y_last, 0.0, next_y(here)))
        y_lo = STIFF_MIN + 0.5 * (here + jnp.where(y_first, 0.0, prev_y(here)))
        z_hi = STIFF_MIN + 0.5 * (here + jnp.where(z_last, 0.0, next_z(here)))
        z_lo = STIFF_MIN + 0.5 * (here + jnp.where(z_first, 0.0, prev_z(here)))
        kept = (1 - sup_v[at]).astype(F32)
        diagonal = DIAG_SHIFT + face_hi + face_lo + y_hi + y_lo + z_hi + z_lo
        if j >= 1:
            kx[pl.ds(j - 1, n)] = face_lo
        if j + n <= last:
            kx[at] = face_hi
        kyp[at] = jnp.where(y_last, 0.0, y_hi)
        kym[at] = jnp.where(y_first, 0.0, y_lo)
        kzp[at] = jnp.where(z_last, 0.0, z_hi)
        kzm[at] = jnp.where(z_first, 0.0, z_lo)
        keep[at] = kept
        rdk[at] = kept / diagonal

    def filter_sum(j, n=1):
        here = inv[pl.ds(j + 1, n)]
        total = 2.0 * here + inv[pl.ds(j, n)] + inv[pl.ds(j + 2, n)] + around(here)
        hsum[pl.ds(j, n)] = 1.5 * cube[pl.ds(j + 1, n)] * total

    def in_plane(centre, at):
        total = kyp[at] * next_y(centre) + kym[at] * prev_y(centre)
        return total + kzp[at] * next_z(centre) + kzm[at] * prev_z(centre)

    def settle(centre, total, at, factor):
        return (keep[at] * (1.0 - factor)) * centre + (rdk[at] * factor) * total

    def sweep(src, dst, c, j, n, factor):
        at = pl.ds(j, n)
        centre = src[c, :, at]
        load = f[c, :, pl.ds(j - 1, n)]
        total = load + kx[pl.ds(j - 1, n)] * src[c, :, pl.ds(j - 1, n)]
        total = total + kx[at] * src[c, :, pl.ds(j + 1, n)] + in_plane(centre, at)
        result = settle(centre, total, at, factor)
        dst[c, :, at] = result
        return jnp.sum(jnp.sum(load * result, axis=0), axis=0)

    def energy(c, j, n, low="in", high="in"):
        x_faces, y_faces, z_faces, squares, first, final = [], [], [], [], [], []
        for k in range(comps):
            centre = s2[c, k, pl.ds(j, n)]
            step = centre[1:] - centre[:-1]
            x_faces.append(step * step)
            if low == "none":
                step = jnp.zeros((1, rows, lanes), F32)
            elif low == "end":
                step = centre[:1] * no_lo
            else:
                step = centre[:1] - s2[c, k, pl.ds(j - 1, 1)]
            first.append(step * step)
            if high == "none":
                step = jnp.zeros((1, rows, lanes), F32)
            elif high == "end":
                step = centre[n - 1:] * no_hi
            else:
                step = centre[n - 1:] - s2[c, k, pl.ds(j + n, 1)]
            final.append(step * step)
            step = centre - jnp.where(y_last, 0.0, next_y(centre))
            y_faces.append(step * step)
            step = centre - jnp.where(z_last, 0.0, next_z(centre))
            z_faces.append(step * step)
            squares.append(centre * centre)
        x_faces, y_faces, z_faces, squares, first, final = (
            functools.reduce(lambda a, b: a + b, terms)
            for terms in (x_faces, y_faces, z_faces, squares, first, final)
        )
        value = y_faces + jnp.where(y_first, squares, prev_y(y_faces))
        value = value + z_faces + jnp.where(z_first, squares, prev_z(z_faces))
        value = value + jnp.concatenate([first, x_faces], axis=0)
        value = value + jnp.concatenate([x_faces, final], axis=0)
        e[mine, c, pl.ds(j, n)] = value
        return jnp.sum(value * hsum[pl.ds(j, n)], axis=0), first[0], final[0]

    def side_faces(j):
        here = cube[j + 1]
        kyp[j] = jnp.where(y_last, 0.0, STIFF_MIN + 0.5 * (here + next_y(here)))
        kym[j] = jnp.where(y_first, 0.0, STIFF_MIN + 0.5 * (here + prev_y(here)))
        kzp[j] = jnp.where(z_last, 0.0, STIFF_MIN + 0.5 * (here + next_z(here)))
        kzm[j] = jnp.where(z_first, 0.0, STIFF_MIN + 0.5 * (here + prev_z(here)))

    for copy in dens_loads:
        copy.wait()
    for j, n in blocks(1, last, 2):
        cube_of(j, n)
    for j in (1, planes):
        side_faces(j)
    for j in (2, planes - 1):
        coefficients(j)

    def partial(c, side):
        j = 1 if side == LO else planes
        beyond, face = (2, 1) if side == LO else (planes - 1, planes - 1)
        load = f[c, :, j - 1]
        total = load + kx[face] * v[c, :, beyond] + in_plane(v[c, :, j], j)
        ab[c, side, pl.ds(0, comps)] = total
        sweep(v, s1, c, beyond, 1, STEP_ONE)
        if whole_of(side, c, HI):
            ab[c, side, pl.ds(comps, comps)] = load + kx[face] * s1[c, :, beyond]

    for c in range(cases):
        disp_load(c).wait()
        force_load(c).wait()
        partial(c, LO)
        partial(c, HI)
        send_by(c, part_in)
    for c in order:
        send_direct(c, part_send)

    for j, n in blocks(3, planes - 1, 2):
        coefficients(j, n)

    def interior_one(c):
        for j, n in blocks(3, planes - 1, 2):
            sweep(v, s1, c, j, n, STEP_ONE)

    loop(0, cases, interior_one)
    widen_wait(0)
    widen_start(1)

    def face_hand(side, c):
        face_in(side, c).wait_recv()
        face_on(side, c).start()

    def part_hand(side, c):
        part_in(side, c).wait_recv()
        part_on(side, c).start()

    for c in order:
        hand_on(c, lambda side: face_hand(side, c))

    def first_share(side, step):
        at = pl.ds(0, 2) if side == HI else pl.ds(planes + 2, 2)
        plane = 0 if side == HI else last
        return [
            pltpu.make_async_remote_copy(
                src_ref=ref, dst_ref=ref, send_sem=psend.at[step, side, i],
                recv_sem=precv.at[side, i],
                device_id={"case": lax.rem(mine + step, n_case)}, device_id_type=MESH,
            )
            for i, ref in enumerate((d.at[at], sup_v.at[plane]))
        ]

    def first_pass(side):
        dens_send(side).wait_recv()
        sup_send(side).wait_recv()
        for step in range(1, n_case):
            for copy in first_share(side, step):
                copy.start()

    @pl.when(bearer)
    def _():
        from_both(first_pass)

    def interior_two(c):
        acc[0, c] = sum(sweep(s1, s2, c, j, n, STEP_TWO) for j, n in blocks(3, planes - 1, 2))

    loop(0, cases, interior_two)
    for c in order:
        hand_on(c, lambda side: part_hand(side, c))

    def first_waits(side):
        for copy in first_share(side, 1):
            copy.wait_recv()

    @pl.when(jnp.logical_not(bearer))
    def _():
        from_both(first_waits)

    for j in (-1, last):
        cube_of(j, 2)
        coefficients(j + 1 if j < 0 else planes, 2)

    widen_wait(1)
    widen_start(2)
    for j, n in blocks(-1, planes + 3, 2):
        inv_of(j, n)
    for j, n in blocks(0, last + 1, 2):
        filter_sum(j, n)

    for k in range(2, len(distances)):
        if k > 2:
            widen_start(k)
        widen_wait(k)

    def interior_three(c):
        inside = blocks(3, planes - 1, 4)
        acc[1, c] = sum(
            energy(
                c, j, n, low="none" if j == inside[0][0] else "in",
                high="none" if j == inside[-1][0] else "in",
            )[0]
            for j, n in inside
        )
        for side, j, inner, face in ((LO, 2, 3, 2), (HI, planes - 1, planes - 2, planes - 2)):
            total = f[c, :, j - 1] + kx[face] * s1[c, :, inner]
            hb[c, side] = total + in_plane(s1[c, :, j], j)

    loop(0, cases, interior_three)

    def across(c, step, at, which):
        return pltpu.make_async_remote_copy(
            src_ref=e.at[mine, c, at], dst_ref=e.at[mine, c, at],
            send_sem=csend.at[step - 1, c, which], recv_sem=crecv.at[step - 1, c, which],
            device_id={"case": lax.rem(mine + step, n_case)}, device_id_type=MESH,
        )

    def across_wait(c, step, at, which):
        there = lax.rem(mine + n_case - step, n_case)
        pltpu.make_async_copy(
            e.at[there, c, at], e.at[there, c, at], crecv.at[step - 1, c, which]
        ).wait()

    pieces = ((pl.ds(2, planes - 2), 0), (pl.ds(0, 2), 1), (pl.ds(planes, 2), 2))

    def finish_edges(c):
        def face_waits(side):
            face_send(side, c).wait_recv()
            part_send(side, c).wait_recv()

        from_both(face_waits)
        for j, beside, face, sums in (
            (1, 0, 0, ab[c, LO]), (planes, last, planes, ab[c, HI]),
            (0, 1, 0, ar[c, LO]), (last, planes, planes, ar[c, HI]),
        ):
            total = sums[:comps] + kx[face] * v[c, :, beside]
            s1[c, :, j] = settle(v[c, :, j], total, j, STEP_ONE)
        part = acc[0, c]
        for side, j, outer, face in ((LO, 2, 1, 1), (HI, planes - 1, planes, planes - 1)):
            total = hb[c, side] + kx[face] * s1[c, :, outer]
            result = settle(s1[c, :, j], total, j, STEP_TWO)
            s2[c, :, j] = result
            part = part + jnp.sum(f[c, :, j - 1] * result, axis=0)
            part = part + sweep(s1, s2, c, outer, 1, STEP_TWO)
        acc[0, c] = part
        outside, inside, face, side = (0, 1, 0, LO) if c >= half else (last, planes, planes, HI)
        centre = s1[c, :, outside]
        total = ar[c, side, pl.ds(comps, comps)] + kx[face] * s1[c, :, inside]
        s2[c, :, outside] = settle(centre, total + in_plane(centre, outside), outside, STEP_TWO)

        at_lo, first, near = energy(c, 1, 2, low="in" if c >= half else "end")
        at_hi, far, final = energy(c, planes - 1, 2, high="in" if c < half else "end")
        e[mine, c, 3] = e[mine, c, 3] + near
        e[mine, c, planes - 2] = e[mine, c, planes - 2] + far
        total = acc[1, c] + at_lo + at_hi + near * hsum[3] + far * hsum[planes - 2]
        if c >= half:
            rb[c, LO, 1] = first
            total = total + first * hsum[0]
        else:
            rb[c, HI, 1] = final
            total = total + final * hsum[last]
        rb[c, LO, 0] = e[mine, c, 1]
        rb[c, HI, 0] = e[mine, c, planes]
        acc[1, c] = total
        to_both(lambda side: rim_send(side, c).start())
        for step in range(1, n_case):
            across(c, step, *pieces[0]).start()

    for c in order:
        finish_edges(c)

    def gather_copy(peer):
        return pltpu.make_async_remote_copy(
            src_ref=gath.at[me], dst_ref=gath.at[me], send_sem=gsend, recv_sem=grecv,
            device_id={"space": peer // n_case, "case": lax.rem(peer, n_case)},
            device_id_type=MESH,
        )

    for which in range(2):
        for c in range(cases):
            stat[pl.ds(which * cases + c, 1)] = jnp.sum(acc[which, c], axis=0, keepdims=True)
    row = lax.broadcasted_iota(jnp.int32, (2 * cases, lanes), 0)
    lane = lax.broadcasted_iota(jnp.int32, (2 * cases, lanes), 1)
    place = jnp.where(row < cases, row, row - cases + lanes // 2) + mine * cases
    sums = jnp.sum(stat[...], axis=1, keepdims=True)
    gath[me] = jnp.sum(jnp.where(lane == place, sums, 0.0), axis=0, keepdims=True)
    loop(1, members, lambda step: gather_copy(lax.rem(me + step, members)).start())

    def rim_waits(side):
        for c in range(cases):
            rim_send(side, c).wait_recv()

    from_both(rim_waits)
    for c in range(cases):
        if c >= half:
            e[mine, c, 0] = rr[c, LO, 0] + rb[c, LO, 1]
            e[mine, c, last] = rr[c, HI, 0]
            e[mine, c, planes] = rb[c, HI, 0] + rr[c, HI, 1]
        else:
            e[mine, c, 0] = rr[c, LO, 0]
            e[mine, c, 1] = rb[c, LO, 0] + rr[c, LO, 1]
            e[mine, c, last] = rr[c, HI, 0] + rb[c, HI, 1]
        for step in range(1, n_case):
            across(c, step, *pieces[1]).start()
            across(c, step, *pieces[2]).start()

    others = gath.at[pl.ds(0, members - 1)]
    for step in range(1, n_case):
        for c in range(cases):
            for at, which in pieces:
                across_wait(c, step, at, which)
    pltpu.make_async_copy(others, others, grecv).wait()

    def first_sent(side):
        dens_send(side).wait_send()
        sup_send(side).wait_send()

    def first_passed(side):
        for step in range(1, n_case):
            for copy in first_share(side, step):
                copy.wait_send()

    @pl.when(bearer)
    def _():
        to_both(first_sent)
        from_both(first_passed)

    def sent(side):
        for c in range(cases):
            face_send(side, c).wait_send()
            part_send(side, c).wait_send()
            rim_send(side, c).wait_send()

    to_both(sent)

    def handed(side, c):
        face_on(side, c).wait_send()
        part_on(side, c).wait_send()

    for c in range(cases):
        hand_on(c, lambda side: handed(side, c))
    for step in range(1, n_case):
        for c in range(cases):
            for at, which in pieces:
                across(c, step, at, which).wait_send()
    pltpu.make_async_copy(others, others, gsend).wait()


def finish(
    n_space, s2, e, gath, d, cube, inv, void_v, out, newd, ks, cu, new_v, ks_v, sem
):
    n_case, cases = e.shape[:2]
    planes, rows, lanes = newd.shape
    last = planes + 1
    copies = [
        pltpu.make_async_copy(s2.at[c, :, pl.ds(1, planes)], out.at[c], sem.at[c])
        for c in range(cases)
    ]
    for copy in copies:
        copy.start()

    sums = jnp.sum(gath[...], axis=0)
    lane = lax.broadcasted_iota(jnp.int32, (1, lanes), 1)
    cells = planes * n_space * rows * lanes
    valid = lane < cases * n_case
    scores = (KS_BETA / (3.0 * cells)) * sums
    top = jnp.max(jnp.where(valid, scores, -3.0e38), axis=1, keepdims=True)
    exponent = jnp.where(valid, jnp.exp(jnp.where(valid, scores - top, 0.0)), 0.0)
    total = jnp.sum(exponent, axis=1, keepdims=True)
    weights = exponent / total
    ks_v[0] = jnp.max((top + jnp.log(total)) / KS_BETA)
    score = pltpu.make_async_copy(ks_v, ks, sem.at[cases + 1])
    score.start()
    moved = pltpu.roll(sums, lanes // 2, 1)
    scale = jnp.sum(weights * jnp.where(valid, moved, 0.0), axis=1, keepdims=True)
    gain = MOVE_LIMIT / (scale / cells + 1e-06)
    picks = [
        jnp.sum(jnp.where(lane == c, weights, 0.0), axis=1, keepdims=True)
        for c in range(n_case * cases)
    ]

    for j, n in blocks(0, last + 1, 2):
        at = pl.ds(j, n)
        value = picks[0] * e[0, 0, at]
        for c in range(1, n_case * cases):
            value = value + picks[c] * e[c // cases, c % cases, at]
        cu[at] = 1.5 * cube[pl.ds(j + 1, n)] * value

    for j, n in blocks(1, last, 2):
        at = pl.ds(j - 1, n)
        here = cu[pl.ds(j, n)]
        beside = cu[at] + cu[pl.ds(j + 1, n)]
        filtered = inv[pl.ds(j + 1, n)] * (2.0 * here + beside + around(here))
        value = d[pl.ds(j + 1, n)] + (filtered * gain - MOVE_LIMIT)
        value = jnp.minimum(jnp.maximum(value, DENSITY_MIN), 1.0)
        new_v[at] = jnp.where(void_v[at] == 1, DENSITY_MIN, value)

    store = pltpu.make_async_copy(new_v, newd, sem.at[cases])
    store.start()
    for copy in copies:
        copy.wait()
    store.wait()
    score.wait()


def solution(mesh):
    n_space, n_case = mesh.shape["space"], mesh.shape["case"]
    members = n_space * n_case

    def body(*args):
        displacement, _, density, _, void_mask = args
        cases, comps, planes, rows, lanes = displacement.shape
        padded = (cases, comps, planes + 2, rows, lanes)
        slab = (planes, rows, lanes)
        thick = (planes + 2, rows, lanes)
        wide = (planes + 4, rows, lanes)
        in_vmem = pl.BlockSpec(memory_space=pltpu.VMEM)
        in_hbm = pl.BlockSpec(memory_space=pltpu.HBM)
        vmem = lambda shape, dtype=F32: pltpu.VMEM(shape, dtype)
        dma = pltpu.SemaphoreType.DMA
        limit = 24 * 2**20
        kept = pl.pallas_call(
            functools.partial(kernel, n_space, n_case),
            out_shape=(
                vmem(padded), vmem((n_case, cases) + thick), vmem((members, 1, lanes)),
                vmem(wide), vmem(wide), vmem(wide), vmem(slab, jnp.int32),
            ),
            in_specs=[in_hbm] * 5,
            out_specs=(in_vmem,) * 7,
            scratch_shapes=[
                vmem(padded), vmem(displacement.shape), vmem(padded), vmem(thick, jnp.int32),
                vmem((planes + 1, rows, lanes)),
                vmem(thick), vmem(thick), vmem(thick), vmem(thick), vmem(thick), vmem(thick),
                vmem(thick),
                vmem((cases, 2, 2 * comps, rows, lanes)), vmem((cases, 2, 2 * comps, rows, lanes)),
                vmem((cases, 2, 2, rows, lanes)), vmem((cases, 2, 2, rows, lanes)),
                vmem((cases, comps, rows, lanes)), vmem((cases, 2 * comps, rows, lanes)),
                vmem((cases, 2, comps, rows, lanes)),
                vmem((2, cases, rows, lanes)), vmem((2 * cases, lanes)),
                dma((2, cases)), dma((3,)), dma((2, 2)), dma((2, 2)),
                dma((2, cases)), dma((2, cases)), dma((2, cases)), dma((2, cases)),
                dma((2, cases)), dma((2, cases)), dma((n_case, 2, 2)), dma((2, 2)),
                dma((2, cases)), dma((2, cases)),
                dma((n_case, cases, 3)), dma((n_case, cases, 3)), dma, dma,
                pltpu.SemaphoreType.REGULAR((16,)),
            ],
            compiler_params=pltpu.CompilerParams(
                collective_id=0, has_side_effects=True, vmem_limit_bytes=limit
            ),
        )(*(pltpu.with_memory_space_constraint(arg, pltpu.HBM) for arg in args))
        return pl.pallas_call(
            functools.partial(finish, n_space),
            out_shape=(
                jax.ShapeDtypeStruct(displacement.shape, F32),
                jax.ShapeDtypeStruct(density.shape, F32),
                jax.ShapeDtypeStruct((1,), F32),
            ),
            in_specs=[in_vmem] * 7,
            out_specs=(
                pl.BlockSpec(memory_space=pl.ANY),
                pl.BlockSpec(memory_space=pl.ANY),
                pl.BlockSpec(memory_space=pl.ANY),
            ),
            scratch_shapes=[vmem(thick), vmem(slab), pltpu.SMEM((1,), F32), dma((cases + 2,))],
            compiler_params=pltpu.CompilerParams(vmem_limit_bytes=limit),
        )(*kept)

    return jax.shard_map(
        body,
        mesh=mesh,
        in_specs=(
            P(("design", "case"), None, "space", None, None),
            P(("design", "case"), None, "space", None, None),
            P(("design", "space"), None, None),
            P(("design", "space"), None, None),
            P(("design", "space"), None, None),
        ),
        out_specs=(
            P(("design", "case"), None, "space", None, None),
            P(("design", "space"), None, None),
            P("design"),
        ),
        check_vma=False,
    )
```

```python
import functools
import math

import jax
import jax.numpy as jnp
from jax import lax
from jax.experimental import pallas as pl
from jax.experimental.pallas import tpu as pltpu
from jax.sharding import PartitionSpec as P

STIFF_MIN = 0.001
DIAG_SHIFT = 0.5
KS_BETA = 8.0
MOVE_LIMIT = 0.2
DENSITY_MIN = 0.001
STEP_ONE = 1.0 / (1.15 + 0.85 * math.cos(math.pi / 4))
STEP_TWO = 1.0 / (1.15 - 0.85 * math.cos(math.pi / 4))
F32 = jnp.float32
MESH = pl.DeviceIdType.MESH
LO, HI = 0, 1
UP_MORE, DOWN_LESS = (0, 1), (2, 1)


def loop(start, stop, fn, unroll=1):
    def step(i, carry):
        fn(i)
        return carry

    lax.fori_loop(start, stop, step, 0, unroll=unroll)


def blocks(start, stop, size):
    return [(j, min(size, stop - j)) for j in range(start, stop, size)]


def edges(rows, lanes):
    y_id = lax.broadcasted_iota(jnp.int32, (rows, lanes), 0)
    z_id = lax.broadcasted_iota(jnp.int32, (rows, lanes), 1)
    return y_id == 0, y_id == rows - 1, z_id == 0, z_id == lanes - 1


def next_y(value):
    return pltpu.roll(value, value.shape[-2] - 1, value.ndim - 2)


def prev_y(value):
    return pltpu.roll(value, 1, value.ndim - 2)


def next_z(value):
    return pltpu.roll(value, value.shape[-1] - 1, value.ndim - 1)


def prev_z(value):
    return pltpu.roll(value, 1, value.ndim - 1)


def around(value):
    y_first, y_last, z_first, z_last = edges(*value.shape[-2:])
    return (
        jnp.where(y_last, 0.0, next_y(value)) + jnp.where(y_first, 0.0, prev_y(value))
        + jnp.where(z_last, 0.0, next_z(value)) + jnp.where(z_first, 0.0, prev_z(value))
    )


def kernel(
    n_space, n_case,
    disp, forces, dens, sup, void,
    s2, e, gath, d, cube, inv, void_v,
    v, f, s1, sup_v, kx, kyp, kym, kzp, kzm, keep, rdk, hsum,
    ab, ar, rb, rr, hv, ha, hb, acc, stat,
    load_sem, dens_load, dsend, drecv, vsend, vrecv, asend, arecv, rsend, rrecv,
    psend, precv, hrecv, hsend, csend, crecv, gsend, grecv, known,
):
    cases, comps, planes, rows, lanes = disp.shape
    s = lax.axis_index("space")
    mine = lax.axis_index("case")
    members = n_space * n_case
    me = s * n_case + mine
    has_lo = s > 0
    has_hi = s < n_space - 1
    last = planes + 1
    half = cases // 2
    odd = lax.rem(s, 2) == 1
    even = jnp.logical_not(odd)
    levels = n_space // 2
    sends_by = jnp.where(odd, s + 1 < n_space, s > 0)
    hands_on = jnp.where(odd, s > 2, s + 2 < n_space)

    more = jnp.where(mine == 0, UP_MORE[0], UP_MORE[1])
    less = jnp.where(mine == 0, DOWN_LESS[0], DOWN_LESS[1])

    def by_partner(rises, level):
        up = (cases * (levels - 1 - level)) // max(levels, 1) + more
        down = (cases * (level + 1)) // max(levels, 1) - less
        return jnp.clip(jnp.where(rises, up, down), 0, cases)

    by_count = jnp.where(sends_by, by_partner(odd, (s - 1) // 2), 0)
    on_count = jnp.where(hands_on, by_partner(even, jnp.where(odd, s - 2, s) // 2), 0)
    no_lo = 1.0 - has_lo.astype(F32)
    no_hi = 1.0 - has_hi.astype(F32)
    y_first, y_last, z_first, z_last = edges(rows, lanes)

    barrier = pltpu.get_barrier_semaphore()

    def greet(sem, distance):
        @pl.when(s >= distance)
        def _():
            pl.semaphore_signal(
                sem, inc=1, device_id={"space": jnp.maximum(s - distance, 0)}, device_id_type=MESH
            )

        @pl.when(s < n_space - distance)
        def _():
            pl.semaphore_signal(
                sem, inc=1, device_id={"space": jnp.minimum(s + distance, n_space - 1)},
                device_id_type=MESH,
            )

    def greeted(distance):
        return (s >= distance).astype(jnp.int32) + (s < n_space - distance).astype(jnp.int32)

    greet(barrier, 1)
    for step in range(1, n_case):
        pl.semaphore_signal(
            barrier, inc=1, device_id={"case": lax.rem(mine + step, n_case)}, device_id_type=MESH
        )

    distances = []
    while 2 ** len(distances) < n_space:
        distances.append(2 ** len(distances))

    def widen_start(k):
        if k < len(distances):
            greet(known.at[k], distances[k])

    def widen_wait(k):
        if k < len(distances):
            pl.semaphore_wait(known.at[k], greeted(distances[k]))

    own = pl.ds(1, planes)
    d_own = pl.ds(2, planes)
    dens_loads = [
        pltpu.make_async_copy(dens, d.at[d_own], dens_load.at[0]),
        pltpu.make_async_copy(sup, sup_v.at[own], dens_load.at[1]),
        pltpu.make_async_copy(void, void_v, dens_load.at[2]),
    ]
    for copy in dens_loads:
        copy.start()

    def disp_load(c):
        return pltpu.make_async_copy(disp.at[c], v.at[c, :, own], load_sem.at[0, c])

    def force_load(c):
        return pltpu.make_async_copy(forces.at[c], f.at[c], load_sem.at[1, c])

    for c in range(cases):
        disp_load(c).start()
        force_load(c).start()

    for side, absent, wide, at in (
        (LO, s == 0, pl.ds(0, 2), 0), (HI, s == n_space - 1, pl.ds(planes + 2, 2), last)
    ):
        @pl.when(absent)
        def _():
            d[wide] = jnp.zeros((2, rows, lanes), F32)
            sup_v[at] = jnp.ones((rows, lanes), jnp.int32)
            v[:, :, at] = jnp.zeros((cases, comps, rows, lanes), F32)
            ar[:, side] = jnp.zeros((cases, 2 * comps, rows, lanes), F32)
            rr[:, side] = jnp.zeros((cases, 2, rows, lanes), F32)

    pl.semaphore_wait(barrier, greeted(1) + (n_case - 1))

    def remote(src, dst, ssem, rsem, side, distance=1):
        peer = jnp.minimum(s + distance, n_space - 1) if side == HI else jnp.maximum(s - distance, 0)
        return pltpu.make_async_remote_copy(
            src_ref=src, dst_ref=dst, send_sem=ssem, recv_sem=rsem,
            device_id={"space": peer}, device_id_type=MESH,
        )

    def dens_send(side):
        here = pl.ds(planes - 2, 2) if side == HI else pl.ds(0, 2)
        there = pl.ds(0, 2) if side == HI else pl.ds(planes + 2, 2)
        return remote(dens.at[here], d.at[there], dsend.at[side, 0], drecv.at[side, 0], side)

    def sup_send(side):
        here = planes - 1 if side == HI else 0
        there = 0 if side == HI else last
        return remote(sup.at[here], sup_v.at[there], dsend.at[side, 1], drecv.at[side, 1], side)

    def face_send(side, c):
        here = planes - 1 if side == HI else 0
        there = 0 if side == HI else last
        return remote(
            disp.at[c, :, here], v.at[c, :, there], vsend.at[side, c], vrecv.at[side, c], side
        )

    def whole_of(side, c, at_hi):
        return (c >= half) == (side == at_hi)

    def part_send(side, c):
        n = 2 * comps if whole_of(side, c, HI) else comps
        return remote(
            ab.at[c, side, pl.ds(0, n)], ar.at[c, 1 - side, pl.ds(0, n)],
            asend.at[side, c], arecv.at[side, c], side,
        )

    def face_in(side, c):
        here = planes - 1 if side == HI else 0
        return remote(disp.at[c, :, here], hv.at[c], vsend.at[side, c], hrecv.at[0, c], 1 - side)

    def face_on(side, c):
        there = 0 if side == HI else last
        return remote(hv.at[c], v.at[c, :, there], hsend.at[0, c], vrecv.at[side, c], side, 2)

    def part_in(side, c):
        n = 2 * comps if whole_of(side, c, HI) else comps
        return remote(
            ab.at[c, side, pl.ds(0, n)], ha.at[c, pl.ds(0, n)],
            asend.at[side, c], hrecv.at[1, c], 1 - side,
        )

    def part_on(side, c):
        n = 2 * comps if whole_of(side, c, HI) else comps
        return remote(
            ha.at[c, pl.ds(0, n)], ar.at[c, 1 - side, pl.ds(0, n)],
            hsend.at[1, c], arecv.at[side, c], side, 2,
        )

    def send_by(c, inward):
        for side, between in ((HI, odd), (LO, even)):
            @pl.when(jnp.logical_and(between, c < by_count))
            def _():
                inward(side, c).start()

    def send_direct(c, direct):
        for side, has, between in ((HI, has_hi, odd), (LO, has_lo, even)):
            by = jnp.logical_and(between, c < by_count)

            @pl.when(jnp.logical_and(has, jnp.logical_not(by)))
            def _():
                direct(side, c).start()

    def hand_on(c, fn):
        for side, between in ((HI, even), (LO, odd)):
            @pl.when(jnp.logical_and(between, c < on_count))
            def _():
                fn(side)

    order = tuple(reversed(range(cases)))

    def rim_send(side, c):
        n = 2 if whole_of(side, c, LO) else 1
        return remote(
            rb.at[c, side, pl.ds(0, n)], rr.at[c, 1 - side, pl.ds(0, n)],
            rsend.at[side, c], rrecv.at[side, c], side,
        )

    def to_both(fn):
        @pl.when(has_hi)
        def _():
            fn(HI)

        @pl.when(has_lo)
        def _():
            fn(LO)

    def from_both(fn):
        @pl.when(has_lo)
        def _():
            fn(HI)

        @pl.when(has_hi)
        def _():
            fn(LO)

    def first_sends(side):
        dens_send(side).start()
        sup_send(side).start()

    for c in range(cases):
        send_by(c, face_in)
    bearer = mine == n_case - 1

    @pl.when(bearer)
    def _():
        to_both(first_sends)

    for c in order:
        send_direct(c, face_send)
    widen_start(0)

    yz_count = (
        4.0 + 2.0 - y_first.astype(F32) - y_last.astype(F32)
        - z_first.astype(F32) - z_last.astype(F32)
    )
    total_planes = planes * n_space

    def cube_of(j, n=1):
        value = d[pl.ds(j + 1, n)]
        cube[pl.ds(j + 1, n)] = value * value * value

    def inv_of(j, n=1):
        g = s * planes + j - 1 + lax.broadcasted_iota(jnp.int32, (n, rows, lanes), 0)
        x_count = (g > 0).astype(F32) + (g < total_planes - 1).astype(F32)
        inside = jnp.logical_and(g >= 0, g < total_planes)
        value = jnp.where(inside, d[pl.ds(j + 1, n)], 1.0)
        inv[pl.ds(j + 1, n)] = jnp.where(inside, 1.0 / (value * (yz_count + x_count)), 0.0)

    def coefficients(j, n=1):
        at = pl.ds(j, n)
        here = cube[pl.ds(j + 1, n)]
        face_lo = STIFF_MIN + 0.5 * (cube[at] + here)
        face_hi = STIFF_MIN + 0.5 * (here + cube[pl.ds(j + 2, n)])
        y_hi = STIFF_MIN + 0.5 * (here + jnp.where(y_last, 0.0, next_y(here)))
        y_lo = STIFF_MIN + 0.5 * (here + jnp.where(y_first, 0.0, prev_y(here)))
        z_hi = STIFF_MIN + 0.5 * (here + jnp.where(z_last, 0.0, next_z(here)))
        z_lo = STIFF_MIN + 0.5 * (here + jnp.where(z_first, 0.0, prev_z(here)))
        kept = (1 - sup_v[at]).astype(F32)
        diagonal = DIAG_SHIFT + face_hi + face_lo + y_hi + y_lo + z_hi + z_lo
        if j >= 1:
            kx[pl.ds(j - 1, n)] = face_lo
        if j + n <= last:
            kx[at] = face_hi
        kyp[at] = jnp.where(y_last, 0.0, y_hi)
        kym[at] = jnp.where(y_first, 0.0, y_lo)
        kzp[at] = jnp.where(z_last, 0.0, z_hi)
        kzm[at] = jnp.where(z_first, 0.0, z_lo)
        keep[at] = kept
        rdk[at] = kept / diagonal

    def filter_sum(j, n=1):
        here = inv[pl.ds(j + 1, n)]
        total = 2.0 * here + inv[pl.ds(j, n)] + inv[pl.ds(j + 2, n)] + around(here)
        hsum[pl.ds(j, n)] = 1.5 * cube[pl.ds(j + 1, n)] * total

    def in_plane(centre, at):
        total = kyp[at] * next_y(centre) + kym[at] * prev_y(centre)
        return total + kzp[at] * next_z(centre) + kzm[at] * prev_z(centre)

    def settle(centre, total, at, factor):
        return (keep[at] * (1.0 - factor)) * centre + (rdk[at] * factor) * total

    def sweep(src, dst, c, j, n, factor):
        at = pl.ds(j, n)
        centre = src[c, :, at]
        load = f[c, :, pl.ds(j - 1, n)]
        total = load + kx[pl.ds(j - 1, n)] * src[c, :, pl.ds(j - 1, n)]
        total = total + kx[at] * src[c, :, pl.ds(j + 1, n)] + in_plane(centre, at)
        result = settle(centre, total, at, factor)
        dst[c, :, at] = result
        return jnp.sum(jnp.sum(load * result, axis=0), axis=0)

    def energy(c, j, n, low="in", high="in"):
        x_faces, y_faces, z_faces, squares, first, final = [], [], [], [], [], []
        for k in range(comps):
            centre = s2[c, k, pl.ds(j, n)]
            step = centre[1:] - centre[:-1]
            x_faces.append(step * step)
            if low == "none":
                step = jnp.zeros((1, rows, lanes), F32)
            elif low == "end":
                step = centre[:1] * no_lo
            else:
                step = centre[:1] - s2[c, k, pl.ds(j - 1, 1)]
            first.append(step * step)
            if high == "none":
                step = jnp.zeros((1, rows, lanes), F32)
            elif high == "end":
                step = centre[n - 1:] * no_hi
            else:
                step = centre[n - 1:] - s2[c, k, pl.ds(j + n, 1)]
            final.append(step * step)
            step = centre - jnp.where(y_last, 0.0, next_y(centre))
            y_faces.append(step * step)
            step = centre - jnp.where(z_last, 0.0, next_z(centre))
            z_faces.append(step * step)
            squares.append(centre * centre)
        x_faces, y_faces, z_faces, squares, first, final = (
            functools.reduce(lambda a, b: a + b, terms)
            for terms in (x_faces, y_faces, z_faces, squares, first, final)
        )
        value = y_faces + jnp.where(y_first, squares, prev_y(y_faces))
        value = value + z_faces + jnp.where(z_first, squares, prev_z(z_faces))
        value = value + jnp.concatenate([first, x_faces], axis=0)
        value = value + jnp.concatenate([x_faces, final], axis=0)
        e[mine, c, pl.ds(j, n)] = value
        return jnp.sum(value * hsum[pl.ds(j, n)], axis=0), first[0], final[0]

    def side_faces(j):
        here = cube[j + 1]
        kyp[j] = jnp.where(y_last, 0.0, STIFF_MIN + 0.5 * (here + next_y(here)))
        kym[j] = jnp.where(y_first, 0.0, STIFF_MIN + 0.5 * (here + prev_y(here)))
        kzp[j] = jnp.where(z_last, 0.0, STIFF_MIN + 0.5 * (here + next_z(here)))
        kzm[j] = jnp.where(z_first, 0.0, STIFF_MIN + 0.5 * (here + prev_z(here)))

    for copy in dens_loads:
        copy.wait()
    for j, n in blocks(1, last, 2):
        cube_of(j, n)
    for j in (1, planes):
        side_faces(j)
    for j in (2, planes - 1):
        coefficients(j)

    def partial(c, side):
        j = 1 if side == LO else planes
        beyond, face = (2, 1) if side == LO else (planes - 1, planes - 1)
        load = f[c, :, j - 1]
        total = load + kx[face] * v[c, :, beyond] + in_plane(v[c, :, j], j)
        ab[c, side, pl.ds(0, comps)] = total
        sweep(v, s1, c, beyond, 1, STEP_ONE)
        if whole_of(side, c, HI):
            ab[c, side, pl.ds(comps, comps)] = load + kx[face] * s1[c, :, beyond]

    for c in range(cases):
        disp_load(c).wait()
        force_load(c).wait()
        partial(c, LO)
        partial(c, HI)
        send_by(c, part_in)
    for c in order:
        send_direct(c, part_send)

    for j, n in blocks(3, planes - 1, 2):
        coefficients(j, n)

    def interior_one(c):
        for j, n in blocks(3, planes - 1, 2):
            sweep(v, s1, c, j, n, STEP_ONE)

    loop(0, cases, interior_one)
    widen_wait(0)
    widen_start(1)

    def face_hand(side, c):
        face_in(side, c).wait_recv()
        face_on(side, c).start()

    def part_hand(side, c):
        part_in(side, c).wait_recv()
        part_on(side, c).start()

    for c in order:
        hand_on(c, lambda side: face_hand(side, c))

    def first_share(side, step):
        at = pl.ds(0, 2) if side == HI else pl.ds(planes + 2, 2)
        plane = 0 if side == HI else last
        return [
            pltpu.make_async_remote_copy(
                src_ref=ref, dst_ref=ref, send_sem=psend.at[step, side, i],
                recv_sem=precv.at[side, i],
                device_id={"case": lax.rem(mine + step, n_case)}, device_id_type=MESH,
            )
            for i, ref in enumerate((d.at[at], sup_v.at[plane]))
        ]

    def first_pass(side):
        dens_send(side).wait_recv()
        sup_send(side).wait_recv()
        for step in range(1, n_case):
            for copy in first_share(side, step):
                copy.start()

    @pl.when(bearer)
    def _():
        from_both(first_pass)

    def interior_two(c):
        acc[0, c] = sum(sweep(s1, s2, c, j, n, STEP_TWO) for j, n in blocks(3, planes - 1, 2))

    loop(0, cases, interior_two)
    for c in order:
        hand_on(c, lambda side: part_hand(side, c))

    def first_waits(side):
        for copy in first_share(side, 1):
            copy.wait_recv()

    @pl.when(jnp.logical_not(bearer))
    def _():
        from_both(first_waits)

    for j in (-1, last):
        cube_of(j, 2)
        coefficients(j + 1 if j < 0 else planes, 2)

    widen_wait(1)
    widen_start(2)
    for j, n in blocks(-1, planes + 3, 2):
        inv_of(j, n)
    for j, n in blocks(0, last + 1, 2):
        filter_sum(j, n)

    for k in range(2, len(distances)):
        if k > 2:
            widen_start(k)
        widen_wait(k)

    def interior_three(c):
        inside = blocks(3, planes - 1, 4)
        acc[1, c] = sum(
            energy(
                c, j, n, low="none" if j == inside[0][0] else "in",
                high="none" if j == inside[-1][0] else "in",
            )[0]
            for j, n in inside
        )
        for side, j, inner, face in ((LO, 2, 3, 2), (HI, planes - 1, planes - 2, planes - 2)):
            total = f[c, :, j - 1] + kx[face] * s1[c, :, inner]
            hb[c, side] = total + in_plane(s1[c, :, j], j)

    loop(0, cases, interior_three)

    def across(c, step, at, which):
        return pltpu.make_async_remote_copy(
            src_ref=e.at[mine, c, at], dst_ref=e.at[mine, c, at],
            send_sem=csend.at[step - 1, c, which], recv_sem=crecv.at[step - 1, c, which],
            device_id={"case": lax.rem(mine + step, n_case)}, device_id_type=MESH,
        )

    def across_wait(c, step, at, which):
        there = lax.rem(mine + n_case - step, n_case)
        pltpu.make_async_copy(
            e.at[there, c, at], e.at[there, c, at], crecv.at[step - 1, c, which]
        ).wait()

    pieces = ((pl.ds(2, planes - 2), 0), (pl.ds(0, 2), 1), (pl.ds(planes, 2), 2))

    def finish_edges(c):
        def face_waits(side):
            face_send(side, c).wait_recv()
            part_send(side, c).wait_recv()

        from_both(face_waits)
        for j, beside, face, sums in (
            (1, 0, 0, ab[c, LO]), (planes, last, planes, ab[c, HI]),
            (0, 1, 0, ar[c, LO]), (last, planes, planes, ar[c, HI]),
        ):
            total = sums[:comps] + kx[face] * v[c, :, beside]
            s1[c, :, j] = settle(v[c, :, j], total, j, STEP_ONE)
        part = acc[0, c]
        for side, j, outer, face in ((LO, 2, 1, 1), (HI, planes - 1, planes, planes - 1)):
            total = hb[c, side] + kx[face] * s1[c, :, outer]
            result = settle(s1[c, :, j], total, j, STEP_TWO)
            s2[c, :, j] = result
            part = part + jnp.sum(f[c, :, j - 1] * result, axis=0)
            part = part + sweep(s1, s2, c, outer, 1, STEP_TWO)
        acc[0, c] = part
        outside, inside, face, side = (0, 1, 0, LO) if c >= half else (last, planes, planes, HI)
        centre = s1[c, :, outside]
        total = ar[c, side, pl.ds(comps, comps)] + kx[face] * s1[c, :, inside]
        s2[c, :, outside] = settle(centre, total + in_plane(centre, outside), outside, STEP_TWO)

        at_lo, first, near = energy(c, 1, 2, low="in" if c >= half else "end")
        at_hi, far, final = energy(c, planes - 1, 2, high="in" if c < half else "end")
        e[mine, c, 3] = e[mine, c, 3] + near
        e[mine, c, planes - 2] = e[mine, c, planes - 2] + far
        total = acc[1, c] + at_lo + at_hi + near * hsum[3] + far * hsum[planes - 2]
        if c >= half:
            rb[c, LO, 1] = first
            total = total + first * hsum[0]
        else:
            rb[c, HI, 1] = final
            total = total + final * hsum[last]
        rb[c, LO, 0] = e[mine, c, 1]
        rb[c, HI, 0] = e[mine, c, planes]
        acc[1, c] = total
        to_both(lambda side: rim_send(side, c).start())
        for step in range(1, n_case):
            across(c, step, *pieces[0]).start()

    for c in order:
        finish_edges(c)

    def gather_copy(peer):
        return pltpu.make_async_remote_copy(
            src_ref=gath.at[me], dst_ref=gath.at[me], send_sem=gsend, recv_sem=grecv,
            device_id={"space": peer // n_case, "case": lax.rem(peer, n_case)},
            device_id_type=MESH,
        )

    for which in range(2):
        for c in range(cases):
            stat[pl.ds(which * cases + c, 1)] = jnp.sum(acc[which, c], axis=0, keepdims=True)
    row = lax.broadcasted_iota(jnp.int32, (2 * cases, lanes), 0)
    lane = lax.broadcasted_iota(jnp.int32, (2 * cases, lanes), 1)
    place = jnp.where(row < cases, row, row - cases + lanes // 2) + mine * cases
    sums = jnp.sum(stat[...], axis=1, keepdims=True)
    gath[me] = jnp.sum(jnp.where(lane == place, sums, 0.0), axis=0, keepdims=True)
    loop(1, members, lambda step: gather_copy(lax.rem(me + step, members)).start())

    def rim_waits(side):
        for c in range(cases):
            rim_send(side, c).wait_recv()

    from_both(rim_waits)
    for c in range(cases):
        if c >= half:
            e[mine, c, 0] = rr[c, LO, 0] + rb[c, LO, 1]
            e[mine, c, last] = rr[c, HI, 0]
            e[mine, c, planes] = rb[c, HI, 0] + rr[c, HI, 1]
        else:
            e[mine, c, 0] = rr[c, LO, 0]
            e[mine, c, 1] = rb[c, LO, 0] + rr[c, LO, 1]
            e[mine, c, last] = rr[c, HI, 0] + rb[c, HI, 1]
        for step in range(1, n_case):
            across(c, step, *pieces[1]).start()
            across(c, step, *pieces[2]).start()

    others = gath.at[pl.ds(0, members - 1)]
    for step in range(1, n_case):
        for c in range(cases):
            for at, which in pieces:
                across_wait(c, step, at, which)
    pltpu.make_async_copy(others, others, grecv).wait()

    def first_sent(side):
        dens_send(side).wait_send()
        sup_send(side).wait_send()

    def first_passed(side):
        for step in range(1, n_case):
            for copy in first_share(side, step):
                copy.wait_send()

    @pl.when(bearer)
    def _():
        to_both(first_sent)
        from_both(first_passed)

    def sent(side):
        for c in range(cases):
            face_send(side, c).wait_send()
            part_send(side, c).wait_send()
            rim_send(side, c).wait_send()

    to_both(sent)

    def handed(side, c):
        face_on(side, c).wait_send()
        part_on(side, c).wait_send()

    for c in range(cases):
        hand_on(c, lambda side: handed(side, c))
    for step in range(1, n_case):
        for c in range(cases):
            for at, which in pieces:
                across(c, step, at, which).wait_send()
    pltpu.make_async_copy(others, others, gsend).wait()


def finish(
    n_space, s2, e, gath, d, cube, inv, void_v, out, newd, ks, cu, new_v, ks_v, sem
):
    n_case, cases = e.shape[:2]
    planes, rows, lanes = newd.shape
    last = planes + 1
    copies = [
        pltpu.make_async_copy(s2.at[c, :, pl.ds(1, planes)], out.at[c], sem.at[c])
        for c in range(cases)
    ]
    for copy in copies:
        copy.start()

    sums = jnp.sum(gath[...], axis=0)
    lane = lax.broadcasted_iota(jnp.int32, (1, lanes), 1)
    cells = planes * n_space * rows * lanes
    valid = lane < cases * n_case
    scores = (KS_BETA / (3.0 * cells)) * sums
    top = jnp.max(jnp.where(valid, scores, -3.0e38), axis=1, keepdims=True)
    exponent = jnp.where(valid, jnp.exp(jnp.where(valid, scores - top, 0.0)), 0.0)
    total = jnp.sum(exponent, axis=1, keepdims=True)
    weights = exponent / total
    ks_v[0] = jnp.max((top + jnp.log(total)) / KS_BETA)
    score = pltpu.make_async_copy(ks_v, ks, sem.at[cases + 1])
    score.start()
    moved = pltpu.roll(sums, lanes // 2, 1)
    scale = jnp.sum(weights * jnp.where(valid, moved, 0.0), axis=1, keepdims=True)
    gain = MOVE_LIMIT / (scale / cells + 1e-06)
    picks = [
        jnp.sum(jnp.where(lane == c, weights, 0.0), axis=1, keepdims=True)
        for c in range(n_case * cases)
    ]

    for j, n in blocks(0, last + 1, 2):
        at = pl.ds(j, n)
        value = picks[0] * e[0, 0, at]
        for c in range(1, n_case * cases):
            value = value + picks[c] * e[c // cases, c % cases, at]
        cu[at] = 1.5 * cube[pl.ds(j + 1, n)] * value

    for j, n in blocks(1, last, 2):
        at = pl.ds(j - 1, n)
        here = cu[pl.ds(j, n)]
        beside = cu[at] + cu[pl.ds(j + 1, n)]
        filtered = inv[pl.ds(j + 1, n)] * (2.0 * here + beside + around(here))
        value = d[pl.ds(j + 1, n)] + (filtered * gain - MOVE_LIMIT)
        value = jnp.minimum(jnp.maximum(value, DENSITY_MIN), 1.0)
        new_v[at] = jnp.where(void_v[at] == 1, DENSITY_MIN, value)

    store = pltpu.make_async_copy(new_v, newd, sem.at[cases])
    store.start()
    for copy in copies:
        copy.wait()
    store.wait()
    score.wait()


def solution(mesh):
    n_space, n_case = mesh.shape["space"], mesh.shape["case"]
    members = n_space * n_case

    def body(*args):
        displacement, _, density, _, void_mask = args
        cases, comps, planes, rows, lanes = displacement.shape
        padded = (cases, comps, planes + 2, rows, lanes)
        slab = (planes, rows, lanes)
        thick = (planes + 2, rows, lanes)
        wide = (planes + 4, rows, lanes)
        in_vmem = pl.BlockSpec(memory_space=pltpu.VMEM)
        in_hbm = pl.BlockSpec(memory_space=pltpu.HBM)
        vmem = lambda shape, dtype=F32: pltpu.VMEM(shape, dtype)
        dma = pltpu.SemaphoreType.DMA
        limit = 24 * 2**20
        kept = pl.pallas_call(
            functools.partial(kernel, n_space, n_case),
            out_shape=(
                vmem(padded), vmem((n_case, cases) + thick), vmem((members, 1, lanes)),
                vmem(wide), vmem(wide), vmem(wide), vmem(slab, jnp.int32),
            ),
            in_specs=[in_hbm] * 5,
            out_specs=(in_vmem,) * 7,
            scratch_shapes=[
                vmem(padded), vmem(displacement.shape), vmem(padded), vmem(thick, jnp.int32),
                vmem((planes + 1, rows, lanes)),
                vmem(thick), vmem(thick), vmem(thick), vmem(thick), vmem(thick), vmem(thick),
                vmem(thick),
                vmem((cases, 2, 2 * comps, rows, lanes)), vmem((cases, 2, 2 * comps, rows, lanes)),
                vmem((cases, 2, 2, rows, lanes)), vmem((cases, 2, 2, rows, lanes)),
                vmem((cases, comps, rows, lanes)), vmem((cases, 2 * comps, rows, lanes)),
                vmem((cases, 2, comps, rows, lanes)),
                vmem((2, cases, rows, lanes)), vmem((2 * cases, lanes)),
                dma((2, cases)), dma((3,)), dma((2, 2)), dma((2, 2)),
                dma((2, cases)), dma((2, cases)), dma((2, cases)), dma((2, cases)),
                dma((2, cases)), dma((2, cases)), dma((n_case, 2, 2)), dma((2, 2)),
                dma((2, cases)), dma((2, cases)),
                dma((n_case, cases, 3)), dma((n_case, cases, 3)), dma, dma,
                pltpu.SemaphoreType.REGULAR((16,)),
            ],
            compiler_params=pltpu.CompilerParams(
                collective_id=0, has_side_effects=True, vmem_limit_bytes=limit
            ),
        )(*(pltpu.with_memory_space_constraint(arg, pltpu.HBM) for arg in args))
        return pl.pallas_call(
            functools.partial(finish, n_space),
            out_shape=(
                jax.ShapeDtypeStruct(displacement.shape, F32),
                jax.ShapeDtypeStruct(density.shape, F32),
                jax.ShapeDtypeStruct((1,), F32),
            ),
            in_specs=[in_vmem] * 7,
            out_specs=(
                pl.BlockSpec(memory_space=pl.ANY),
                pl.BlockSpec(memory_space=pl.ANY),
                pl.BlockSpec(memory_space=pl.ANY),
            ),
            scratch_shapes=[vmem(thick), vmem(slab), pltpu.SMEM((1,), F32), dma((cases + 2,))],
            compiler_params=pltpu.CompilerParams(vmem_limit_bytes=limit),
        )(*kept)

    return jax.shard_map(
        body,
        mesh=mesh,
        in_specs=(
            P(("design", "case"), None, "space", None, None),
            P(("design", "case"), None, "space", None, None),
            P(("design", "space"), None, None),
            P(("design", "space"), None, None),
            P(("design", "space"), None, None),
        ),
        out_specs=(
            P(("design", "case"), None, "space", None, None),
            P(("design", "space"), None, None),
            P("design"),
        ),
        check_vma=False,
    )
```
